512 devices in a mesh: gz: 32 (over y, z_hi, core), gy: 16 (over z_lo, x).
Axes of the slice: x: 4, y: 4, z: 16 (z_hi: 4, z_lo: 4; z = z_hi * 4 + z_lo), core: 2. Of those that a mesh axis runs over, the one named last changes fastest.
Arguments:
- features: bfloat16 [16, 128, 128, 128], P(None, 'gz', 'gy'), may hold values from -6 to 6
- labels: int32 [128, 128, 128], P('gz', 'gy'), may hold values from 0 to 1
- sign_map: int32 [128, 128, 128], P('gz', 'gy'), may hold values from 0 to 1
- conv_first: bfloat16 [16, 16, 3, 3, 3], replicated, may hold values from -0.3125 to 0.3125
- conv_second: bfloat16 [16, 16, 3, 3, 3], replicated, may hold values from -0.3125 to 0.3125
- speed_weight: float32 [16], replicated, may hold values from -1.5 to 1.5
Outputs:
- d_features: bfloat16 [16, 128, 128, 128], P(None, 'gz', 'gy')
- grad_first: float32 [16, 16, 3, 3, 3], replicated
- grad_second: float32 [16, 16, 3, 3, 3], replicated
- grad_speed: float32 [16], replicated
The draws below stay inside these ranges and needn't reach their ends.
All inputs are finite; a program needn't handle non-finite values.
Results may differ from the reference program's by a relative error of at most 0.01.
Values may be sent and summed in bfloat16 or wider, within the bound.
No kernel may reach another device: no remote copies, remote signals or barrier semaphores. Data moves between devices by JAX's collectives and lax.ppermute only.
A program may use at most 128 MiB of HBM per device.

```python
import jax
import jax.numpy as jnp
from jax import lax

C = 16
STEPS = 4
X = 128
NZ = 128
NY = 128


def touch_ends(array, stream_key, least, largest):
    dims = array.shape
    spot = [jax.random.randint(jax.random.fold_in(stream_key, axis), (), 0, dims[axis]) for axis in range(len(dims))]
    array = array.at[tuple(spot)].set(least)
    longest = dims.index(max(dims))
    spot[longest] = (spot[longest] + 1) % dims[longest]
    return array.at[tuple(spot)].set(largest)


def shard_levels(stream_key, shape, shards, low, top_value):
    def one(dim, parts):
        draws = jax.random.uniform(jax.random.fold_in(jax.random.fold_in(stream_key, 6), dim), (parts,), jnp.float32, low / len(shards), top_value / len(shards))
        return jnp.repeat(jnp.exp(draws), shape[dim] // parts).reshape((-1,) + (1,) * (len(shape) - dim - 1))

    loudness = one(*shards[0])
    for cut in shards[1:]:
        loudness = loudness * one(*cut)
    return loudness


def scatter_about(key, shape, spread, limit, cuts=(), dtype=jnp.bfloat16):
    gain = shard_levels(key, shape, cuts, -0.22, 0.18) if cuts else 1.0
    array = jax.random.normal(key, shape, jnp.float32) * spread * gain
    return jnp.minimum(jnp.maximum(array, -limit), limit).astype(dtype)


def setup_inputs(seed: int = 0) -> dict:
    keys = jax.random.split(jax.random.key(seed), 7)
    features = scatter_about(keys[0], (C, NZ, NY, X), 1.0, 6.0, ((1, 32), (2, 16)))
    labels = touch_ends(jax.random.randint(keys[1], (NZ, NY, X), 0, 2), jax.random.fold_in(keys[1], 1), 0, 1).astype(jnp.int32)
    sign_map = touch_ends(jax.random.randint(keys[2], (NZ, NY, X), 0, 2), jax.random.fold_in(keys[2], 1), 0, 1).astype(jnp.int32)
    conv_first = scatter_about(keys[3], (C, C, 3, 3, 3), (27 * C) ** -0.5, 0.3125)
    conv_second = scatter_about(keys[4], (C, C, 3, 3, 3), (27 * C) ** -0.5, 0.3125)
    speed_weight = scatter_about(keys[5], (C,), C ** -0.5, 1.5, (), jnp.float32)
    return {"features": features, "labels": labels, "sign_map": sign_map, "conv_first": conv_first, "conv_second": conv_second, "speed_weight": speed_weight}


time_step = 0.25
spread_rate = 0.5
slope_floor = 0.1

def front(padded, speed):
    grid = jnp.pad(padded, ((0, 0), (0, 0), (1, 1)))
    centre = grid[1:-1, 1:-1, 1:-1]
    up_z = grid[2:, 1:-1, 1:-1]
    low_z = grid[:-2, 1:-1, 1:-1]
    up_y = grid[1:-1, 2:, 1:-1]
    low_y = grid[1:-1, :-2, 1:-1]
    up_x = grid[1:-1, 1:-1, 2:]
    low_x = grid[1:-1, 1:-1, :-2]
    dif_z = (up_z - low_z) * 0.5
    dif_y = (up_y - low_y) * 0.5
    dif_x = (up_x - low_x) * 0.5
    slope = jnp.sqrt(dif_z * dif_z + dif_y * dif_y + dif_x * dif_x + slope_floor)
    laplace = up_z + low_z + up_y + low_y + up_x + low_x - 6.0 * centre
    return centre + time_step * (speed * slope + spread_rate * laplace)

def silu_slope(value):
    sig = jax.nn.sigmoid(value)
    return sig * (1.0 + value * (1.0 - sig))

def conv_full(inputs, weight):
    return lax.conv_general_dilated(inputs[None], weight, (1, 1, 1), ((1, 1), (1, 1), (1, 1)), dimension_numbers=('NCDHW', 'OIDHW', 'NCDHW'), precision=lax.Precision.HIGHEST)[0]

def reference(features, labels, sign_map, conv_first, conv_second, speed_weight):
    high = lax.Precision.HIGHEST
    feat32 = features.astype(jnp.float32)
    first32 = conv_first.astype(jnp.float32)
    second32 = conv_second.astype(jnp.float32)
    act_first = conv_full(feat32, first32)
    hidden = jax.nn.silu(act_first).astype(jnp.bfloat16)
    hidden32 = hidden.astype(jnp.float32)
    act_second = conv_full(hidden32, second32)
    top = jax.nn.silu(act_second)
    speed = jnp.tanh(jnp.einsum('c,czyx->zyx', speed_weight, top, precision=high))
    phi_start = 2.0 * sign_map.astype(jnp.float32) - 1.0

    def march(speed_field):
        phi = phi_start
        for step in range(STEPS):
            phi = front(jnp.pad(phi, ((1, 1), (1, 1), (0, 0))), speed_field)
        return phi
    final, back = jax.vjp(march, speed)
    d_phi = jax.nn.sigmoid(final) - labels.astype(jnp.float32)
    d_speed = back(d_phi)[0]
    d_pre = d_speed * (1.0 - speed * speed)
    raw_speed = jnp.einsum('zyx,czyx->c', d_pre, top, precision=high)
    d_second = (speed_weight[:, None, None, None] * d_pre[None] * silu_slope(act_second)).astype(jnp.bfloat16)
    back_second = jax.vjp(conv_full, hidden32, second32)[1]
    d_hidden, raw_second = back_second(d_second.astype(jnp.float32))
    d_first = (d_hidden * silu_slope(act_first)).astype(jnp.bfloat16)
    back_first = jax.vjp(conv_full, feat32, first32)[1]
    d_feat, raw_first = back_first(d_first.astype(jnp.float32))
    total = jnp.sum(raw_first * raw_first) + jnp.sum(raw_second * raw_second) + jnp.sum(raw_speed * raw_speed)
    count = 54.0 * C * C + C
    factor = 1.0 / jnp.maximum(jnp.sqrt(total) / jnp.sqrt(jnp.float32(count)), 1.0)
    return (d_feat.astype(jnp.bfloat16), raw_first * factor, raw_second * factor, raw_speed * factor)
```

```python
import jax
import jax.numpy as jnp
from jax import lax
from jax.experimental import pallas as pl
from jax.experimental.pallas import tpu as pltpu
from jax.sharding import PartitionSpec as P

C = 16
BZ = 4
BY = 8
X = 128
TAPS = 27 * C
A = 0.25
FLOOR = 0.1
SENT = jnp.bfloat16
f32 = jnp.float32
bf16 = jnp.bfloat16


def sides(v):
    axis = v.ndim - 1
    lane = lax.broadcasted_iota(jnp.int32, v.shape, axis)
    low = jnp.where(lane == 0, 0.0, pltpu.roll(v, 1, axis))
    up = jnp.where(lane == X - 1, 0.0, pltpu.roll(v, X - 1, axis))
    return low, up


def put_taps(ref, index, v):
    low, up = sides(v)
    ref[index, :, 0] = low.astype(bf16)
    ref[index, :, 1] = v.astype(bf16)
    ref[index, :, 2] = up.astype(bf16)


def two_rows(weight, taps_ref, z, y):
    patch = taps_ref[pl.ds(z, 3), y : y + 4].reshape(4 * 9 * C, X)
    out = jnp.dot(weight, patch, preferred_element_type=f32)
    return out[:C], out[C:]


def inside(start, shape, limit):
    row = start + lax.broadcasted_iota(jnp.int32, shape, 0)
    return (row >= 0) & (row < limit)


def prepare(at, f_ref, s_ref, ft_ref, me_ref, mo_ref):
    py = at[3]
    row = lax.broadcasted_iota(jnp.int32, (BY, X), 0)
    for z in range(BZ):
        ft_ref[z] = jnp.transpose(f_ref[:, z].astype(f32), (1, 0, 2)).astype(bf16)
    for ref, start, high in ((me_ref, 6 - 6 * py, py == 0), (mo_ref, 6 * py, py == 1)):
        for z in range(BZ):
            ref[2 * z : 2 * z + 2] = ft_ref[z, pl.ds(start, 2)]
        parts = []
        for z in range(BZ):
            own = s_ref[z].astype(f32)
            parts.append(jnp.where(high, pltpu.roll(own, 4, 0), own))
        halves = [jnp.where(row < 4, parts[i], pltpu.roll(parts[i + 1], 4, 0)) for i in (0, 2)]
        ref[2 * BZ] = jnp.concatenate(halves, axis=0).astype(bf16)


def extend(at, ft_ref, s_ref, re_ref, ro_ref, fy_ref, sy_ref, ma_ref, mb_ref):
    pz, py = at[2], at[3]
    row = lax.broadcasted_iota(jnp.int32, (BY, X), 0)
    te = re_ref[2 * BZ].astype(f32)
    to = ro_ref[2 * BZ].astype(f32)
    before = jnp.where(py == 0, to, te)
    after = jnp.where(py == 0, te, to)
    for z in range(BZ):
        fy_ref[z, 2 : 2 + BY] = ft_ref[z]
        fy_ref[z, pl.ds(10 - 10 * py, 2)] = re_ref[2 * z : 2 * z + 2]
        fy_ref[z, pl.ds(10 * py, 2)] = ro_ref[2 * z : 2 * z + 2]
        half, low = (z // 2) * 8, (z % 2) * 4
        own = pltpu.roll(s_ref[z].astype(f32), 4, 0)
        b = before[half : half + 8]
        a = after[half : half + 8]
        b = pltpu.roll(b, 4, 0) if low else b
        a = a if low else pltpu.roll(a, 4, 0)
        sy_ref[z] = jnp.concatenate([jnp.where(row < 4, b, own), jnp.where(row < 4, own, a)], axis=0)
    for ref, start, sign in ((ma_ref, 2 - 2 * pz, 1 - pz), (mb_ref, 2 * pz, pz)):
        for k in range(2):
            ref[12 * k : 12 * k + 12] = fy_ref[start + k]
        for k in range(3):
            ref[24 + k] = sy_ref[sign + k].astype(bf16)


def forward(nz, ny, at, fy_ref, sy_ref, ma_ref, mb_ref, lab_ref, w1_ref, w2_ref, sw_ref,
            fx_ref, hx_ref, slope1_ref, slope2_ref, top_ref, fields_ref, own_ref, g0_ref, p_ref):
    iz, iy, pz = at[0], at[1], at[2]
    for k in range(BZ):
        put_taps(fx_ref, 2 + k, fy_ref[k].astype(f32))
    for k in range(2):
        put_taps(fx_ref, 6 - 6 * pz + k, ma_ref[12 * k : 12 * k + 12].astype(f32))
        put_taps(fx_ref, 6 * pz + k, mb_ref[12 * k : 12 * k + 12].astype(f32))
    w1 = w1_ref[...]
    w2 = w2_ref[...]

    def first(z, carry):
        zg = iz * BZ - 1 + z
        zin = (zg >= 0) & (zg < nz)
        for y in range(0, BY + 2, 2):
            acts = two_rows(w1, fx_ref, z, y)
            hid = []
            for j, act in enumerate(acts):
                yg = iy * BY - 1 + y + j
                keep = jnp.where(zin & (yg >= 0) & (yg < ny), 1.0, 0.0)
                sig = jax.nn.sigmoid(act)
                slope1_ref[z, y + j] = sig * (1.0 + act * (1.0 - sig)) * keep
                hid.append((act * sig * keep)[None])
            hid = jnp.concatenate(hid, axis=0)
            low, up = sides(hid)
            hx_ref[z, y : y + 2, 0] = low.astype(bf16)
            hx_ref[z, y : y + 2, 1] = hid.astype(bf16)
            hx_ref[z, y : y + 2, 2] = up.astype(bf16)
        return carry

    lax.fori_loop(0, BZ + 2, first, 0)
    sw = sw_ref[...]

    def second(z, carry):
        rows = []
        for y in range(0, BY, 2):
            for j, act in enumerate(two_rows(w2, hx_ref, z, y)):
                sig = jax.nn.sigmoid(act)
                top = act * sig
                top_ref[z, y + j] = top
                slope2_ref[z, y + j] = sig * (1.0 + act * (1.0 - sig))
                rows.append(jnp.sum(top * sw, axis=0, keepdims=True))
        own_ref[0, z] = jnp.tanh(jnp.concatenate(rows, axis=0))
        return carry

    lax.fori_loop(0, BZ, second, 0)

    for k in range(BZ):
        p_ref[3 + k] = sy_ref[k]
    for k in range(3):
        p_ref[7 - 7 * pz + k] = ma_ref[24 + k].astype(f32)
        p_ref[7 * pz + k] = mb_ref[24 + k].astype(f32)
    rows_in = inside(iy * BY - 4, (16, X), ny)
    for k in range(10):
        zg = iz * BZ - 3 + k
        p_ref[k] = jnp.where(rows_in & (zg >= 0) & (zg < nz), 2.0 * p_ref[k] - 1.0, 0.0)
    for k in range(8):
        centre, uz, lz = p_ref[k + 1], p_ref[k + 2], p_ref[k]
        ly, uy = pltpu.roll(centre, 1, 0), pltpu.roll(centre, 15, 0)
        lx, ux = sides(centre)
        dz, dy, dx = (uz - lz) * 0.5, (uy - ly) * 0.5, (ux - lx) * 0.5
        g = jnp.sqrt(dz * dz + dy * dy + dx * dx + FLOOR)
        g0_ref[k] = g
        if 2 <= k < 6:
            lap = uz + lz + uy + ly + ux + lx - 6.0 * centre
            base = pltpu.roll(centre + (A * 0.5) * lap, 12, 0)[:8]
            own_ref[1, k - 2] = base + A * own_ref[0, k - 2] * pltpu.roll(g, 12, 0)[:8]
    for z in range(BZ):
        own_ref[2, z] = lab_ref[z].astype(f32)
    fields_ref[...] = own_ref[...].astype(fields_ref.dtype)


def march(nz, ny, at, own_ref, ye_ref, mate_ref, far_ref, far2_ref, g0_ref, dpre_ref,
          sp, lab, ph, w_s, dz_s, dy_s, dx_s, ag_s, ds, dd):
    iz, iy, pz, py = at[0], at[1], at[2], at[3]
    base = 4 * pz

    def place(start, block):
        for k in range(BZ):
            for ref, f in ((sp, 0), (ph, 1), (lab, 2)):
                plane = jnp.concatenate([block(i, f, k).astype(f32) for i in range(3)], axis=0)
                if f == 1:
                    ph[0, start + k] = plane
                else:
                    ref[start + k] = plane

    def mine(i, f, k):
        return own_ref[f, k] if i == 1 else ye_ref[i, f, k]

    place(8 + 4 * pz, mine)
    place(12 - 4 * pz, lambda i, f, k: mate_ref[i, f, k])
    place(16 * pz + 4 - 4 * pz, lambda i, f, k: far_ref[0, i, f, k])
    place(16 * pz + 4 * pz, lambda i, f, k: far_ref[1, i, f, k])
    place(16 - 16 * pz + 4 * pz, lambda i, f, k: far2_ref[0, i, f, k])
    place(16 - 16 * pz + 4 - 4 * pz, lambda i, f, k: far2_ref[1, i, f, k])

    dd[0, 0] = jnp.zeros((24, X), f32)
    rows_in = inside(iy * BY - 8, (24, X), ny)
    first_plane = (iz - pz) * BZ - 8

    def within(z):
        zg = first_plane + z
        return rows_in & (zg >= 0) & (zg < nz)

    for t in (1, 2, 3):

        def step(i, carry, t=t):
            z = base + i
            centre, uz, lz = ph[t - 1, z], ph[t - 1, z + 1], ph[t - 1, z - 1]
            ly, uy = pltpu.roll(centre, 1, 0), pltpu.roll(centre, 23, 0)
            lx, ux = sides(centre)
            dz, dy, dx = (uz - lz) * 0.5, (uy - ly) * 0.5, (ux - lx) * 0.5
            g = jnp.sqrt(dz * dz + dy * dy + dx * dx + FLOOR)
            lap = uz + lz + uy + ly + ux + lx - 6.0 * centre
            speed = sp[z]
            ag = A * g
            new = jnp.where(within(z), centre + speed * ag + (A * 0.5) * lap, 0.0)
            w_s[t - 1, z] = (A * 0.5) * speed / g
            dz_s[t - 1, z] = dz
            dy_s[t - 1, z] = dy
            dx_s[t - 1, z] = dx
            ag_s[t - 1, z] = ag
            if t < 3:
                ph[t, z] = new
            else:
                dd[0, z] = jnp.where(within(z), jax.nn.sigmoid(new) - lab[z], 0.0)
            return carry

        lax.fori_loop(t, 20 - t, step, 0)

    for n, t in enumerate((3, 2, 1)):
        src, dst = n % 2, (n + 1) % 2

        def back(i, carry, t=t, n=n, src=src, dst=dst):
            l1, a1, a2 = carry
            z = base + i
            d = dd[src, z]
            add = ag_s[t - 1, z] * d
            ds[z] = add if n == 0 else ds[z] + add
            w = w_s[t - 1, z] * d
            e = (A * 0.5) * d
            qz, qy, qx = w * dz_s[t - 1, z], w * dy_s[t - 1, z], w * dx_s[t - 1, z]
            local = (1.0 - 3.0 * A) * d
            local = local + pltpu.roll(e + qy, 1, 0) + pltpu.roll(e - qy, 23, 0)
            local = local + sides(e + qx)[0] + sides(e - qx)[1]
            dd[dst, z - 1] = jnp.where(within(z - 1), l1 + a2 + (e - qz), 0.0)
            return local, e + qz, a1

        zero = dd[0, 0]
        lax.fori_loop(2 + n + 1, 18 - n - 1, back, (zero, zero, zero))

    for k in range(8):
        z = base + 6 + k
        speed = sp[z]
        left = 1.0 - speed * speed
        one = pltpu.roll(ds[z] * left, 20, 0)[:16]
        two = pltpu.roll(dd[1, z] * left, 20, 0)[:16]
        dpre_ref[k] = one + A * two * g0_ref[k]


def backward(at, dpre_ref, slope2_ref, s2y_ref, sa_ref, sb_ref, sw_ref, hx_ref, fx_ref, slope1_ref,
             top_ref, w1_ref, w2_ref, df_ref, grad_ref, dx_ref, ex_ref):
    pz = at[2]
    sw = sw_ref[...]

    def second(z, k, slope):
        for y in range(BY + 4):
            d = dpre_ref[z, 2 + y : 3 + y, :]
            value = (sw * d * slope(y))[None]
            low, up = sides(value)
            dx_ref[z, y : y + 1, 0] = low.astype(bf16)
            dx_ref[z, y : y + 1, 1] = value.astype(bf16)
            dx_ref[z, y : y + 1, 2] = up.astype(bf16)

    for k in range(BZ):
        def own(y, k=k):
            if 2 <= y < 2 + BY:
                return slope2_ref[k, y - 2]
            return s2y_ref[k, y].astype(f32)
        second(2 + k, k, own)
    for k in range(2):
        second(6 - 6 * pz + k, k, lambda y, k=k: sa_ref[k, y].astype(f32))
        second(6 * pz + k, k, lambda y, k=k: sb_ref[k, y].astype(f32))

    w2 = w2_ref[...]
    w1 = w1_ref[...]

    def hidden(z, carry):
        for y in range(0, BY + 2, 2):
            both = two_rows(w2, dx_ref, z, y)
            d = jnp.concatenate([(v * slope1_ref[z, y + j])[None] for j, v in enumerate(both)], axis=0)
            low, up = sides(d)
            ex_ref[z, y : y + 2, 0] = low.astype(bf16)
            ex_ref[z, y : y + 2, 1] = d.astype(bf16)
            ex_ref[z, y : y + 2, 2] = up.astype(bf16)
        return carry

    lax.fori_loop(0, BZ + 2, hidden, 0)

    def features(z, carry):
        rows = []
        for y in range(0, BY, 2):
            a, b = two_rows(w1, ex_ref, z, y)
            rows += [a[None], b[None]]
        plane = jnp.concatenate(rows, axis=0)
        df_ref[:, z] = jnp.transpose(plane, (1, 0, 2)).astype(bf16)
        return carry

    lax.fori_loop(0, BZ, features, 0)

    nt = (((1,), (1,)), ((), ()))

    def weights(z, carry):
        g1, g2, gs = carry
        for y in range(BY):
            d2 = dx_ref[z + 2, y + 2, 1]
            d1 = ex_ref[z + 1, y + 1, 1]
            p2 = hx_ref[pl.ds(z, 3), y : y + 3].reshape(TAPS, X)
            p1 = fx_ref[pl.ds(z + 1, 3), y + 1 : y + 4].reshape(TAPS, X)
            g2 = g2 + lax.dot_general(d2, p2, nt, preferred_element_type=f32)
            g1 = g1 + lax.dot_general(d1, p1, nt, preferred_element_type=f32)
            gs = gs + dpre_ref[z + 2, 4 + y : 5 + y, :] * top_ref[z, y]
        return g1, g2, gs

    zero = jnp.zeros((C, TAPS), f32)
    g1, g2, gs = lax.fori_loop(0, BZ, weights, (zero, zero, jnp.zeros((C, X), f32)))
    grad_ref[...] = jnp.zeros_like(grad_ref)
    grad_ref[0, :, :TAPS] = g1
    grad_ref[1, :, :TAPS] = g2
    grad_ref[0, :, TAPS : TAPS + 1] = jnp.sum(gs, axis=1, keepdims=True)


def finish(a_ref, b_ref, out_ref):
    a, b = a_ref[...], b_ref[...]
    total = jnp.sum(a * a) + jnp.sum(b * b)
    count = 54.0 * C * C + C
    factor = 1.0 / jnp.maximum(jnp.sqrt(jnp.full((1, 1), total)) / jnp.sqrt(f32(count)), 1.0)
    out_ref[0] = a * factor
    out_ref[1] = b * factor


def call(kernel, outs, scratch=(), flops=0):
    smem = pl.BlockSpec(memory_space=pltpu.SMEM)
    vmem = pl.BlockSpec(memory_space=pltpu.VMEM)

    def run(at, *args):
        args = ((at,) if at is not None else ()) + args
        specs = [smem if (i == 0 and at is not None) else vmem for i in range(len(args))]
        many = isinstance(outs, (list, tuple))
        size = sum(a.size * a.dtype.itemsize for a in args)
        return pl.pallas_call(
            kernel,
            out_shape=outs,
            in_specs=specs,
            out_specs=[vmem] * len(outs) if many else vmem,
            scratch_shapes=list(scratch),
            cost_estimate=pl.CostEstimate(flops=flops, bytes_accessed=size, transcendentals=0),
            compiler_params=pltpu.CompilerParams(vmem_limit_bytes=40 * 1024 * 1024),
        )(*args)

    return run


def shape(dims, dtype=bf16):
    return jax.ShapeDtypeStruct(dims, dtype)


def even(value, axis):
    n = lax.axis_size(axis)
    return lax.ppermute(value, axis, [(i, i ^ 1) for i in range(n)])


def odd(value, axis):
    n = lax.axis_size(axis)
    pairs = [(i, i + 1) for i in range(1, n - 1, 2)]
    return lax.ppermute(value, axis, pairs + [(j, i) for i, j in pairs])


def row_weights(taps_last):
    first = jnp.pad(taps_last, ((0, 0), (0, 0), (0, 1), (0, 0)))
    second = jnp.pad(taps_last, ((0, 0), (0, 0), (1, 0), (0, 0)))
    return jnp.concatenate([first, second], axis=0).reshape(2 * C, 36 * C)


def taps_of(weight):
    return weight.transpose(0, 2, 3, 4, 1).reshape(C, 3, 3, 3 * C)


def taps_back(weight):
    return jnp.flip(weight, (2, 3, 4)).transpose(1, 2, 3, 4, 0).reshape(C, 3, 3, 3 * C)


def total_of(grad, iz):
    core = iz % 2
    keep = lax.dynamic_index_in_dim(grad, core, 0, keepdims=False)
    give = lax.dynamic_index_in_dim(grad, 1 - core, 0, keepdims=False)
    part = keep + even(give, "gz")
    for axis, masks in (("gy", (1, 3, 4, 8)), ("gz", (8, 24, 2, 6))):
        n = lax.axis_size(axis)
        for mask in masks:
            if mask < n:
                part = part + lax.ppermute(part, axis, [(i, i ^ mask) for i in range(n)])
    other = even(part, "gz")
    return jnp.where(core == 0, part, other), jnp.where(core == 0, other, part)


def on_device(features, labels, sign_map, conv_first, conv_second, speed_weight):
    nz, ny = BZ * lax.axis_size("gz"), BY * lax.axis_size("gy")
    iz, iy = lax.axis_index("gz"), lax.axis_index("gy")
    pz, py = iz % 2, iy % 2
    at = jnp.stack([iz, iy, pz, py]).astype(jnp.int32)
    sw = jnp.broadcast_to(speed_weight[:, None], (C, X))
    w1, w2 = row_weights(taps_of(conv_first)), row_weights(taps_of(conv_second))
    w1b, w2b = row_weights(taps_back(conv_first)), row_weights(taps_back(conv_second))

    ft, me, mo = call(prepare, [shape((BZ, BY, C, X)), shape((9, C, X)), shape((9, C, X))])(
        at, features, sign_map
    )
    re, ro = even(me, "gy"), odd(mo, "gy")
    fy, sy, ma, mb = call(
        extend,
        [shape((BZ, 12, C, X)), shape((BZ, 16, X), f32), shape((27, C, X)), shape((27, C, X))],
    )(at, ft, sign_map, re, ro)
    ra, rb = even(ma, "gz"), odd(mb, "gz")

    fx, hx, slope1, slope2, top, fields, own, g0 = call(
        lambda *refs: forward(nz, ny, *refs),
        [
            shape((8, 12, 3, C, X)),
            shape((6, 10, 3, C, X)),
            shape((6, 10, C, X), f32),
            shape((BZ, BY, C, X), f32),
            shape((BZ, BY, C, X), f32),
            shape((3, BZ, BY, X), SENT),
            shape((3, BZ, BY, X), f32),
            shape((8, 16, X), f32),
        ],
        [pltpu.VMEM((10, 16, X), f32)],
    )(at, fy, sy, ra, rb, labels, w1, w2, sw)

    fe, fo = even(fields, "gy"), odd(fields, "gy")
    before, after = jnp.where(py == 0, fo, fe), jnp.where(py == 0, fe, fo)
    ye = jnp.stack([before, fields, after])
    mate = even(ye, "gz")
    far = odd(jnp.stack([ye, mate]), "gz")
    far2 = even(far, "gz")

    s2 = slope2.astype(bf16)
    se = even(lax.dynamic_slice_in_dim(s2, 6 - 6 * py, 2, 1), "gy")
    so = odd(lax.dynamic_slice_in_dim(s2, 6 * py, 2, 1), "gy")
    s2y = jnp.concatenate([jnp.where(py == 0, so, se), s2, jnp.where(py == 0, se, so)], axis=1)
    sa = even(lax.dynamic_slice_in_dim(s2y, 2 - 2 * pz, 2, 0), "gz")
    sb = odd(lax.dynamic_slice_in_dim(s2y, 2 * pz, 2, 0), "gz")

    plane = (24, 24, X)
    dpre = call(
        lambda *refs: march(nz, ny, *refs),
        shape((8, 16, X), f32),
        [
            pltpu.VMEM(plane, f32),
            pltpu.VMEM(plane, f32),
            pltpu.VMEM((3,) + plane, f32),
            pltpu.VMEM((3,) + plane, f32),
            pltpu.VMEM((3,) + plane, f32),
            pltpu.VMEM((3,) + plane, f32),
            pltpu.VMEM((3,) + plane, f32),
            pltpu.VMEM((3,) + plane, f32),
            pltpu.VMEM(plane, f32),
            pltpu.VMEM((2,) + plane, f32),
        ],
    )(at, own, ye, mate, far, far2, g0)

    d_features, grad = call(
        backward,
        [shape((C, BZ, BY, X)), shape((2, C, 512), f32)],
        [pltpu.VMEM((8, 12, 3, C, X), bf16), pltpu.VMEM((6, 10, 3, C, X), bf16)],
    )(at, dpre, slope2, s2y, sa, sb, sw, hx, fx, slope1, top, w1b, w2b)

    a, b = total_of(grad, iz)
    out = call(finish, shape((2, C, 512), f32))(None, a, b)
    first, second = (
        out[i, :, :TAPS].reshape(C, 3, 3, 3, C).transpose(0, 4, 1, 2, 3) for i in range(2)
    )
    return d_features, first, second, out[0, :, TAPS]


def solution(mesh):
    in_specs = (P(None, "gz", "gy", None), P("gz", "gy", None), P("gz", "gy", None), P(), P(), P())
    out_specs = (P(None, "gz", "gy", None), P(), P(), P())
    return jax.shard_map(
        on_device, mesh=mesh, in_specs=in_specs, out_specs=out_specs, check_vma=False
    )
```

```python
import jax
import jax.numpy as jnp
from jax import lax
from jax.experimental import pallas as pl
from jax.experimental.pallas import tpu as pltpu
from jax.sharding import PartitionSpec as P

C = 16
BZ = 4
BY = 8
X = 128
TAPS = 27 * C
A = 0.25
FLOOR = 0.1
SENT = jnp.bfloat16
f32 = jnp.float32
bf16 = jnp.bfloat16


def sides(v):
    axis = v.ndim - 1
    lane = lax.broadcasted_iota(jnp.int32, v.shape, axis)
    low = jnp.where(lane == 0, 0.0, pltpu.roll(v, 1, axis))
    up = jnp.where(lane == X - 1, 0.0, pltpu.roll(v, X - 1, axis))
    return low, up


def put_taps(ref, index, v):
    low, up = sides(v)
    ref[index, :, 0] = low.astype(bf16)
    ref[index, :, 1] = v.astype(bf16)
    ref[index, :, 2] = up.astype(bf16)


def two_rows(weight, taps_ref, z, y):
    patch = taps_ref[pl.ds(z, 3), y : y + 4].reshape(4 * 9 * C, X)
    out = jnp.dot(weight, patch, preferred_element_type=f32)
    return out[:C], out[C:]


def inside(start, shape, limit):
    row = start + lax.broadcasted_iota(jnp.int32, shape, 0)
    return (row >= 0) & (row < limit)


def prepare(at, f_ref, s_ref, ft_ref, me_ref, mo_ref):
    py = at[3]
    row = lax.broadcasted_iota(jnp.int32, (BY, X), 0)
    for z in range(BZ):
        ft_ref[z] = jnp.transpose(f_ref[:, z].astype(f32), (1, 0, 2)).astype(bf16)
    for ref, start, high in ((me_ref, 6 - 6 * py, py == 0), (mo_ref, 6 * py, py == 1)):
        for z in range(BZ):
            ref[2 * z : 2 * z + 2] = ft_ref[z, pl.ds(start, 2)]
        parts = []
        for z in range(BZ):
            own = s_ref[z].astype(f32)
            parts.append(jnp.where(high, pltpu.roll(own, 4, 0), own))
        halves = [jnp.where(row < 4, parts[i], pltpu.roll(parts[i + 1], 4, 0)) for i in (0, 2)]
        ref[2 * BZ] = jnp.concatenate(halves, axis=0).astype(bf16)


def extend(at, ft_ref, s_ref, re_ref, ro_ref, fy_ref, sy_ref, ma_ref, mb_ref):
    pz, py = at[2], at[3]
    row = lax.broadcasted_iota(jnp.int32, (BY, X), 0)
    te = re_ref[2 * BZ].astype(f32)
    to = ro_ref[2 * BZ].astype(f32)
    before = jnp.where(py == 0, to, te)
    after = jnp.where(py == 0, te, to)
    for z in range(BZ):
        fy_ref[z, 2 : 2 + BY] = ft_ref[z]
        fy_ref[z, pl.ds(10 - 10 * py, 2)] = re_ref[2 * z : 2 * z + 2]
        fy_ref[z, pl.ds(10 * py, 2)] = ro_ref[2 * z : 2 * z + 2]
        half, low = (z // 2) * 8, (z % 2) * 4
        own = pltpu.roll(s_ref[z].astype(f32), 4, 0)
        b = before[half : half + 8]
        a = after[half : half + 8]
        b = pltpu.roll(b, 4, 0) if low else b
        a = a if low else pltpu.roll(a, 4, 0)
        sy_ref[z] = jnp.concatenate([jnp.where(row < 4, b, own), jnp.where(row < 4, own, a)], axis=0)
    for ref, start, sign in ((ma_ref, 2 - 2 * pz, 1 - pz), (mb_ref, 2 * pz, pz)):
        for k in range(2):
            ref[12 * k : 12 * k + 12] = fy_ref[start + k]
        for k in range(3):
            ref[24 + k] = sy_ref[sign + k].astype(bf16)


def forward(nz, ny, at, fy_ref, sy_ref, ma_ref, mb_ref, lab_ref, w1_ref, w2_ref, sw_ref,
            fx_ref, hx_ref, slope1_ref, slope2_ref, top_ref, me_ref, mo_ref, own_ref, g0_ref, p_ref):
    iz, iy, pz, py = at[0], at[1], at[2], at[3]
    for k in range(BZ):
        put_taps(fx_ref, 2 + k, fy_ref[k].astype(f32))
    for k in range(2):
        put_taps(fx_ref, 6 - 6 * pz + k, ma_ref[12 * k : 12 * k + 12].astype(f32))
        put_taps(fx_ref, 6 * pz + k, mb_ref[12 * k : 12 * k + 12].astype(f32))
    w1 = w1_ref[...]
    w2 = w2_ref[...]

    def first(z, carry):
        zg = iz * BZ - 1 + z
        zin = (zg >= 0) & (zg < nz)
        for y in range(0, BY + 2, 2):
            acts = two_rows(w1, fx_ref, z, y)
            hid = []
            for j, act in enumerate(acts):
                yg = iy * BY - 1 + y + j
                keep = jnp.where(zin & (yg >= 0) & (yg < ny), 1.0, 0.0)
                sig = jax.nn.sigmoid(act)
                slope1_ref[z, y + j] = sig * (1.0 + act * (1.0 - sig)) * keep
                hid.append((act * sig * keep)[None])
            hid = jnp.concatenate(hid, axis=0)
            low, up = sides(hid)
            hx_ref[z, y : y + 2, 0] = low.astype(bf16)
            hx_ref[z, y : y + 2, 1] = hid.astype(bf16)
            hx_ref[z, y : y + 2, 2] = up.astype(bf16)
        return carry

    lax.fori_loop(0, BZ + 2, first, 0)
    sw = sw_ref[...]

    def second(z, carry):
        rows = []
        for y in range(0, BY, 2):
            for j, act in enumerate(two_rows(w2, hx_ref, z, y)):
                sig = jax.nn.sigmoid(act)
                top = act * sig
                top_ref[z, y + j] = top
                slope2_ref[z, y + j] = sig * (1.0 + act * (1.0 - sig))
                rows.append(jnp.sum(top * sw, axis=0, keepdims=True))
        own_ref[0, z] = jnp.tanh(jnp.concatenate(rows, axis=0))
        return carry

    lax.fori_loop(0, BZ, second, 0)

    for k in range(BZ):
        p_ref[3 + k] = sy_ref[k]
    for k in range(3):
        p_ref[7 - 7 * pz + k] = ma_ref[24 + k].astype(f32)
        p_ref[7 * pz + k] = mb_ref[24 + k].astype(f32)
    rows_in = inside(iy * BY - 4, (16, X), ny)
    for k in range(10):
        zg = iz * BZ - 3 + k
        p_ref[k] = jnp.where(rows_in & (zg >= 0) & (zg < nz), 2.0 * p_ref[k] - 1.0, 0.0)
    for k in range(8):
        centre, uz, lz = p_ref[k + 1], p_ref[k + 2], p_ref[k]
        ly, uy = pltpu.roll(centre, 1, 0), pltpu.roll(centre, 15, 0)
        lx, ux = sides(centre)
        dz, dy, dx = (uz - lz) * 0.5, (uy - ly) * 0.5, (ux - lx) * 0.5
        g = jnp.sqrt(dz * dz + dy * dy + dx * dx + FLOOR)
        g0_ref[k] = g
        if 2 <= k < 6:
            lap = uz + lz + uy + ly + ux + lx - 6.0 * centre
            base = pltpu.roll(centre + (A * 0.5) * lap, 12, 0)[:8]
            own_ref[1, k - 2] = base + A * own_ref[0, k - 2] * pltpu.roll(g, 12, 0)[:8]
    for z in range(BZ):
        own_ref[2, z] = lab_ref[z].astype(f32)
    for ref, start in ((me_ref, 6 - 6 * py), (mo_ref, 6 * py)):
        ref[:12] = own_ref[...].reshape(12, BY, X).astype(SENT)
        for z in range(BZ):
            ref[12 + 4 * z : 16 + 4 * z] = slope2_ref[z, pl.ds(start, 2)].reshape(4, 8, X).astype(SENT)


def widen(at, me_ref, slope2_ref, re_ref, ro_ref, ma_ref, s2y_ref):
    pz, py = at[2], at[3]
    ma_ref[12:24] = me_ref[:12]
    ma_ref[pl.ds(24 - 24 * py, 12)] = re_ref[:12]
    ma_ref[pl.ds(24 * py, 12)] = ro_ref[:12]
    for z in range(BZ):
        s2y_ref[z, 2 : 2 + BY] = slope2_ref[z].astype(bf16)
        for ref, start in ((re_ref, 10 - 10 * py), (ro_ref, 10 * py)):
            rows = ref[12 + 4 * z : 16 + 4 * z].astype(f32).reshape(2, C, X)
            s2y_ref[z, pl.ds(start, 2)] = rows.astype(bf16)
    for k in range(2):
        rows = s2y_ref[2 - 2 * pz + k].astype(f32).reshape(24, 8, X)
        ma_ref[36 + 24 * k : 60 + 24 * k] = rows.astype(SENT)


def relay(at, ma_ref, ra_ref, s2y_ref, mb_ref):
    pz = at[2]
    mb_ref[:36] = ma_ref[:36]
    mb_ref[36:72] = ra_ref[:36]
    for k in range(2):
        rows = s2y_ref[2 * pz + k].astype(f32).reshape(24, 8, X)
        mb_ref[72 + 24 * k : 96 + 24 * k] = rows.astype(SENT)


def march(nz, ny, at, own_ref, ye_ref, mate_ref, far_ref, far2_ref, g0_ref, dpre_ref,
          sp, lab, ph, w_s, dz_s, dy_s, dx_s, ag_s, ds, dd):
    iz, iy, pz, py = at[0], at[1], at[2], at[3]
    base = 4 * pz

    def place(start, block):
        for k in range(BZ):
            for ref, f in ((sp, 0), (ph, 1), (lab, 2)):
                plane = jnp.concatenate([block(i, f, k).astype(f32) for i in range(3)], axis=0)
                if f == 1:
                    ph[0, start + k] = plane
                else:
                    ref[start + k] = plane

    def piece(ref, first):
        return lambda i, f, k: ref[first + 12 * i + 4 * f + k]

    def mine(i, f, k):
        return own_ref[f, k] if i == 1 else ye_ref[12 * i + 4 * f + k]

    place(8 + 4 * pz, mine)
    place(12 - 4 * pz, piece(mate_ref, 0))
    place(16 * pz + 4 - 4 * pz, piece(far_ref, 0))
    place(16 * pz + 4 * pz, piece(far_ref, 36))
    place(16 - 16 * pz + 4 * pz, piece(far2_ref, 0))
    place(16 - 16 * pz + 4 - 4 * pz, piece(far2_ref, 36))

    dd[0, 0] = jnp.zeros((24, X), f32)
    rows_in = inside(iy * BY - 8, (24, X), ny)
    first_plane = (iz - pz) * BZ - 8

    def within(z):
        zg = first_plane + z
        return rows_in & (zg >= 0) & (zg < nz)

    for t in (1, 2, 3):

        def step(i, carry, t=t):
            z = base + i
            centre, uz, lz = ph[t - 1, z], ph[t - 1, z + 1], ph[t - 1, z - 1]
            ly, uy = pltpu.roll(centre, 1, 0), pltpu.roll(centre, 23, 0)
            lx, ux = sides(centre)
            dz, dy, dx = (uz - lz) * 0.5, (uy - ly) * 0.5, (ux - lx) * 0.5
            g = jnp.sqrt(dz * dz + dy * dy + dx * dx + FLOOR)
            lap = uz + lz + uy + ly + ux + lx - 6.0 * centre
            speed = sp[z]
            ag = A * g
            new = jnp.where(within(z), centre + speed * ag + (A * 0.5) * lap, 0.0)
            w_s[t - 1, z] = (A * 0.5) * speed / g
            dz_s[t - 1, z] = dz
            dy_s[t - 1, z] = dy
            dx_s[t - 1, z] = dx
            ag_s[t - 1, z] = ag
            if t < 3:
                ph[t, z] = new
            else:
                dd[0, z] = jnp.where(within(z), jax.nn.sigmoid(new) - lab[z], 0.0)
            return carry

        lax.fori_loop(t, 20 - t, step, 0, unroll=2)

    for n, t in enumerate((3, 2, 1)):
        src, dst = n % 2, (n + 1) % 2

        def back(i, carry, t=t, n=n, src=src, dst=dst):
            l1, a1, a2 = carry
            z = base + i
            d = dd[src, z]
            add = ag_s[t - 1, z] * d
            ds[z] = add if n == 0 else ds[z] + add
            w = w_s[t - 1, z] * d
            e = (A * 0.5) * d
            qz, qy, qx = w * dz_s[t - 1, z], w * dy_s[t - 1, z], w * dx_s[t - 1, z]
            local = (1.0 - 3.0 * A) * d
            local = local + pltpu.roll(e + qy, 1, 0) + pltpu.roll(e - qy, 23, 0)
            local = local + sides(e + qx)[0] + sides(e - qx)[1]
            dd[dst, z - 1] = jnp.where(within(z - 1), l1 + a2 + (e - qz), 0.0)
            return local, e + qz, a1

        zero = dd[0, 0]
        lax.fori_loop(3 + n, 17 - n, back, (zero, zero, zero), unroll=2)

    for k in range(8):
        z = base + 6 + k
        speed = sp[z]
        left = 1.0 - speed * speed
        one = pltpu.roll(ds[z] * left, 20, 0)[:16]
        two = pltpu.roll(dd[1, z] * left, 20, 0)[:16]
        dpre_ref[k] = one + A * two * g0_ref[k]


def backward(at, dpre_ref, slope2_ref, s2y_ref, ra_ref, rb_ref, sw_ref, hx_ref, fx_ref, slope1_ref,
             top_ref, w1_ref, w2_ref, df_ref, grad_ref, dx_ref, ex_ref):
    pz = at[2]
    sw = sw_ref[...]

    def second(z, k, slope):
        for y in range(BY + 4):
            d = dpre_ref[z, 2 + y : 3 + y, :]
            value = (sw * d * slope(y))[None]
            low, up = sides(value)
            dx_ref[z, y : y + 1, 0] = low.astype(bf16)
            dx_ref[z, y : y + 1, 1] = value.astype(bf16)
            dx_ref[z, y : y + 1, 2] = up.astype(bf16)

    for k in range(BZ):
        def own(y, k=k):
            if 2 <= y < 2 + BY:
                return slope2_ref[k, y - 2]
            return s2y_ref[k, y].astype(f32)
        second(2 + k, k, own)
    for k in range(2):
        for ref, first, z in ((ra_ref, 36, 6 - 6 * pz), (rb_ref, 72, 6 * pz)):
            def far(y, ref=ref, first=first + 24 * k):
                return ref[first + 2 * y : first + 2 * y + 2].astype(f32).reshape(C, X)
            second(z + k, k, far)

    w2 = w2_ref[...]
    w1 = w1_ref[...]

    def hidden(z, carry):
        for y in range(0, BY + 2, 2):
            both = two_rows(w2, dx_ref, z, y)
            d = jnp.concatenate([(v * slope1_ref[z, y + j])[None] for j, v in enumerate(both)], axis=0)
            low, up = sides(d)
            ex_ref[z, y : y + 2, 0] = low.astype(bf16)
            ex_ref[z, y : y + 2, 1] = d.astype(bf16)
            ex_ref[z, y : y + 2, 2] = up.astype(bf16)
        return carry

    lax.fori_loop(0, BZ + 2, hidden, 0)

    def features(z, carry):
        rows = []
        for y in range(0, BY, 2):
            a, b = two_rows(w1, ex_ref, z, y)
            rows += [a[None], b[None]]
        plane = jnp.concatenate(rows, axis=0)
        df_ref[:, z] = jnp.transpose(plane, (1, 0, 2)).astype(bf16)
        return carry

    lax.fori_loop(0, BZ, features, 0)

    nt = (((1,), (1,)), ((), ()))

    def weights(z, carry):
        g1, g2, gs = carry
        d2 = jnp.concatenate([dx_ref[z + 2, y + 2, 1] for y in range(BY)], axis=1)
        d1 = jnp.concatenate([ex_ref[z + 1, y + 1, 1] for y in range(BY)], axis=1)
        p2 = [hx_ref[pl.ds(z, 3), y : y + 3].reshape(TAPS, X) for y in range(BY)]
        p1 = [fx_ref[pl.ds(z + 1, 3), y + 1 : y + 4].reshape(TAPS, X) for y in range(BY)]
        g2 = g2 + lax.dot_general(d2, jnp.concatenate(p2, axis=1), nt, preferred_element_type=f32)
        g1 = g1 + lax.dot_general(d1, jnp.concatenate(p1, axis=1), nt, preferred_element_type=f32)
        for y in range(BY):
            gs = gs + dpre_ref[z + 2, 4 + y : 5 + y, :] * top_ref[z, y]
        return g1, g2, gs

    zero = jnp.zeros((C, TAPS), f32)
    g1, g2, gs = lax.fori_loop(0, BZ, weights, (zero, zero, jnp.zeros((C, X), f32)))
    grad_ref[...] = jnp.zeros_like(grad_ref)
    grad_ref[0, :, :TAPS] = g1
    grad_ref[1, :, :TAPS] = g2
    grad_ref[0, :, TAPS : TAPS + 1] = jnp.sum(gs, axis=1, keepdims=True)


def finish(a_ref, b_ref, out_ref):
    a, b = a_ref[...], b_ref[...]
    total = jnp.sum(a * a) + jnp.sum(b * b)
    count = 54.0 * C * C + C
    factor = 1.0 / jnp.maximum(jnp.sqrt(jnp.full((1, 1), total)) / jnp.sqrt(f32(count)), 1.0)
    out_ref[0] = a * factor
    out_ref[1] = b * factor


def call(kernel, outs, scratch=(), flops=0):
    smem = pl.BlockSpec(memory_space=pltpu.SMEM)
    vmem = pl.BlockSpec(memory_space=pltpu.VMEM)

    def run(at, *args):
        args = ((at,) if at is not None else ()) + args
        specs = [smem if (i == 0 and at is not None) else vmem for i in range(len(args))]
        many = isinstance(outs, (list, tuple))
        size = sum(a.size * a.dtype.itemsize for a in args)
        return pl.pallas_call(
            kernel,
            out_shape=outs,
            in_specs=specs,
            out_specs=[vmem] * len(outs) if many else vmem,
            scratch_shapes=list(scratch),
            cost_estimate=pl.CostEstimate(flops=flops, bytes_accessed=size, transcendentals=0),
            compiler_params=pltpu.CompilerParams(vmem_limit_bytes=16 * 1024 * 1024),
        )(*args)

    return run


def shape(dims, dtype=bf16):
    return jax.ShapeDtypeStruct(dims, dtype)


def even(value, axis):
    n = lax.axis_size(axis)
    return lax.ppermute(value, axis, [(i, i ^ 1) for i in range(n)])


def odd(value, axis):
    n = lax.axis_size(axis)
    pairs = [(i, i + 1) for i in range(1, n - 1, 2)]
    return lax.ppermute(value, axis, pairs + [(j, i) for i, j in pairs])


def row_weights(taps_last):
    first = jnp.pad(taps_last, ((0, 0), (0, 0), (0, 1), (0, 0)))
    second = jnp.pad(taps_last, ((0, 0), (0, 0), (1, 0), (0, 0)))
    return jnp.concatenate([first, second], axis=0).reshape(2 * C, 36 * C)


def taps_of(weight):
    return weight.transpose(0, 2, 3, 4, 1).reshape(C, 3, 3, 3 * C)


def taps_back(weight):
    return jnp.flip(weight, (2, 3, 4)).transpose(1, 2, 3, 4, 0).reshape(C, 3, 3, 3 * C)


def total_of(grad, iz):
    core = iz % 2
    keep = lax.dynamic_index_in_dim(grad, core, 0, keepdims=False)
    give = lax.dynamic_index_in_dim(grad, 1 - core, 0, keepdims=False)
    part = keep + even(give, "gz")
    for axis, unit in (("gy", 1), ("gy", 4), ("gz", 8), ("gz", 2)):
        n = lax.axis_size(axis)
        masks = [m * unit for m in (1, 2, 3) if m * unit < n]
        got = [lax.ppermute(part, axis, [(i, i ^ m) for i in range(n)]) for m in masks]
        if len(got) == 3:
            part = (part + got[0]) + (got[1] + got[2])
        elif got:
            part = part + got[0]
    other = even(part, "gz")
    return jnp.where(core == 0, part, other), jnp.where(core == 0, other, part)


def on_device(features, labels, sign_map, conv_first, conv_second, speed_weight):
    nz, ny = BZ * lax.axis_size("gz"), BY * lax.axis_size("gy")
    iz, iy = lax.axis_index("gz"), lax.axis_index("gy")
    pz, py = iz % 2, iy % 2
    at = jnp.stack([iz, iy, pz, py]).astype(jnp.int32)
    sw = jnp.broadcast_to(speed_weight[:, None], (C, X))
    w1, w2 = row_weights(taps_of(conv_first)), row_weights(taps_of(conv_second))
    w1b, w2b = row_weights(taps_back(conv_first)), row_weights(taps_back(conv_second))

    ft, me, mo = call(prepare, [shape((BZ, BY, C, X)), shape((9, C, X)), shape((9, C, X))])(
        at, features, sign_map
    )
    re, ro = even(me, "gy"), odd(mo, "gy")
    fy, sy, ma, mb = call(
        extend,
        [shape((BZ, 12, C, X)), shape((BZ, 16, X), f32), shape((27, C, X)), shape((27, C, X))],
    )(at, ft, sign_map, re, ro)
    ra, rb = even(ma, "gz"), odd(mb, "gz")

    fx, hx, slope1, slope2, top, fe, fo, own, g0 = call(
        lambda *refs: forward(nz, ny, *refs),
        [
            shape((8, 12, 3, C, X)),
            shape((6, 10, 3, C, X)),
            shape((6, 10, C, X), f32),
            shape((BZ, BY, C, X), f32),
            shape((BZ, BY, C, X), f32),
            shape((28, 8, X), SENT),
            shape((28, 8, X), SENT),
            shape((3, BZ, BY, X), f32),
            shape((8, 16, X), f32),
        ],
        [pltpu.VMEM((10, 16, X), f32)],
    )(at, fy, sy, ra, rb, labels, w1, w2, sw)

    ge, go = even(fe, "gy"), odd(fo, "gy")
    fa, s2y = call(widen, [shape((84, 8, X), SENT), shape((BZ, 12, C, X))])(at, fe, slope2, ge, go)
    ha = even(fa, "gz")
    fb = call(relay, shape((120, 8, X), SENT))(at, fa, ha, s2y)
    hb = odd(fb, "gz")
    hc = even(hb[:72], "gz")

    plane = (24, 24, X)
    dpre = call(
        lambda *refs: march(nz, ny, *refs),
        shape((8, 16, X), f32),
        [
            pltpu.VMEM(plane, f32),
            pltpu.VMEM(plane, f32),
            pltpu.VMEM((3,) + plane, f32),
            pltpu.VMEM((3,) + plane, f32),
            pltpu.VMEM((3,) + plane, f32),
            pltpu.VMEM((3,) + plane, f32),
            pltpu.VMEM((3,) + plane, f32),
            pltpu.VMEM((3,) + plane, f32),
            pltpu.VMEM(plane, f32),
            pltpu.VMEM((2,) + plane, f32),
        ],
    )(at, own, fa, ha, hb, hc, g0)

    d_features, grad = call(
        backward,
        [shape((C, BZ, BY, X)), shape((2, C, 512), f32)],
        [pltpu.VMEM((8, 12, 3, C, X), bf16), pltpu.VMEM((6, 10, 3, C, X), bf16)],
    )(at, dpre, slope2, s2y, ha, hb, sw, hx, fx, slope1, top, w1b, w2b)

    a, b = total_of(grad, iz)
    out = call(finish, shape((2, C, 512), f32))(None, a, b)
    first, second = (
        out[i, :, :TAPS].reshape(C, 3, 3, 3, C).transpose(0, 4, 1, 2, 3) for i in range(2)
    )
    return d_features, first, second, out[0, :, TAPS]


def solution(mesh):
    in_specs = (P(None, "gz", "gy", None), P("gz", "gy", None), P("gz", "gy", None), P(), P(), P())
    out_specs = (P(None, "gz", "gy", None), P(), P(), P())
    return jax.shard_map(
        on_device, mesh=mesh, in_specs=in_specs, out_specs=out_specs, check_vma=False
    )
```

```python
import jax
import jax.numpy as jnp
from jax import lax
from jax.experimental import pallas as pl
from jax.experimental.pallas import tpu as pltpu
from jax.sharding import PartitionSpec as P

C = 16
BZ = 4
BY = 8
X = 128
TAPS = 27 * C
A = 0.25
FLOOR = 0.1
SENT = jnp.bfloat16
f32 = jnp.float32
bf16 = jnp.bfloat16


def sides(v):
    axis = v.ndim - 1
    lane = lax.broadcasted_iota(jnp.int32, v.shape, axis)
    low = jnp.where(lane == 0, 0.0, pltpu.roll(v, 1, axis))
    up = jnp.where(lane == X - 1, 0.0, pltpu.roll(v, X - 1, axis))
    return low, up


def put_taps(ref, index, v):
    low, up = sides(v)
    ref[index, :, 0] = low.astype(bf16)
    ref[index, :, 1] = v.astype(bf16)
    ref[index, :, 2] = up.astype(bf16)


def two_rows(weight, taps_ref, z, y):
    patch = taps_ref[pl.ds(z, 3), y : y + 4].reshape(4 * 9 * C, X)
    out = jnp.dot(weight, patch, preferred_element_type=f32)
    return out[:C], out[C:]


def inside(start, shape, limit):
    row = start + lax.broadcasted_iota(jnp.int32, shape, 0)
    return (row >= 0) & (row < limit)


def build(c1_ref, c2_ref, w1_ref, w2_ref, w1b_ref, w2b_ref):
    zero = jnp.zeros((C, C), f32)
    for src, fwd, adj in ((c1_ref, w1_ref, w1b_ref), (c2_ref, w2_ref, w2b_ref)):
        for j in range(2):
            one, two = [], []
            for a in range(3):
                for b in range(4):
                    for c in range(3):
                        tap = (a * 3 + b - j) * 3 + c
                        ok = 0 <= b - j < 3
                        one.append(src[tap].astype(f32) if ok else zero)
                        two.append(src[26 - tap].astype(f32).T if ok else zero)
            fwd[C * j : C * j + C] = jnp.concatenate(one, axis=1).astype(bf16)
            adj[C * j : C * j + C] = jnp.concatenate(two, axis=1).astype(bf16)


def prepare(at, f_ref, s_ref, ft_ref, me_ref, mo_ref):
    py = at[3]
    row = lax.broadcasted_iota(jnp.int32, (BY, X), 0)
    for z in range(BZ):
        ft_ref[z] = jnp.transpose(f_ref[:, z].astype(f32), (1, 0, 2)).astype(bf16)
    for ref, start, high in ((me_ref, 6 - 6 * py, py == 0), (mo_ref, 6 * py, py == 1)):
        for z in range(BZ):
            ref[2 * z : 2 * z + 2] = ft_ref[z, pl.ds(start, 2)]
        parts = []
        for z in range(BZ):
            own = s_ref[z].astype(f32)
            parts.append(jnp.where(high, pltpu.roll(own, 4, 0), own))
        halves = [jnp.where(row < 4, parts[i], pltpu.roll(parts[i + 1], 4, 0)) for i in (0, 2)]
        ref[2 * BZ] = jnp.concatenate(halves, axis=0).astype(bf16)


def extend(at, ft_ref, s_ref, re_ref, ro_ref, fy_ref, sy_ref, ma_ref, mb_ref):
    pz, py = at[2], at[3]
    row = lax.broadcasted_iota(jnp.int32, (BY, X), 0)
    te = re_ref[2 * BZ].astype(f32)
    to = ro_ref[2 * BZ].astype(f32)
    before = jnp.where(py == 0, to, te)
    after = jnp.where(py == 0, te, to)
    for z in range(BZ):
        fy_ref[z, 2 : 2 + BY] = ft_ref[z]
        fy_ref[z, pl.ds(10 - 10 * py, 2)] = re_ref[2 * z : 2 * z + 2]
        fy_ref[z, pl.ds(10 * py, 2)] = ro_ref[2 * z : 2 * z + 2]
        half, low = (z // 2) * 8, (z % 2) * 4
        own = pltpu.roll(s_ref[z].astype(f32), 4, 0)
        b = before[half : half + 8]
        a = after[half : half + 8]
        b = pltpu.roll(b, 4, 0) if low else b
        a = a if low else pltpu.roll(a, 4, 0)
        sy_ref[z] = jnp.concatenate([jnp.where(row < 4, b, own), jnp.where(row < 4, own, a)], axis=0)
    for ref, start, sign in ((ma_ref, 2 - 2 * pz, 1 - pz), (mb_ref, 2 * pz, pz)):
        for k in range(2):
            ref[12 * k : 12 * k + 12] = fy_ref[start + k]
        for k in range(3):
            ref[24 + k] = sy_ref[sign + k].astype(bf16)


def forward(nz, ny, at, fy_ref, sy_ref, ma_ref, mb_ref, lab_ref, w1_ref, w2_ref, sw_ref,
            fx_ref, hx_ref, slope1_ref, slope2_ref, top_ref, me_ref, mo_ref, own_ref, g0_ref, p_ref):
    iz, iy, pz, py = at[0], at[1], at[2], at[3]
    for k in range(BZ):
        put_taps(fx_ref, 2 + k, fy_ref[k].astype(f32))
    for k in range(2):
        put_taps(fx_ref, 6 - 6 * pz + k, ma_ref[12 * k : 12 * k + 12].astype(f32))
        put_taps(fx_ref, 6 * pz + k, mb_ref[12 * k : 12 * k + 12].astype(f32))
    w1 = w1_ref[...]
    w2 = w2_ref[...]

    def first(z, carry):
        zg = iz * BZ - 1 + z
        zin = (zg >= 0) & (zg < nz)
        for y in range(0, BY + 2, 2):
            acts = two_rows(w1, fx_ref, z, y)
            hid = []
            for j, act in enumerate(acts):
                yg = iy * BY - 1 + y + j
                keep = jnp.where(zin & (yg >= 0) & (yg < ny), 1.0, 0.0)
                sig = jax.nn.sigmoid(act)
                slope1_ref[z, y + j] = sig * (1.0 + act * (1.0 - sig)) * keep
                hid.append((act * sig * keep)[None])
            hid = jnp.concatenate(hid, axis=0)
            low, up = sides(hid)
            hx_ref[z, y : y + 2, 0] = low.astype(bf16)
            hx_ref[z, y : y + 2, 1] = hid.astype(bf16)
            hx_ref[z, y : y + 2, 2] = up.astype(bf16)
        return carry

    lax.fori_loop(0, BZ + 2, first, 0)
    sw = sw_ref[...]

    def second(z, carry):
        rows = []
        for y in range(0, BY, 2):
            for j, act in enumerate(two_rows(w2, hx_ref, z, y)):
                sig = jax.nn.sigmoid(act)
                top = act * sig
                top_ref[z, y + j] = top
                slope2_ref[z, y + j] = sig * (1.0 + act * (1.0 - sig))
                rows.append(jnp.sum(top * sw, axis=0, keepdims=True))
        own_ref[0, z] = jnp.tanh(jnp.concatenate(rows, axis=0))
        return carry

    lax.fori_loop(0, BZ, second, 0)

    for k in range(BZ):
        p_ref[3 + k] = sy_ref[k]
    for k in range(3):
        p_ref[7 - 7 * pz + k] = ma_ref[24 + k].astype(f32)
        p_ref[7 * pz + k] = mb_ref[24 + k].astype(f32)
    rows_in = inside(iy * BY - 4, (16, X), ny)
    for k in range(10):
        zg = iz * BZ - 3 + k
        p_ref[k] = jnp.where(rows_in & (zg >= 0) & (zg < nz), 2.0 * p_ref[k] - 1.0, 0.0)
    for k in range(8):
        centre, uz, lz = p_ref[k + 1], p_ref[k + 2], p_ref[k]
        ly, uy = pltpu.roll(centre, 1, 0), pltpu.roll(centre, 15, 0)
        lx, ux = sides(centre)
        dz, dy, dx = (uz - lz) * 0.5, (uy - ly) * 0.5, (ux - lx) * 0.5
        g = jnp.sqrt(dz * dz + dy * dy + dx * dx + FLOOR)
        g0_ref[k] = g
        if 2 <= k < 6:
            lap = uz + lz + uy + ly + ux + lx - 6.0 * centre
            base = pltpu.roll(centre + (A * 0.5) * lap, 12, 0)[:8]
            own_ref[1, k - 2] = base + A * own_ref[0, k - 2] * pltpu.roll(g, 12, 0)[:8]
    for z in range(BZ):
        own_ref[2, z] = lab_ref[z].astype(f32)
    for ref, start in ((me_ref, 6 - 6 * py), (mo_ref, 6 * py)):
        ref[:12] = own_ref[...].reshape(12, BY, X).astype(SENT)
        for z in range(BZ):
            ref[12 + 4 * z : 16 + 4 * z] = slope2_ref[z, pl.ds(start, 2)].reshape(4, 8, X).astype(SENT)


def widen(at, me_ref, slope2_ref, re_ref, ro_ref, ma_ref, mb_ref, s2y_ref):
    pz, py = at[2], at[3]
    ma_ref[12:24] = me_ref[:12]
    ma_ref[pl.ds(24 - 24 * py, 12)] = re_ref[:12]
    ma_ref[pl.ds(24 * py, 12)] = ro_ref[:12]
    for z in range(BZ):
        s2y_ref[z, 2 : 2 + BY] = slope2_ref[z].astype(bf16)
        for ref, start in ((re_ref, 10 - 10 * py), (ro_ref, 10 * py)):
            rows = ref[12 + 4 * z : 16 + 4 * z].astype(f32).reshape(2, C, X)
            s2y_ref[z, pl.ds(start, 2)] = rows.astype(bf16)
    for k in range(2):
        rows = s2y_ref[2 - 2 * pz + k].astype(f32).reshape(24, 8, X)
        ma_ref[36 + 24 * k : 60 + 24 * k] = rows.astype(SENT)
        rows = s2y_ref[2 * pz + k].astype(f32).reshape(24, 8, X)
        mb_ref[24 * k : 24 + 24 * k] = rows.astype(SENT)


def relay(ma_ref, ra_ref, mb_ref):
    mb_ref[:36] = ma_ref[:36]
    mb_ref[36:] = ra_ref[:36]


def march(nz, ny, at, own_ref, ye_ref, mate_ref, far_ref, far2_ref, g0_ref, dpre_ref,
          sp, lab, ph, w_s, dz_s, dy_s, dx_s, ag_s, ds, dd):
    iz, iy, pz, py = at[0], at[1], at[2], at[3]
    base = 4 * pz

    def place(start, block):
        for k in range(BZ):
            for ref, f in ((sp, 0), (ph, 1), (lab, 2)):
                plane = jnp.concatenate([block(i, f, k).astype(f32) for i in range(3)], axis=0)
                if f == 1:
                    ph[0, start + k] = plane
                else:
                    ref[start + k] = plane

    def piece(ref, first):
        return lambda i, f, k: ref[first + 12 * i + 4 * f + k]

    def mine(i, f, k):
        return own_ref[f, k] if i == 1 else ye_ref[12 * i + 4 * f + k]

    place(8 + 4 * pz, mine)
    place(12 - 4 * pz, piece(mate_ref, 0))
    place(16 * pz + 4 - 4 * pz, piece(far_ref, 0))
    place(16 * pz + 4 * pz, piece(far_ref, 36))
    place(16 - 16 * pz + 4 * pz, piece(far2_ref, 0))
    place(16 - 16 * pz + 4 - 4 * pz, piece(far2_ref, 36))

    dd[0, 0] = jnp.zeros((24, X), f32)
    rows_in = inside(iy * BY - 8, (24, X), ny)
    first_plane = (iz - pz) * BZ - 8

    def within(z):
        zg = first_plane + z
        return rows_in & (zg >= 0) & (zg < nz)

    for t in (1, 2, 3):

        def step(i, carry, t=t):
            z = base + i
            centre, uz, lz = ph[t - 1, z], ph[t - 1, z + 1], ph[t - 1, z - 1]
            ly, uy = pltpu.roll(centre, 1, 0), pltpu.roll(centre, 23, 0)
            lx, ux = sides(centre)
            dz, dy, dx = (uz - lz) * 0.5, (uy - ly) * 0.5, (ux - lx) * 0.5
            g = jnp.sqrt(dz * dz + dy * dy + dx * dx + FLOOR)
            lap = uz + lz + uy + ly + ux + lx - 6.0 * centre
            speed = sp[z]
            ag = A * g
            new = jnp.where(within(z), centre + speed * ag + (A * 0.5) * lap, 0.0)
            w_s[t - 1, z] = (A * 0.5) * speed / g
            dz_s[t - 1, z] = dz
            dy_s[t - 1, z] = dy
            dx_s[t - 1, z] = dx
            ag_s[t - 1, z] = ag
            if t < 3:
                ph[t, z] = new
            else:
                dd[0, z] = jnp.where(within(z), jax.nn.sigmoid(new) - lab[z], 0.0)
            return carry

        lax.fori_loop(t, 20 - t, step, 0, unroll=2)

    for n, t in enumerate((3, 2, 1)):
        src, dst = n % 2, (n + 1) % 2

        def back(i, carry, t=t, n=n, src=src, dst=dst):
            l1, a1, a2 = carry
            z = base + i
            d = dd[src, z]
            add = ag_s[t - 1, z] * d
            ds[z] = add if n == 0 else ds[z] + add
            w = w_s[t - 1, z] * d
            e = (A * 0.5) * d
            qz, qy, qx = w * dz_s[t - 1, z], w * dy_s[t - 1, z], w * dx_s[t - 1, z]
            local = (1.0 - 3.0 * A) * d
            local = local + pltpu.roll(e + qy, 1, 0) + pltpu.roll(e - qy, 23, 0)
            local = local + sides(e + qx)[0] + sides(e - qx)[1]
            dd[dst, z - 1] = jnp.where(within(z - 1), l1 + a2 + (e - qz), 0.0)
            return local, e + qz, a1

        zero = dd[0, 0]
        lax.fori_loop(3 + n, 17 - n, back, (zero, zero, zero), unroll=2)

    for k in range(8):
        z = base + 6 + k
        speed = sp[z]
        left = 1.0 - speed * speed
        one = pltpu.roll(ds[z] * left, 20, 0)[:16]
        two = pltpu.roll(dd[1, z] * left, 20, 0)[:16]
        dpre_ref[k] = one + A * two * g0_ref[k]


def backward(at, dpre_ref, slope2_ref, s2y_ref, ra_ref, rb_ref, sw_ref, hx_ref, fx_ref, slope1_ref,
             top_ref, w1_ref, w2_ref, df_ref, grad_ref, dx_ref, ex_ref):
    pz = at[2]
    sw = sw_ref[...]

    def second(z, k, slope):
        for y in range(BY + 4):
            d = dpre_ref[z, 2 + y : 3 + y, :]
            value = (sw * d * slope(y))[None]
            low, up = sides(value)
            dx_ref[z, y : y + 1, 0] = low.astype(bf16)
            dx_ref[z, y : y + 1, 1] = value.astype(bf16)
            dx_ref[z, y : y + 1, 2] = up.astype(bf16)

    for k in range(BZ):
        def own(y, k=k):
            if 2 <= y < 2 + BY:
                return slope2_ref[k, y - 2]
            return s2y_ref[k, y].astype(f32)
        second(2 + k, k, own)
    for k in range(2):
        for ref, first, z in ((ra_ref, 36, 6 - 6 * pz), (rb_ref, 0, 6 * pz)):
            def far(y, ref=ref, first=first + 24 * k):
                return ref[first + 2 * y : first + 2 * y + 2].astype(f32).reshape(C, X)
            second(z + k, k, far)

    w2 = w2_ref[...]
    w1 = w1_ref[...]

    def hidden(z, carry):
        for y in range(0, BY + 2, 2):
            both = two_rows(w2, dx_ref, z, y)
            d = jnp.concatenate([(v * slope1_ref[z, y + j])[None] for j, v in enumerate(both)], axis=0)
            low, up = sides(d)
            ex_ref[z, y : y + 2, 0] = low.astype(bf16)
            ex_ref[z, y : y + 2, 1] = d.astype(bf16)
            ex_ref[z, y : y + 2, 2] = up.astype(bf16)
        return carry

    lax.fori_loop(0, BZ + 2, hidden, 0)

    def features(z, carry):
        rows = []
        for y in range(0, BY, 2):
            a, b = two_rows(w1, ex_ref, z, y)
            rows += [a[None], b[None]]
        plane = jnp.concatenate(rows, axis=0)
        df_ref[:, z] = jnp.transpose(plane, (1, 0, 2)).astype(bf16)
        return carry

    lax.fori_loop(0, BZ, features, 0)

    nt = (((1,), (1,)), ((), ()))

    def weights(z, carry):
        g1, g2, gs = carry
        d2 = jnp.concatenate([dx_ref[z + 2, y + 2, 1] for y in range(BY)], axis=1)
        d1 = jnp.concatenate([ex_ref[z + 1, y + 1, 1] for y in range(BY)], axis=1)
        p2 = [hx_ref[pl.ds(z, 3), y : y + 3].reshape(TAPS, X) for y in range(BY)]
        p1 = [fx_ref[pl.ds(z + 1, 3), y + 1 : y + 4].reshape(TAPS, X) for y in range(BY)]
        g2 = g2 + lax.dot_general(d2, jnp.concatenate(p2, axis=1), nt, preferred_element_type=f32)
        g1 = g1 + lax.dot_general(d1, jnp.concatenate(p1, axis=1), nt, preferred_element_type=f32)
        for y in range(BY):
            gs = gs + dpre_ref[z + 2, 4 + y : 5 + y, :] * top_ref[z, y]
        return g1, g2, gs

    zero = jnp.zeros((C, TAPS), f32)
    g1, g2, gs = lax.fori_loop(0, BZ, weights, (zero, zero, jnp.zeros((C, X), f32)))
    grad_ref[...] = jnp.zeros_like(grad_ref)
    grad_ref[0, :, :TAPS] = g1
    grad_ref[1, :, :TAPS] = g2
    grad_ref[0, :1, TAPS : TAPS + C] = jnp.sum(jnp.transpose(gs), axis=0, keepdims=True)


def finish(a_ref, b_ref, first_ref, second_ref, speed_ref):
    a, b = a_ref[...], b_ref[...]
    total = jnp.sum(a * a) + jnp.sum(b * b)
    count = 54.0 * C * C + C
    factor = 1.0 / jnp.maximum(jnp.sqrt(jnp.full((1, 1), total)) / jnp.sqrt(f32(count)), 1.0)
    a, b = a * factor, b * factor
    for t in range(27):
        first_ref[t] = a[:, C * t : C * t + C]
        second_ref[t] = b[:, C * t : C * t + C]
    speed_ref[...] = a[:1, TAPS : TAPS + C]


def call(kernel, outs, scratch=(), flops=0):
    smem = pl.BlockSpec(memory_space=pltpu.SMEM)
    vmem = pl.BlockSpec(memory_space=pltpu.VMEM)

    def run(at, *args):
        args = ((at,) if at is not None else ()) + args
        specs = [smem if (i == 0 and at is not None) else vmem for i in range(len(args))]
        many = isinstance(outs, (list, tuple))
        size = sum(a.size * a.dtype.itemsize for a in args)
        return pl.pallas_call(
            kernel,
            out_shape=outs,
            in_specs=specs,
            out_specs=[vmem] * len(outs) if many else vmem,
            scratch_shapes=list(scratch),
            cost_estimate=pl.CostEstimate(flops=flops, bytes_accessed=size, transcendentals=0),
            compiler_params=pltpu.CompilerParams(vmem_limit_bytes=16 * 1024 * 1024),
        )(*args)

    return run


def shape(dims, dtype=bf16):
    return jax.ShapeDtypeStruct(dims, dtype)


def even(value, axis):
    n = lax.axis_size(axis)
    return lax.ppermute(value, axis, [(i, i ^ 1) for i in range(n)])


def odd(value, axis):
    n = lax.axis_size(axis)
    pairs = [(i, i + 1) for i in range(1, n - 1, 2)]
    return lax.ppermute(value, axis, pairs + [(j, i) for i, j in pairs])


def total_of(grad, iz):
    core = iz % 2
    keep = lax.dynamic_index_in_dim(grad, core, 0, keepdims=False)
    give = lax.dynamic_index_in_dim(grad, 1 - core, 0, keepdims=False)
    part = keep + even(give, "gz")
    for axis, unit in (("gy", 1), ("gy", 4), ("gz", 8), ("gz", 2)):
        n = lax.axis_size(axis)
        size = min(4, n // unit)
        if size > 1:
            firsts = [i for i in range(n) if (i // unit) % size == 0]
            groups = [[i + unit * k for k in range(size)] for i in firsts]
            parts = lax.all_gather(part, axis, axis_index_groups=groups)
            part = jnp.sum(parts, axis=0)
    other = even(part, "gz")
    return jnp.where(core == 0, part, other), jnp.where(core == 0, other, part)


def on_device(features, labels, sign_map, conv_first, conv_second, speed_weight):
    nz, ny = BZ * lax.axis_size("gz"), BY * lax.axis_size("gy")
    iz, iy = lax.axis_index("gz"), lax.axis_index("gy")
    pz, py = iz % 2, iy % 2
    at = jnp.stack([iz, iy, pz, py]).astype(jnp.int32)
    sw = jnp.broadcast_to(speed_weight[:, None], (C, X))
    taps = [w.transpose(2, 3, 4, 0, 1).reshape(27, C, C) for w in (conv_first, conv_second)]
    w1, w2, w1b, w2b = call(build, [shape((2 * C, 36 * C))] * 4)(None, *taps)

    ft, me, mo = call(prepare, [shape((BZ, BY, C, X)), shape((9, C, X)), shape((9, C, X))])(
        at, features, sign_map
    )
    re, ro = even(me, "gy"), odd(mo, "gy")
    fy, sy, ma, mb = call(
        extend,
        [shape((BZ, 12, C, X)), shape((BZ, 16, X), f32), shape((27, C, X)), shape((27, C, X))],
    )(at, ft, sign_map, re, ro)
    ra, rb = even(ma, "gz"), odd(mb, "gz")

    fx, hx, slope1, slope2, top, fe, fo, own, g0 = call(
        lambda *refs: forward(nz, ny, *refs),
        [
            shape((8, 12, 3, C, X)),
            shape((6, 10, 3, C, X)),
            shape((6, 10, C, X), f32),
            shape((BZ, BY, C, X), f32),
            shape((BZ, BY, C, X), f32),
            shape((28, 8, X), SENT),
            shape((28, 8, X), SENT),
            shape((3, BZ, BY, X), f32),
            shape((8, 16, X), f32),
        ],
        [pltpu.VMEM((10, 16, X), f32)],
    )(at, fy, sy, ra, rb, labels, w1, w2, sw)

    ge, go = even(fe, "gy"), odd(fo, "gy")
    fa, fs, s2y = call(
        widen, [shape((84, 8, X), SENT), shape((48, 8, X), SENT), shape((BZ, 12, C, X))]
    )(at, fe, slope2, ge, go)
    ha = even(fa, "gz")
    hb = odd(call(relay, shape((72, 8, X), SENT))(None, fa, ha), "gz")
    hb, fs = lax.optimization_barrier((hb, fs))
    hc = even(hb, "gz")
    hs = odd(fs, "gz")

    plane = (24, 24, X)
    dpre = call(
        lambda *refs: march(nz, ny, *refs),
        shape((8, 16, X), f32),
        [
            pltpu.VMEM(plane, f32),
            pltpu.VMEM(plane, f32),
            pltpu.VMEM((3,) + plane, f32),
            pltpu.VMEM((3,) + plane, f32),
            pltpu.VMEM((3,) + plane, f32),
            pltpu.VMEM((3,) + plane, f32),
            pltpu.VMEM((3,) + plane, f32),
            pltpu.VMEM((3,) + plane, f32),
            pltpu.VMEM(plane, f32),
            pltpu.VMEM((2,) + plane, f32),
        ],
    )(at, own, fa, ha, hb, hc, g0)

    d_features, grad = call(
        backward,
        [shape((C, BZ, BY, X)), shape((2, C, 512), f32)],
        [pltpu.VMEM((8, 12, 3, C, X), bf16), pltpu.VMEM((6, 10, 3, C, X), bf16)],
    )(at, dpre, slope2, s2y, ha, hs, sw, hx, fx, slope1, top, w1b, w2b)

    a, b = total_of(grad, iz)
    tap_major = shape((27, C, C), f32)
    first, second, speed = call(finish, [tap_major, tap_major, shape((1, C), f32)])(None, a, b)
    first, second = (
        g.reshape(3, 3, 3, C, C).transpose(3, 4, 0, 1, 2) for g in (first, second)
    )
    return d_features, first, second, speed.reshape(C)


def solution(mesh):
    in_specs = (P(None, "gz", "gy", None), P("gz", "gy", None), P("gz", "gy", None), P(), P(), P())
    out_specs = (P(None, "gz", "gy", None), P(), P(), P())
    return jax.shard_map(
        on_device, mesh=mesh, in_specs=in_specs, out_specs=out_specs, check_vma=False
    )
```

```python
import jax
import jax.numpy as jnp
from jax import lax
from jax.experimental import pallas as pl
from jax.experimental.pallas import tpu as pltpu
from jax.sharding import PartitionSpec as P

C = 16
BZ = 4
BY = 8
X = 128
TAPS = 27 * C
A = 0.25
FLOOR = 0.1
SENT = jnp.bfloat16
f32 = jnp.float32
bf16 = jnp.bfloat16


def sides(v):
    axis = v.ndim - 1
    lane = lax.broadcasted_iota(jnp.int32, v.shape, axis)
    low = jnp.where(lane == 0, 0.0, pltpu.roll(v, 1, axis))
    up = jnp.where(lane == X - 1, 0.0, pltpu.roll(v, X - 1, axis))
    return low, up


def put_taps(ref, index, v):
    low, up = sides(v)
    ref[index, :, 0] = low.astype(bf16)
    ref[index, :, 1] = v.astype(bf16)
    ref[index, :, 2] = up.astype(bf16)


def two_rows(weight, taps_ref, z, y):
    patch = taps_ref[pl.ds(z, 3), y : y + 4].reshape(4 * 9 * C, X)
    out = jnp.dot(weight, patch, preferred_element_type=f32)
    return out[:C], out[C:]


def inside(start, shape, limit):
    row = start + lax.broadcasted_iota(jnp.int32, shape, 0)
    return (row >= 0) & (row < limit)


def build(c1_ref, c2_ref, sp_ref, lab_ref, w1_ref, w2_ref, w1b_ref, w2b_ref, sw_ref, labf_ref):
    sw_ref[...] = jnp.transpose(jnp.broadcast_to(sp_ref[...], (X, C)))
    labf_ref[...] = lab_ref[...].astype(f32)
    zero = jnp.zeros((C, C), f32)
    for src, fwd, adj in ((c1_ref, w1_ref, w1b_ref), (c2_ref, w2_ref, w2b_ref)):
        for j in range(2):
            one, two = [], []
            for a in range(3):
                for b in range(4):
                    for c in range(3):
                        tap = (a * 3 + b - j) * 3 + c
                        ok = 0 <= b - j < 3
                        one.append(src[tap].astype(f32) if ok else zero)
                        two.append(src[26 - tap].astype(f32).T if ok else zero)
            fwd[C * j : C * j + C] = jnp.concatenate(one, axis=1).astype(bf16)
            adj[C * j : C * j + C] = jnp.concatenate(two, axis=1).astype(bf16)


def prepare(at, f_ref, s_ref, ft_ref, me_ref, mo_ref):
    py = at[3]
    row = lax.broadcasted_iota(jnp.int32, (BY, X), 0)
    for z in range(BZ):
        ft_ref[z] = jnp.transpose(f_ref[:, z].astype(f32), (1, 0, 2)).astype(bf16)
    for ref, start, high in ((me_ref, 6 - 6 * py, py == 0), (mo_ref, 6 * py, py == 1)):
        for z in range(BZ):
            ref[2 * z : 2 * z + 2] = ft_ref[z, pl.ds(start, 2)]
        parts = []
        for z in range(BZ):
            own = s_ref[z].astype(f32)
            parts.append(jnp.where(high, pltpu.roll(own, 4, 0), own))
        halves = [jnp.where(row < 4, parts[i], pltpu.roll(parts[i + 1], 4, 0)) for i in (0, 2)]
        ref[2 * BZ] = jnp.concatenate(halves, axis=0).astype(bf16)


def extend(at, ft_ref, s_ref, re_ref, ro_ref, fy_ref, sy_ref, ma_ref, mb_ref):
    pz, py = at[2], at[3]
    row = lax.broadcasted_iota(jnp.int32, (BY, X), 0)
    te = re_ref[2 * BZ].astype(f32)
    to = ro_ref[2 * BZ].astype(f32)
    before = jnp.where(py == 0, to, te)
    after = jnp.where(py == 0, te, to)
    for z in range(BZ):
        fy_ref[z, 2 : 2 + BY] = ft_ref[z]
        fy_ref[z, pl.ds(10 - 10 * py, 2)] = re_ref[2 * z : 2 * z + 2]
        fy_ref[z, pl.ds(10 * py, 2)] = ro_ref[2 * z : 2 * z + 2]
        half, low = (z // 2) * 8, (z % 2) * 4
        own = pltpu.roll(s_ref[z].astype(f32), 4, 0)
        b = before[half : half + 8]
        a = after[half : half + 8]
        b = pltpu.roll(b, 4, 0) if low else b
        a = a if low else pltpu.roll(a, 4, 0)
        sy_ref[z] = jnp.concatenate([jnp.where(row < 4, b, own), jnp.where(row < 4, own, a)], axis=0)
    for ref, start, sign in ((ma_ref, 2 - 2 * pz, 1 - pz), (mb_ref, 2 * pz, pz)):
        for k in range(2):
            ref[12 * k : 12 * k + 12] = fy_ref[start + k]
        for k in range(3):
            ref[24 + k] = sy_ref[sign + k].astype(bf16)


def forward(nz, ny, at, fy_ref, sy_ref, ma_ref, mb_ref, lab_ref, w1_ref, w2_ref, sw_ref,
            fc_ref, hx_ref, slope1_ref, slope2_ref, top_ref, me_ref, mo_ref, own_ref, g0_ref, p_ref, fx_ref):
    iz, iy, pz, py = at[0], at[1], at[2], at[3]
    for k in range(BZ):
        put_taps(fx_ref, 2 + k, fy_ref[k].astype(f32))
    for k in range(2):
        put_taps(fx_ref, 6 - 6 * pz + k, ma_ref[12 * k : 12 * k + 12].astype(f32))
        put_taps(fx_ref, 6 * pz + k, mb_ref[12 * k : 12 * k + 12].astype(f32))
    fc_ref[...] = fx_ref[1:7, 1:11]
    w1 = w1_ref[...]
    w2 = w2_ref[...]

    def first(z, carry):
        zg = iz * BZ - 1 + z
        zin = (zg >= 0) & (zg < nz)
        for y in range(0, BY + 2, 2):
            acts = two_rows(w1, fx_ref, z, y)
            hid = []
            for j, act in enumerate(acts):
                yg = iy * BY - 1 + y + j
                keep = jnp.where(zin & (yg >= 0) & (yg < ny), 1.0, 0.0)
                sig = jax.nn.sigmoid(act)
                slope1_ref[z, y + j] = sig * (1.0 + act * (1.0 - sig)) * keep
                hid.append((act * sig * keep)[None])
            hid = jnp.concatenate(hid, axis=0)
            low, up = sides(hid)
            hx_ref[z, y : y + 2, 0] = low.astype(bf16)
            hx_ref[z, y : y + 2, 1] = hid.astype(bf16)
            hx_ref[z, y : y + 2, 2] = up.astype(bf16)
        return carry

    lax.fori_loop(0, BZ + 2, first, 0)
    sw = sw_ref[...]

    def second(z, carry):
        rows = []
        for y in range(0, BY, 2):
            for j, act in enumerate(two_rows(w2, hx_ref, z, y)):
                sig = jax.nn.sigmoid(act)
                top = act * sig
                top_ref[z, y + j] = top
                slope2_ref[z, y + j] = sig * (1.0 + act * (1.0 - sig))
                rows.append(jnp.sum(top * sw, axis=0, keepdims=True))
        own_ref[0, z] = jnp.tanh(jnp.concatenate(rows, axis=0))
        return carry

    lax.fori_loop(0, BZ, second, 0)

    for k in range(BZ):
        p_ref[3 + k] = sy_ref[k]
    for k in range(3):
        p_ref[7 - 7 * pz + k] = ma_ref[24 + k].astype(f32)
        p_ref[7 * pz + k] = mb_ref[24 + k].astype(f32)
    rows_in = inside(iy * BY - 4, (16, X), ny)
    for k in range(10):
        zg = iz * BZ - 3 + k
        p_ref[k] = jnp.where(rows_in & (zg >= 0) & (zg < nz), 2.0 * p_ref[k] - 1.0, 0.0)
    for k in range(8):
        centre, uz, lz = p_ref[k + 1], p_ref[k + 2], p_ref[k]
        ly, uy = pltpu.roll(centre, 1, 0), pltpu.roll(centre, 15, 0)
        lx, ux = sides(centre)
        dz, dy, dx = (uz - lz) * 0.5, (uy - ly) * 0.5, (ux - lx) * 0.5
        g = jnp.sqrt(dz * dz + dy * dy + dx * dx + FLOOR)
        g0_ref[k] = g
        if 2 <= k < 6:
            lap = uz + lz + uy + ly + ux + lx - 6.0 * centre
            base = pltpu.roll(centre + (A * 0.5) * lap, 12, 0)[:8]
            own_ref[1, k - 2] = base + A * own_ref[0, k - 2] * pltpu.roll(g, 12, 0)[:8]
    for z in range(BZ):
        own_ref[2, z] = lab_ref[z]
    for ref, start in ((me_ref, 6 - 6 * py), (mo_ref, 6 * py)):
        ref[:12] = own_ref[...].reshape(12, BY, X).astype(SENT)
        for z in range(BZ):
            ref[12 + 4 * z : 16 + 4 * z] = slope2_ref[z, pl.ds(start, 2)].reshape(4, 8, X).astype(SENT)


def widen(at, me_ref, slope2_ref, re_ref, ro_ref, ma_ref, mb_ref, s2y_ref):
    pz, py = at[2], at[3]
    ma_ref[12:24] = me_ref[:12]
    ma_ref[pl.ds(24 - 24 * py, 12)] = re_ref[:12]
    ma_ref[pl.ds(24 * py, 12)] = ro_ref[:12]
    for z in range(BZ):
        s2y_ref[z, 2 : 2 + BY] = slope2_ref[z].astype(bf16)
        for ref, start in ((re_ref, 10 - 10 * py), (ro_ref, 10 * py)):
            rows = ref[12 + 4 * z : 16 + 4 * z].astype(f32).reshape(2, C, X)
            s2y_ref[z, pl.ds(start, 2)] = rows.astype(bf16)
    for k in range(2):
        rows = s2y_ref[2 - 2 * pz + k].astype(f32).reshape(24, 8, X)
        ma_ref[36 + 24 * k : 60 + 24 * k] = rows.astype(SENT)
        rows = s2y_ref[2 * pz + k].astype(f32).reshape(24, 8, X)
        mb_ref[24 * k : 24 + 24 * k] = rows.astype(SENT)


def relay(ma_ref, ra_ref, mb_ref):
    mb_ref[:36] = ma_ref[:36]
    mb_ref[36:] = ra_ref[:36]


def march(nz, ny, at, own_ref, ye_ref, mate_ref, far_ref, far2_ref, g0_ref, dpre_ref,
          sp, lab, ph, w_s, dz_s, dy_s, dx_s, ag_s, ds, dd):
    iz, iy, pz, py = at[0], at[1], at[2], at[3]
    base = 4 * pz

    def place(start, block):
        for k in range(BZ):
            for ref, f in ((sp, 0), (ph, 1), (lab, 2)):
                plane = jnp.concatenate([block(i, f, k).astype(f32) for i in range(3)], axis=0)
                if f == 1:
                    ph[0, start + k] = plane
                else:
                    ref[start + k] = plane

    def piece(ref, first):
        return lambda i, f, k: ref[first + 12 * i + 4 * f + k]

    def mine(i, f, k):
        return own_ref[f, k] if i == 1 else ye_ref[12 * i + 4 * f + k]

    place(8 + 4 * pz, mine)
    place(12 - 4 * pz, piece(mate_ref, 0))
    place(16 * pz + 4 - 4 * pz, piece(far_ref, 0))
    place(16 * pz + 4 * pz, piece(far_ref, 36))
    place(16 - 16 * pz + 4 * pz, piece(far2_ref, 0))
    place(16 - 16 * pz + 4 - 4 * pz, piece(far2_ref, 36))

    dd[0, 0] = jnp.zeros((24, X), f32)
    rows_in = inside(iy * BY - 8, (24, X), ny)
    first_plane = (iz - pz) * BZ - 8

    def within(z):
        zg = first_plane + z
        return rows_in & (zg >= 0) & (zg < nz)

    for t in (1, 2, 3):

        def step(i, carry, t=t):
            z = base + i
            centre, uz, lz = ph[t - 1, z], ph[t - 1, z + 1], ph[t - 1, z - 1]
            ly, uy = pltpu.roll(centre, 1, 0), pltpu.roll(centre, 23, 0)
            lx, ux = sides(centre)
            dz, dy, dx = (uz - lz) * 0.5, (uy - ly) * 0.5, (ux - lx) * 0.5
            g = jnp.sqrt(dz * dz + dy * dy + dx * dx + FLOOR)
            lap = uz + lz + uy + ly + ux + lx - 6.0 * centre
            speed = sp[z]
            ag = A * g
            new = jnp.where(within(z), centre + speed * ag + (A * 0.5) * lap, 0.0)
            w_s[t - 1, z] = (A * 0.5) * speed / g
            dz_s[t - 1, z] = dz
            dy_s[t - 1, z] = dy
            dx_s[t - 1, z] = dx
            ag_s[t - 1, z] = ag
            if t < 3:
                ph[t, z] = new
            else:
                dd[0, z] = jnp.where(within(z), jax.nn.sigmoid(new) - lab[z], 0.0)
            return carry

        lax.fori_loop(t, 20 - t, step, 0, unroll=2)

    for n, t in enumerate((3, 2, 1)):
        src, dst = n % 2, (n + 1) % 2

        def back(i, carry, t=t, n=n, src=src, dst=dst):
            l1, a1, a2 = carry
            z = base + i
            d = dd[src, z]
            add = ag_s[t - 1, z] * d
            ds[z] = add if n == 0 else ds[z] + add
            w = w_s[t - 1, z] * d
            e = (A * 0.5) * d
            qz, qy, qx = w * dz_s[t - 1, z], w * dy_s[t - 1, z], w * dx_s[t - 1, z]
            local = (1.0 - 3.0 * A) * d
            local = local + pltpu.roll(e + qy, 1, 0) + pltpu.roll(e - qy, 23, 0)
            local = local + sides(e + qx)[0] + sides(e - qx)[1]
            dd[dst, z - 1] = jnp.where(within(z - 1), l1 + a2 + (e - qz), 0.0)
            return local, e + qz, a1

        zero = dd[0, 0]
        lax.fori_loop(3 + n, 17 - n, back, (zero, zero, zero), unroll=2)

    for k in range(8):
        z = base + 6 + k
        speed = sp[z]
        left = 1.0 - speed * speed
        one = pltpu.roll(ds[z] * left, 20, 0)[:16]
        two = pltpu.roll(dd[1, z] * left, 20, 0)[:16]
        dpre_ref[k] = one + A * two * g0_ref[k]


def backward(at, dpre_ref, slope2_ref, s2y_ref, ra_ref, rb_ref, sw_ref, hx_ref, fx_ref, slope1_ref,
             top_ref, w1_ref, w2_ref, df_ref, grad_ref, dx_ref, ex_ref):
    pz = at[2]
    sw = sw_ref[...]

    def second(z, k, slope):
        for y in range(BY + 4):
            d = dpre_ref[z, 2 + y : 3 + y, :]
            value = (sw * d * slope(y))[None]
            low, up = sides(value)
            dx_ref[z, y : y + 1, 0] = low.astype(bf16)
            dx_ref[z, y : y + 1, 1] = value.astype(bf16)
            dx_ref[z, y : y + 1, 2] = up.astype(bf16)

    for k in range(BZ):
        def own(y, k=k):
            if 2 <= y < 2 + BY:
                return slope2_ref[k, y - 2]
            return s2y_ref[k, y].astype(f32)
        second(2 + k, k, own)
    for k in range(2):
        for ref, first, z in ((ra_ref, 36, 6 - 6 * pz), (rb_ref, 0, 6 * pz)):
            def far(y, ref=ref, first=first + 24 * k):
                return ref[first + 2 * y : first + 2 * y + 2].astype(f32).reshape(C, X)
            second(z + k, k, far)

    w2 = w2_ref[...]
    w1 = w1_ref[...]

    def hidden(z, carry):
        for y in range(0, BY + 2, 2):
            both = two_rows(w2, dx_ref, z, y)
            d = jnp.concatenate([(v * slope1_ref[z, y + j])[None] for j, v in enumerate(both)], axis=0)
            low, up = sides(d)
            ex_ref[z, y : y + 2, 0] = low.astype(bf16)
            ex_ref[z, y : y + 2, 1] = d.astype(bf16)
            ex_ref[z, y : y + 2, 2] = up.astype(bf16)
        return carry

    lax.fori_loop(0, BZ + 2, hidden, 0)

    def features(z, carry):
        rows = []
        for y in range(0, BY, 2):
            a, b = two_rows(w1, ex_ref, z, y)
            rows += [a[None], b[None]]
        plane = jnp.concatenate(rows, axis=0)
        df_ref[:, z] = jnp.transpose(plane, (1, 0, 2)).astype(bf16)
        return carry

    lax.fori_loop(0, BZ, features, 0)

    nt = (((1,), (1,)), ((), ()))

    def weights(z, carry):
        g1, g2, gs = carry
        d2 = jnp.concatenate([dx_ref[z + 2, y + 2, 1] for y in range(BY)], axis=1)
        d1 = jnp.concatenate([ex_ref[z + 1, y + 1, 1] for y in range(BY)], axis=1)
        p2 = [hx_ref[pl.ds(z, 3), y : y + 3].reshape(TAPS, X) for y in range(BY)]
        p1 = [fx_ref[pl.ds(z, 3), y : y + 3].reshape(TAPS, X) for y in range(BY)]
        g2 = g2 + lax.dot_general(d2, jnp.concatenate(p2, axis=1), nt, preferred_element_type=f32)
        g1 = g1 + lax.dot_general(d1, jnp.concatenate(p1, axis=1), nt, preferred_element_type=f32)
        for y in range(BY):
            gs = gs + dpre_ref[z + 2, 4 + y : 5 + y, :] * top_ref[z, y]
        return g1, g2, gs

    zero = jnp.zeros((C, TAPS), f32)
    g1, g2, gs = lax.fori_loop(0, BZ, weights, (zero, zero, jnp.zeros((C, X), f32)))
    grad_ref[...] = jnp.zeros_like(grad_ref)
    for i, g in enumerate((g1, g2)):
        grad_ref[i, :C] = g[:, :256]
        grad_ref[i, C:, : TAPS - 256] = g[:, 256:]
    grad_ref[0, C : C + 1, TAPS - 256 : TAPS - 240] = jnp.sum(jnp.transpose(gs), axis=0, keepdims=True)


def finish(a_ref, b_ref, first_ref, second_ref, speed_ref):
    a, b = a_ref[...], b_ref[...]
    total = jnp.sum(a * a) + jnp.sum(b * b)
    count = 54.0 * C * C + C
    factor = 1.0 / jnp.maximum(jnp.sqrt(jnp.full((1, 1), total)) / jnp.sqrt(f32(count)), 1.0)
    a, b = a * factor, b * factor
    for t in range(27):
        row, lane = C * (t // 16), C * (t % 16)
        first_ref[t] = a[row : row + C, lane : lane + C]
        second_ref[t] = b[row : row + C, lane : lane + C]
    speed_ref[...] = a[C : C + 1, TAPS - 256 : TAPS - 240]


def call(kernel, outs, scratch=(), flops=0):
    smem = pl.BlockSpec(memory_space=pltpu.SMEM)
    vmem = pl.BlockSpec(memory_space=pltpu.VMEM)

    def run(at, *args):
        args = ((at,) if at is not None else ()) + args
        specs = [smem if (i == 0 and at is not None) else vmem for i in range(len(args))]
        many = isinstance(outs, (list, tuple))
        size = sum(a.size * a.dtype.itemsize for a in args)
        return pl.pallas_call(
            kernel,
            out_shape=outs,
            in_specs=specs,
            out_specs=[vmem] * len(outs) if many else vmem,
            scratch_shapes=list(scratch),
            cost_estimate=pl.CostEstimate(flops=flops, bytes_accessed=size, transcendentals=0),
            compiler_params=pltpu.CompilerParams(vmem_limit_bytes=16 * 1024 * 1024),
        )(*args)

    return run


def shape(dims, dtype=bf16):
    return jax.ShapeDtypeStruct(dims, dtype)


def even(value, axis):
    n = lax.axis_size(axis)
    return lax.ppermute(value, axis, [(i, i ^ 1) for i in range(n)])


def odd(value, axis):
    n = lax.axis_size(axis)
    pairs = [(i, i + 1) for i in range(1, n - 1, 2)]
    return lax.ppermute(value, axis, pairs + [(j, i) for i, j in pairs])


def groups(n, unit):
    size = max(1, min(4, n // unit))
    firsts = [i for i in range(n) if (i // unit) % size == 0]
    return [[i + unit * k for k in range(size)] for i in firsts]


def total_of(grad, iz):
    core = iz % 2
    keep = lax.dynamic_index_in_dim(grad, core, 0, keepdims=False)
    give = lax.dynamic_index_in_dim(grad, 1 - core, 0, keepdims=False)
    part = keep + even(give, "gz")
    row = groups(lax.axis_size("gy"), 1)
    size = len(row[0])
    chunks = part.reshape(size, 2 * C // size, 256)
    part = jnp.sum(lax.all_to_all(chunks, "gy", 0, 0, axis_index_groups=row), axis=0)
    for axis, unit in (("gy", 4), ("gz", 8), ("gz", 2)):
        sets = groups(lax.axis_size(axis), unit)
        if len(sets[0]) > 1:
            part = jnp.sum(lax.all_gather(part, axis, axis_index_groups=sets), axis=0)
    part = lax.all_gather(part, "gy", axis_index_groups=row).reshape(2 * C, 256)
    other = even(part, "gz")
    return jnp.where(core == 0, part, other), jnp.where(core == 0, other, part)


def on_device(features, labels, sign_map, conv_first, conv_second, speed_weight):
    nz, ny = BZ * lax.axis_size("gz"), BY * lax.axis_size("gy")
    iz, iy = lax.axis_index("gz"), lax.axis_index("gy")
    pz, py = iz % 2, iy % 2
    at = jnp.stack([iz, iy, pz, py]).astype(jnp.int32)
    taps = [w.transpose(2, 3, 4, 0, 1).reshape(27, C, C) for w in (conv_first, conv_second)]
    w1, w2, w1b, w2b, sw, target = call(
        build, [shape((2 * C, 36 * C))] * 4 + [shape((C, X), f32), shape((BZ, BY, X), f32)]
    )(None, *taps, speed_weight.reshape(1, C), labels)

    ft, me, mo = call(prepare, [shape((BZ, BY, C, X)), shape((9, C, X)), shape((9, C, X))])(
        at, features, sign_map
    )
    ro = odd(mo, "gy")
    re = even(me, "gy")
    fy, sy, ma, mb = call(
        extend,
        [shape((BZ, 12, C, X)), shape((BZ, 16, X), f32), shape((27, C, X)), shape((27, C, X))],
    )(at, ft, sign_map, re, ro)
    rb = odd(mb, "gz")
    ra = even(ma, "gz")

    fx, hx, slope1, slope2, top, fe, fo, own, g0 = call(
        lambda *refs: forward(nz, ny, *refs),
        [
            shape((6, 10, 3, C, X)),
            shape((6, 10, 3, C, X)),
            shape((6, 10, C, X), f32),
            shape((BZ, BY, C, X), f32),
            shape((BZ, BY, C, X), f32),
            shape((28, 8, X), SENT),
            shape((28, 8, X), SENT),
            shape((3, BZ, BY, X), f32),
            shape((8, 16, X), f32),
        ],
        [pltpu.VMEM((10, 16, X), f32), pltpu.VMEM((8, 12, 3, C, X), bf16)],
    )(at, fy, sy, ra, rb, target, w1, w2, sw)

    go = odd(fo, "gy")
    ge = even(fe, "gy")
    fa, fs, s2y = call(
        widen, [shape((84, 8, X), SENT), shape((48, 8, X), SENT), shape((BZ, 12, C, X))]
    )(at, fe, slope2, ge, go)
    ha = even(fa, "gz")
    hb = odd(call(relay, shape((72, 8, X), SENT))(None, fa, ha), "gz")
    hb, fs = lax.optimization_barrier((hb, fs))
    hc = even(hb, "gz")
    hs = odd(fs, "gz")

    plane = (24, 24, X)
    dpre = call(
        lambda *refs: march(nz, ny, *refs),
        shape((8, 16, X), f32),
        [
            pltpu.VMEM(plane, f32),
            pltpu.VMEM(plane, f32),
            pltpu.VMEM((3,) + plane, f32),
            pltpu.VMEM((3,) + plane, f32),
            pltpu.VMEM((3,) + plane, f32),
            pltpu.VMEM((3,) + plane, f32),
            pltpu.VMEM((3,) + plane, f32),
            pltpu.VMEM((3,) + plane, f32),
            pltpu.VMEM(plane, f32),
            pltpu.VMEM((2,) + plane, f32),
        ],
    )(at, own, fa, ha, hb, hc, g0)

    d_features, grad = call(
        backward,
        [shape((C, BZ, BY, X)), shape((2, 2 * C, 256), f32)],
        [pltpu.VMEM((8, 12, 3, C, X), bf16), pltpu.VMEM((6, 10, 3, C, X), bf16)],
    )(at, dpre, slope2, s2y, ha, hs, sw, hx, fx, slope1, top, w1b, w2b)

    a, b = total_of(grad, iz)
    tap_major = shape((27, C, C), f32)
    first, second, speed = call(finish, [tap_major, tap_major, shape((1, C), f32)])(None, a, b)
    first, second = (
        g.reshape(3, 3, 3, C, C).transpose(3, 4, 0, 1, 2) for g in (first, second)
    )
    return d_features, first, second, speed.reshape(C)


def solution(mesh):
    in_specs = (P(None, "gz", "gy", None), P("gz", "gy", None), P("gz", "gy", None), P(), P(), P())
    out_specs = (P(None, "gz", "gy", None), P(), P(), P())
    return jax.shard_map(
        on_device, mesh=mesh, in_specs=in_specs, out_specs=out_specs, check_vma=False
    )
```

```python
import jax
import jax.numpy as jnp
from jax import lax
from jax.experimental import pallas as pl
from jax.experimental.pallas import tpu as pltpu
from jax.sharding import PartitionSpec as P


C = 16
BZ = 4
BY = 8
X = 128
TAPS = 27 * C
A = 0.25
FLOOR = 0.1
SENT = jnp.bfloat16
f32 = jnp.float32
bf16 = jnp.bfloat16


def sides(v):
    axis = v.ndim - 1
    lane = lax.broadcasted_iota(jnp.int32, v.shape, axis)
    low = jnp.where(lane == 0, 0.0, pltpu.roll(v, 1, axis))
    up = jnp.where(lane == X - 1, 0.0, pltpu.roll(v, X - 1, axis))
    return low, up


def put_taps(ref, index, v):
    low, up = sides(v)
    ref[index, :, 0] = low.astype(bf16)
    ref[index, :, 1] = v.astype(bf16)
    ref[index, :, 2] = up.astype(bf16)


def two_rows(weight, taps_ref, z, y):
    patch = taps_ref[pl.ds(z, 3), y : y + 4].reshape(4 * 9 * C, X)
    out = jnp.dot(weight, patch, preferred_element_type=f32)
    return out[:C], out[C:]


def inside(start, shape, limit):
    row = start + lax.broadcasted_iota(jnp.int32, shape, 0)
    return (row >= 0) & (row < limit)


def build(c1_ref, c2_ref, sp_ref, lab_ref, w1_ref, w2_ref, w1b_ref, w2b_ref, sw_ref, labf_ref):
    sw_ref[...] = jnp.transpose(jnp.broadcast_to(sp_ref[...], (X, C)))
    labf_ref[...] = lab_ref[...].astype(f32)
    zero = jnp.zeros((C, C), f32)
    for src, fwd, adj in ((c1_ref, w1_ref, w1b_ref), (c2_ref, w2_ref, w2b_ref)):
        for j in range(2):
            one, two = [], []
            for a in range(3):
                for b in range(4):
                    for c in range(3):
                        tap = (a * 3 + b - j) * 3 + c
                        ok = 0 <= b - j < 3
                        one.append(src[tap].astype(f32) if ok else zero)
                        two.append(src[26 - tap].astype(f32).T if ok else zero)
            fwd[C * j : C * j + C] = jnp.concatenate(one, axis=1).astype(bf16)
            adj[C * j : C * j + C] = jnp.concatenate(two, axis=1).astype(bf16)


def prepare(at, f_ref, s_ref, ft_ref, me_ref, mo_ref):
    py = at[3]
    row = lax.broadcasted_iota(jnp.int32, (BY, X), 0)
    for z in range(BZ):
        ft_ref[z] = jnp.transpose(f_ref[:, z].astype(f32), (1, 0, 2)).astype(bf16)
    for ref, start, high in ((me_ref, 6 - 6 * py, py == 0), (mo_ref, 6 * py, py == 1)):
        for z in range(BZ):
            ref[2 * z : 2 * z + 2] = ft_ref[z, pl.ds(start, 2)]
        parts = []
        for z in range(BZ):
            own = s_ref[z].astype(f32)
            parts.append(jnp.where(high, pltpu.roll(own, 4, 0), own))
        halves = [jnp.where(row < 4, parts[i], pltpu.roll(parts[i + 1], 4, 0)) for i in (0, 2)]
        ref[2 * BZ] = jnp.concatenate(halves, axis=0).astype(bf16)


def extend(at, ft_ref, s_ref, re_ref, ro_ref, fy_ref, sy_ref, ma_ref, mb_ref):
    pz, py = at[2], at[3]
    row = lax.broadcasted_iota(jnp.int32, (BY, X), 0)
    te = re_ref[2 * BZ].astype(f32)
    to = ro_ref[2 * BZ].astype(f32)
    before = jnp.where(py == 0, to, te)
    after = jnp.where(py == 0, te, to)
    for z in range(BZ):
        fy_ref[z, 2 : 2 + BY] = ft_ref[z]
        fy_ref[z, pl.ds(10 - 10 * py, 2)] = re_ref[2 * z : 2 * z + 2]
        fy_ref[z, pl.ds(10 * py, 2)] = ro_ref[2 * z : 2 * z + 2]
        half, low = (z // 2) * 8, (z % 2) * 4
        own = pltpu.roll(s_ref[z].astype(f32), 4, 0)
        b = before[half : half + 8]
        a = after[half : half + 8]
        b = pltpu.roll(b, 4, 0) if low else b
        a = a if low else pltpu.roll(a, 4, 0)
        sy_ref[z] = jnp.concatenate([jnp.where(row < 4, b, own), jnp.where(row < 4, own, a)], axis=0)
    for ref, start, sign in ((ma_ref, 2 - 2 * pz, 1 - pz), (mb_ref, 2 * pz, pz)):
        for k in range(2):
            ref[12 * k : 12 * k + 12] = fy_ref[start + k]
        for k in range(3):
            ref[24 + k] = sy_ref[sign + k].astype(bf16)


def forward(nz, ny, at, fy_ref, sy_ref, ma_ref, mb_ref, lab_ref, w1_ref, w2_ref, sw_ref,
            fc_ref, hx_ref, slope1_ref, slope2_ref, top_ref, me_ref, mo_ref, own_ref, g0_ref, p_ref, fx_ref):
    iz, iy, pz, py = at[0], at[1], at[2], at[3]
    for k in range(BZ):
        put_taps(fx_ref, 2 + k, fy_ref[k].astype(f32))
    for k in range(2):
        put_taps(fx_ref, 6 - 6 * pz + k, ma_ref[12 * k : 12 * k + 12].astype(f32))
        put_taps(fx_ref, 6 * pz + k, mb_ref[12 * k : 12 * k + 12].astype(f32))
    fc_ref[...] = fx_ref[1:7, 1:11]
    w1 = w1_ref[...]
    w2 = w2_ref[...]

    def first(z, carry):
        zg = iz * BZ - 1 + z
        zin = (zg >= 0) & (zg < nz)
        for y in range(0, BY + 2, 2):
            acts = two_rows(w1, fx_ref, z, y)
            hid = []
            for j, act in enumerate(acts):
                yg = iy * BY - 1 + y + j
                keep = jnp.where(zin & (yg >= 0) & (yg < ny), 1.0, 0.0)
                sig = jax.nn.sigmoid(act)
                slope1_ref[z, y + j] = sig * (1.0 + act * (1.0 - sig)) * keep
                hid.append((act * sig * keep)[None])
            hid = jnp.concatenate(hid, axis=0)
            low, up = sides(hid)
            hx_ref[z, y : y + 2, 0] = low.astype(bf16)
            hx_ref[z, y : y + 2, 1] = hid.astype(bf16)
            hx_ref[z, y : y + 2, 2] = up.astype(bf16)
        return carry

    lax.fori_loop(0, BZ + 2, first, 0)
    sw = sw_ref[...]

    def second(z, carry):
        rows = []
        for y in range(0, BY, 2):
            for j, act in enumerate(two_rows(w2, hx_ref, z, y)):
                sig = jax.nn.sigmoid(act)
                top = act * sig
                top_ref[z, y + j] = top
                slope2_ref[z, y + j] = sig * (1.0 + act * (1.0 - sig))
                rows.append(jnp.sum(top * sw, axis=0, keepdims=True))
        own_ref[0, z] = jnp.tanh(jnp.concatenate(rows, axis=0))
        return carry

    lax.fori_loop(0, BZ, second, 0)

    for k in range(BZ):
        p_ref[3 + k] = sy_ref[k]
    for k in range(3):
        p_ref[7 - 7 * pz + k] = ma_ref[24 + k].astype(f32)
        p_ref[7 * pz + k] = mb_ref[24 + k].astype(f32)
    rows_in = inside(iy * BY - 4, (16, X), ny)
    for k in range(10):
        zg = iz * BZ - 3 + k
        p_ref[k] = jnp.where(rows_in & (zg >= 0) & (zg < nz), 2.0 * p_ref[k] - 1.0, 0.0)
    for k in range(8):
        centre, uz, lz = p_ref[k + 1], p_ref[k + 2], p_ref[k]
        ly, uy = pltpu.roll(centre, 1, 0), pltpu.roll(centre, 15, 0)
        lx, ux = sides(centre)
        dz, dy, dx = (uz - lz) * 0.5, (uy - ly) * 0.5, (ux - lx) * 0.5
        g = jnp.sqrt(dz * dz + dy * dy + dx * dx + FLOOR)
        g0_ref[k] = g
        if 2 <= k < 6:
            lap = uz + lz + uy + ly + ux + lx - 6.0 * centre
            base = pltpu.roll(centre + (A * 0.5) * lap, 12, 0)[:8]
            own_ref[1, k - 2] = base + A * own_ref[0, k - 2] * pltpu.roll(g, 12, 0)[:8]
    for z in range(BZ):
        own_ref[2, z] = lab_ref[z]
    for ref, start in ((me_ref, 6 - 6 * py), (mo_ref, 6 * py)):
        ref[:12] = own_ref[...].reshape(12, BY, X).astype(SENT)
        for z in range(BZ):
            ref[12 + 4 * z : 16 + 4 * z] = slope2_ref[z, pl.ds(start, 2)].reshape(4, 8, X).astype(SENT)


def widen(at, me_ref, slope2_ref, re_ref, ro_ref, ma_ref, mb_ref, s2y_ref):
    pz, py = at[2], at[3]
    ma_ref[12:24] = me_ref[:12]
    ma_ref[pl.ds(24 - 24 * py, 12)] = re_ref[:12]
    ma_ref[pl.ds(24 * py, 12)] = ro_ref[:12]
    for z in range(BZ):
        s2y_ref[z, 2 : 2 + BY] = slope2_ref[z].astype(bf16)
        for ref, start in ((re_ref, 10 - 10 * py), (ro_ref, 10 * py)):
            rows = ref[12 + 4 * z : 16 + 4 * z].astype(f32).reshape(2, C, X)
            s2y_ref[z, pl.ds(start, 2)] = rows.astype(bf16)
    for k in range(2):
        rows = s2y_ref[2 - 2 * pz + k].astype(f32).reshape(24, 8, X)
        ma_ref[36 + 24 * k : 60 + 24 * k] = rows.astype(SENT)
        rows = s2y_ref[2 * pz + k].astype(f32).reshape(24, 8, X)
        mb_ref[24 * k : 24 + 24 * k] = rows.astype(SENT)


def relay(ma_ref, ra_ref, mb_ref):
    mb_ref[:36] = ma_ref[:36]
    mb_ref[36:] = ra_ref[:36]


def march(nz, ny, at, own_ref, ye_ref, mate_ref, far_ref, far2_ref, g0_ref, dpre_ref,
          sp, lab, ph, w_s, dz_s, dy_s, dx_s, ag_s, ds, dd):
    iz, iy, pz = at[0], at[1], at[2]
    base = 4 * pz

    def place(start, block):
        for k in range(BZ):
            for ref, f in ((sp, 0), (ph, 1), (lab, 2)):
                plane = jnp.concatenate([block(i, f, k).astype(f32) for i in range(3)], axis=0)
                if f == 1:
                    ph[0, start + k] = plane
                else:
                    ref[start + k] = plane

    def piece(ref, first):
        return lambda i, f, k: ref[first + 12 * i + 4 * f + k]

    def mine(i, f, k):
        return own_ref[f, k] if i == 1 else ye_ref[12 * i + 4 * f + k]

    place(8 + 4 * pz, mine)
    place(12 - 4 * pz, piece(mate_ref, 0))
    place(16 * pz + 4 - 4 * pz, piece(far_ref, 0))
    place(16 * pz + 4 * pz, piece(far_ref, 36))
    place(16 - 16 * pz + 4 * pz, piece(far2_ref, 0))
    place(16 - 16 * pz + 4 - 4 * pz, piece(far2_ref, 36))

    dd[0, 0] = jnp.zeros((24, X), f32)
    rows_in = inside(iy * BY - 8, (24, X), ny)
    first_plane = (iz - pz) * BZ - 8

    def within(z):
        zg = first_plane + z
        return rows_in & (zg >= 0) & (zg < nz)

    for t in (1, 2, 3):

        def step(i, carry, t=t):
            z = base + i
            centre, uz, lz = ph[t - 1, z], ph[t - 1, z + 1], ph[t - 1, z - 1]
            ly, uy = pltpu.roll(centre, 1, 0), pltpu.roll(centre, 23, 0)
            lx, ux = sides(centre)
            dz, dy, dx = (uz - lz) * 0.5, (uy - ly) * 0.5, (ux - lx) * 0.5
            g = jnp.sqrt(dz * dz + dy * dy + dx * dx + FLOOR)
            lap = uz + lz + uy + ly + ux + lx - 6.0 * centre
            speed = sp[z]
            ag = A * g
            new = jnp.where(within(z), centre + speed * ag + (A * 0.5) * lap, 0.0)
            w_s[t - 1, z] = (A * 0.5) * speed / g
            dz_s[t - 1, z] = dz
            dy_s[t - 1, z] = dy
            dx_s[t - 1, z] = dx
            ag_s[t - 1, z] = ag
            if t < 3:
                ph[t, z] = new
            else:
                dd[0, z] = jnp.where(within(z), jax.nn.sigmoid(new) - lab[z], 0.0)
            return carry

        lax.fori_loop(t, 20 - t, step, 0, unroll=2)

    for n, t in enumerate((3, 2, 1)):
        src, dst = n % 2, (n + 1) % 2

        def back(i, carry, t=t, n=n, src=src, dst=dst):
            l1, a1, a2 = carry
            z = base + i
            d = dd[src, z]
            add = ag_s[t - 1, z] * d
            ds[z] = add if n == 0 else ds[z] + add
            w = w_s[t - 1, z] * d
            e = (A * 0.5) * d
            qz, qy, qx = w * dz_s[t - 1, z], w * dy_s[t - 1, z], w * dx_s[t - 1, z]
            local = (1.0 - 3.0 * A) * d
            local = local + pltpu.roll(e + qy, 1, 0) + pltpu.roll(e - qy, 23, 0)
            local = local + sides(e + qx)[0] + sides(e - qx)[1]
            dd[dst, z - 1] = jnp.where(within(z - 1), l1 + a2 + (e - qz), 0.0)
            return local, e + qz, a1

        zero = dd[0, 0]
        lax.fori_loop(3 + n, 17 - n, back, (zero, zero, zero), unroll=2)

    for k in range(8):
        z = base + 6 + k
        speed = sp[z]
        left = 1.0 - speed * speed
        one = pltpu.roll(ds[z] * left, 20, 0)[:16]
        two = pltpu.roll(dd[1, z] * left, 20, 0)[:16]
        dpre_ref[k] = one + A * two * g0_ref[k]


def backward(at, dpre_ref, slope2_ref, s2y_ref, ra_ref, rb_ref, sw_ref, hx_ref, fx_ref, slope1_ref,
             top_ref, w1_ref, w2_ref, df_ref, grad_ref, dx_ref, ex_ref):
    pz = at[2]
    sw = sw_ref[...]

    def second(z, slope):
        for y in range(BY + 4):
            d = dpre_ref[z, 2 + y : 3 + y, :]
            value = (sw * d * slope(y))[None]
            low, up = sides(value)
            dx_ref[z, y : y + 1, 0] = low.astype(bf16)
            dx_ref[z, y : y + 1, 1] = value.astype(bf16)
            dx_ref[z, y : y + 1, 2] = up.astype(bf16)

    for k in range(BZ):
        def own(y, k=k):
            if 2 <= y < 2 + BY:
                return slope2_ref[k, y - 2]
            return s2y_ref[k, y].astype(f32)

        second(2 + k, own)
    for k in range(2):
        for ref, first, z in ((ra_ref, 36, 6 - 6 * pz), (rb_ref, 0, 6 * pz)):
            def far(y, ref=ref, first=first + 24 * k):
                return ref[first + 2 * y : first + 2 * y + 2].astype(f32).reshape(C, X)

            second(z + k, far)

    w2 = w2_ref[...]
    w1 = w1_ref[...]

    def hidden(z, carry):
        for y in range(0, BY + 2, 2):
            both = two_rows(w2, dx_ref, z, y)
            d = jnp.concatenate([(v * slope1_ref[z, y + j])[None] for j, v in enumerate(both)], axis=0)
            low, up = sides(d)
            ex_ref[z, y : y + 2, 0] = low.astype(bf16)
            ex_ref[z, y : y + 2, 1] = d.astype(bf16)
            ex_ref[z, y : y + 2, 2] = up.astype(bf16)
        return carry

    lax.fori_loop(0, BZ + 2, hidden, 0)

    def features(z, carry):
        rows = []
        for y in range(0, BY, 2):
            a, b = two_rows(w1, ex_ref, z, y)
            rows += [a[None], b[None]]
        plane = jnp.concatenate(rows, axis=0)
        df_ref[:, z] = jnp.transpose(plane, (1, 0, 2)).astype(bf16)
        return carry

    lax.fori_loop(0, BZ, features, 0)

    nt = (((1,), (1,)), ((), ()))

    def weights(z, carry):
        g1, g2, gs = carry
        d2 = jnp.concatenate([dx_ref[z + 2, y + 2, 1] for y in range(BY)], axis=1)
        d1 = jnp.concatenate([ex_ref[z + 1, y + 1, 1] for y in range(BY)], axis=1)
        p2 = [hx_ref[pl.ds(z, 3), y : y + 3].reshape(TAPS, X) for y in range(BY)]
        p1 = [fx_ref[pl.ds(z, 3), y : y + 3].reshape(TAPS, X) for y in range(BY)]
        g2 = g2 + lax.dot_general(d2, jnp.concatenate(p2, axis=1), nt, preferred_element_type=f32)
        g1 = g1 + lax.dot_general(d1, jnp.concatenate(p1, axis=1), nt, preferred_element_type=f32)
        for y in range(BY):
            gs = gs + dpre_ref[z + 2, 4 + y : 5 + y, :] * top_ref[z, y]
        return g1, g2, gs

    zero = jnp.zeros((C, TAPS), f32)
    g1, g2, gs = lax.fori_loop(0, BZ, weights, (zero, zero, jnp.zeros((C, X), f32)))
    grad_ref[...] = jnp.zeros_like(grad_ref)
    for i, g in enumerate((g1, g2)):
        grad_ref[i, :C] = g[:, :256]
        grad_ref[i, C:, : TAPS - 256] = g[:, 256:]
    grad_ref[0, C : C + 1, TAPS - 256 : TAPS - 240] = jnp.sum(jnp.transpose(gs), axis=0, keepdims=True)


def finish(a_ref, b_ref, first_ref, second_ref, speed_ref):
    a, b = a_ref[...], b_ref[...]
    total = jnp.sum(a * a) + jnp.sum(b * b)
    count = 54.0 * C * C + C
    factor = 1.0 / jnp.maximum(jnp.sqrt(jnp.full((1, 1), total)) / jnp.sqrt(f32(count)), 1.0)
    a, b = a * factor, b * factor
    for t in range(27):
        row, lane = C * (t // 16), C * (t % 16)
        first_ref[t] = a[row : row + C, lane : lane + C]
        second_ref[t] = b[row : row + C, lane : lane + C]
    speed_ref[...] = a[C : C + 1, TAPS - 256 : TAPS - 240]


def call(kernel, outs, scratch=(), flops=0):
    smem = pl.BlockSpec(memory_space=pltpu.SMEM)
    vmem = pl.BlockSpec(memory_space=pltpu.VMEM)

    def run(at, *args):
        args = ((at,) if at is not None else ()) + args
        specs = [smem if (i == 0 and at is not None) else vmem for i in range(len(args))]
        many = isinstance(outs, (list, tuple))
        size = sum(a.size * a.dtype.itemsize for a in args)
        return pl.pallas_call(
            kernel,
            out_shape=outs,
            in_specs=specs,
            out_specs=[vmem] * len(outs) if many else vmem,
            scratch_shapes=list(scratch),
            cost_estimate=pl.CostEstimate(flops=flops, bytes_accessed=size, transcendentals=0),
            compiler_params=pltpu.CompilerParams(vmem_limit_bytes=16 * 1024 * 1024),
        )(*args)

    return run


def shape(dims, dtype=bf16):
    return jax.ShapeDtypeStruct(dims, dtype)


def even(value, axis):
    n = lax.axis_size(axis)
    return lax.ppermute(value, axis, [(i, i ^ 1) for i in range(n)])


def odd(value, axis):
    n = lax.axis_size(axis)
    pairs = [(i, i + 1) for i in range(1, n - 1, 2)]
    return lax.ppermute(value, axis, pairs + [(j, i) for i, j in pairs])


def groups(n, unit):
    size = max(1, min(4, n // unit))
    firsts = [i for i in range(n) if (i // unit) % size == 0]
    return [[i + unit * k for k in range(size)] for i in firsts]


def total_of(grad, iz):
    core = iz % 2
    keep = lax.dynamic_index_in_dim(grad, core, 0, keepdims=False)
    give = lax.dynamic_index_in_dim(grad, 1 - core, 0, keepdims=False)
    part = keep + even(give, "gz")
    for axis, unit in (("gy", 1), ("gy", 4), ("gz", 8), ("gz", 2)):
        sets = groups(lax.axis_size(axis), unit)
        if len(sets[0]) > 1 and unit == 8:
            copies = jnp.broadcast_to(part[None], (len(sets[0]),) + part.shape)
            part = jnp.sum(lax.all_to_all(copies, axis, 0, 0, axis_index_groups=sets), axis=0)
        elif len(sets[0]) > 1:
            part = jnp.sum(lax.all_gather(part, axis, axis_index_groups=sets), axis=0)
    other = even(part, "gz")
    return jnp.where(core == 0, part, other), jnp.where(core == 0, other, part)


def on_device(features, labels, sign_map, conv_first, conv_second, speed_weight):
    nz, ny = BZ * lax.axis_size("gz"), BY * lax.axis_size("gy")
    iz, iy = lax.axis_index("gz"), lax.axis_index("gy")
    pz, py = iz % 2, iy % 2
    at = jnp.stack([iz, iy, pz, py]).astype(jnp.int32)
    taps = [w.transpose(2, 3, 4, 0, 1).reshape(27, C, C) for w in (conv_first, conv_second)]
    w1, w2, w1b, w2b, sw, target = call(
        build, [shape((2 * C, 36 * C))] * 4 + [shape((C, X), f32), shape((BZ, BY, X), f32)]
    )(None, *taps, speed_weight.reshape(1, C), labels)

    ft, me, mo = call(prepare, [shape((BZ, BY, C, X)), shape((9, C, X)), shape((9, C, X))])(
        at, features, sign_map
    )
    ro = odd(mo, "gy")
    re = even(me, "gy")
    fy, sy, ma, mb = call(
        extend,
        [shape((BZ, 12, C, X)), shape((BZ, 16, X), f32), shape((27, C, X)), shape((27, C, X))],
    )(at, ft, sign_map, re, ro)
    rb = odd(mb, "gz")
    ra = even(ma, "gz")

    fx, hx, slope1, slope2, top, fe, fo, own, g0 = call(
        lambda *refs: forward(nz, ny, *refs),
        [
            shape((6, 10, 3, C, X)),
            shape((6, 10, 3, C, X)),
            shape((6, 10, C, X), f32),
            shape((BZ, BY, C, X), f32),
            shape((BZ, BY, C, X), f32),
            shape((28, 8, X), SENT),
            shape((28, 8, X), SENT),
            shape((3, BZ, BY, X), f32),
            shape((8, 16, X), f32),
        ],
        [pltpu.VMEM((10, 16, X), f32), pltpu.VMEM((8, 12, 3, C, X), bf16)],
    )(at, fy, sy, ra, rb, target, w1, w2, sw)

    go = odd(fo, "gy")
    ge = even(fe, "gy")
    fa, fs, s2y = call(
        widen, [shape((84, 8, X), SENT), shape((48, 8, X), SENT), shape((BZ, 12, C, X))]
    )(at, fe, slope2, ge, go)
    ha = even(fa, "gz")
    hb = odd(call(relay, shape((72, 8, X), SENT))(None, fa, ha), "gz")
    hb, fs = lax.optimization_barrier((hb, fs))
    hs = odd(fs, "gz")
    hc = even(hb, "gz")

    plane = (24, 24, X)
    dpre = call(
        lambda *refs: march(nz, ny, *refs),
        shape((8, 16, X), f32),
        [
            pltpu.VMEM(plane, f32),
            pltpu.VMEM(plane, f32),
            pltpu.VMEM((3,) + plane, f32),
            pltpu.VMEM((3,) + plane, f32),
            pltpu.VMEM((3,) + plane, f32),
            pltpu.VMEM((3,) + plane, f32),
            pltpu.VMEM((3,) + plane, f32),
            pltpu.VMEM((3,) + plane, f32),
            pltpu.VMEM(plane, f32),
            pltpu.VMEM((2,) + plane, f32),
        ],
    )(at, own, fa, ha, hb, hc, g0)

    d_features, grad = call(
        backward,
        [shape((C, BZ, BY, X)), shape((2, 2 * C, 256), f32)],
        [pltpu.VMEM((8, 12, 3, C, X), bf16), pltpu.VMEM((6, 10, 3, C, X), bf16)],
    )(at, dpre, slope2, s2y, ha, hs, sw, hx, fx, slope1, top, w1b, w2b)

    a, b = total_of(grad, iz)
    tap_major = shape((27, C, C), f32)
    first, second, speed = call(finish, [tap_major, tap_major, shape((1, C), f32)])(None, a, b)
    first, second = (
        g.reshape(3, 3, 3, C, C).transpose(3, 4, 0, 1, 2) for g in (first, second)
    )
    return d_features, first, second, speed.reshape(C)


def solution(mesh):
    in_specs = (P(None, "gz", "gy", None), P("gz", "gy", None), P("gz", "gy", None), P(), P(), P())
    out_specs = (P(None, "gz", "gy", None), P(), P(), P())

    return jax.shard_map(
        on_device, mesh=mesh, in_specs=in_specs, out_specs=out_specs, check_vma=False
    )
```

```python
import jax
import jax.numpy as jnp
from jax import lax
from jax.experimental import pallas as pl
from jax.experimental.pallas import tpu as pltpu
from jax.sharding import PartitionSpec as P


C = 16
BZ = 4
BY = 8
X = 128
TAPS = 27 * C
A = 0.25
FLOOR = 0.1
SENT = jnp.bfloat16
f32 = jnp.float32
bf16 = jnp.bfloat16


def sides(v):
    axis = v.ndim - 1
    lane = lax.broadcasted_iota(jnp.int32, v.shape, axis)
    low = jnp.where(lane == 0, 0.0, pltpu.roll(v, 1, axis))
    up = jnp.where(lane == X - 1, 0.0, pltpu.roll(v, X - 1, axis))
    return low, up


def put_taps(ref, index, v):
    low, up = sides(v)
    ref[index, :, 0] = low.astype(bf16)
    ref[index, :, 1] = v.astype(bf16)
    ref[index, :, 2] = up.astype(bf16)


def two_rows(weight, taps_ref, z, y):
    patch = taps_ref[pl.ds(z, 3), y : y + 4].reshape(4 * 9 * C, X)
    out = jnp.dot(weight, patch, preferred_element_type=f32)
    return out[:C], out[C:]


def inside(start, shape, limit):
    row = start + lax.broadcasted_iota(jnp.int32, shape, 0)
    return (row >= 0) & (row < limit)


def build(c1_ref, c2_ref, sp_ref, lab_ref, w1_ref, w2_ref, w1b_ref, w2b_ref, sw_ref, labf_ref):
    sw_ref[...] = jnp.transpose(jnp.broadcast_to(sp_ref[...], (X, C)))
    labf_ref[...] = lab_ref[...].astype(f32)
    zero = jnp.zeros((C, C), f32)
    for src, fwd, adj in ((c1_ref, w1_ref, w1b_ref), (c2_ref, w2_ref, w2b_ref)):
        for j in range(2):
            one, two = [], []
            for a in range(3):
                for b in range(4):
                    for c in range(3):
                        tap = (a * 3 + b - j) * 3 + c
                        ok = 0 <= b - j < 3
                        one.append(src[tap].astype(f32) if ok else zero)
                        two.append(src[26 - tap].astype(f32).T if ok else zero)
            fwd[C * j : C * j + C] = jnp.concatenate(one, axis=1).astype(bf16)
            adj[C * j : C * j + C] = jnp.concatenate(two, axis=1).astype(bf16)


def prepare(at, f_ref, s_ref, ft_ref, me_ref, mo_ref):
    py = at[3]
    row = lax.broadcasted_iota(jnp.int32, (BY, X), 0)
    for z in range(BZ):
        ft_ref[z] = jnp.transpose(f_ref[:, z].astype(f32), (1, 0, 2)).astype(bf16)
    for ref, start, high in ((me_ref, 6 - 6 * py, py == 0), (mo_ref, 6 * py, py == 1)):
        for z in range(BZ):
            ref[2 * z : 2 * z + 2] = ft_ref[z, pl.ds(start, 2)]
        parts = []
        for z in range(BZ):
            own = s_ref[z].astype(f32)
            parts.append(jnp.where(high, pltpu.roll(own, 4, 0), own))
        halves = [jnp.where(row < 4, parts[i], pltpu.roll(parts[i + 1], 4, 0)) for i in (0, 2)]
        ref[2 * BZ] = jnp.concatenate(halves, axis=0).astype(bf16)


def extend(at, ft_ref, s_ref, re_ref, ro_ref, fy_ref, sy_ref, ma_ref, mb_ref):
    pz, py = at[2], at[3]
    row = lax.broadcasted_iota(jnp.int32, (BY, X), 0)
    te = re_ref[2 * BZ].astype(f32)
    to = ro_ref[2 * BZ].astype(f32)
    before = jnp.where(py == 0, to, te)
    after = jnp.where(py == 0, te, to)
    for z in range(BZ):
        fy_ref[z, 2 : 2 + BY] = ft_ref[z]
        fy_ref[z, pl.ds(10 - 10 * py, 2)] = re_ref[2 * z : 2 * z + 2]
        fy_ref[z, pl.ds(10 * py, 2)] = ro_ref[2 * z : 2 * z + 2]
        half, low = (z // 2) * 8, (z % 2) * 4
        own = pltpu.roll(s_ref[z].astype(f32), 4, 0)
        b = before[half : half + 8]
        a = after[half : half + 8]
        b = pltpu.roll(b, 4, 0) if low else b
        a = a if low else pltpu.roll(a, 4, 0)
        sy_ref[z] = jnp.concatenate([jnp.where(row < 4, b, own), jnp.where(row < 4, own, a)], axis=0)
    for ref, start, sign in ((ma_ref, 2 - 2 * pz, 1 - pz), (mb_ref, 2 * pz, pz)):
        for k in range(2):
            ref[12 * k : 12 * k + 12] = fy_ref[start + k]
        for k in range(3):
            ref[24 + k] = sy_ref[sign + k].astype(bf16)


def forward(nz, ny, at, fy_ref, sy_ref, ma_ref, mb_ref, lab_ref, w1_ref, w2_ref, sw_ref,
            fc_ref, hx_ref, slope1_ref, slope2_ref, top_ref, me_ref, mo_ref, own_ref, g0_ref, p_ref, fx_ref):
    iz, iy, pz, py = at[0], at[1], at[2], at[3]
    for k in range(BZ):
        put_taps(fx_ref, 2 + k, fy_ref[k].astype(f32))
    for k in range(2):
        put_taps(fx_ref, 6 - 6 * pz + k, ma_ref[12 * k : 12 * k + 12].astype(f32))
        put_taps(fx_ref, 6 * pz + k, mb_ref[12 * k : 12 * k + 12].astype(f32))
    fc_ref[...] = fx_ref[1:7, 1:11]
    w1 = w1_ref[...]
    w2 = w2_ref[...]

    def first(z, carry):
        zg = iz * BZ - 1 + z
        zin = (zg >= 0) & (zg < nz)
        for y in range(0, BY + 2, 2):
            acts = two_rows(w1, fx_ref, z, y)
            hid = []
            for j, act in enumerate(acts):
                yg = iy * BY - 1 + y + j
                keep = jnp.where(zin & (yg >= 0) & (yg < ny), 1.0, 0.0)
                sig = jax.nn.sigmoid(act)
                slope1_ref[z, y + j] = sig * (1.0 + act * (1.0 - sig)) * keep
                hid.append((act * sig * keep)[None])
            hid = jnp.concatenate(hid, axis=0)
            low, up = sides(hid)
            hx_ref[z, y : y + 2, 0] = low.astype(bf16)
            hx_ref[z, y : y + 2, 1] = hid.astype(bf16)
            hx_ref[z, y : y + 2, 2] = up.astype(bf16)
        return carry

    lax.fori_loop(0, BZ + 2, first, 0)
    sw = sw_ref[...]

    def second(z, carry):
        rows = []
        for y in range(0, BY, 2):
            for j, act in enumerate(two_rows(w2, hx_ref, z, y)):
                sig = jax.nn.sigmoid(act)
                top = act * sig
                top_ref[z, y + j] = top
                slope2_ref[z, y + j] = sig * (1.0 + act * (1.0 - sig))
                rows.append(jnp.sum(top * sw, axis=0, keepdims=True))
        own_ref[0, z] = jnp.tanh(jnp.concatenate(rows, axis=0))
        return carry

    lax.fori_loop(0, BZ, second, 0)

    for k in range(BZ):
        p_ref[3 + k] = sy_ref[k]
    for k in range(3):
        p_ref[7 - 7 * pz + k] = ma_ref[24 + k].astype(f32)
        p_ref[7 * pz + k] = mb_ref[24 + k].astype(f32)
    rows_in = inside(iy * BY - 4, (16, X), ny)
    for k in range(10):
        zg = iz * BZ - 3 + k
        p_ref[k] = jnp.where(rows_in & (zg >= 0) & (zg < nz), 2.0 * p_ref[k] - 1.0, 0.0)
    for k in range(8):
        centre, uz, lz = p_ref[k + 1], p_ref[k + 2], p_ref[k]
        ly, uy = pltpu.roll(centre, 1, 0), pltpu.roll(centre, 15, 0)
        lx, ux = sides(centre)
        dz, dy, dx = (uz - lz) * 0.5, (uy - ly) * 0.5, (ux - lx) * 0.5
        g = jnp.sqrt(dz * dz + dy * dy + dx * dx + FLOOR)
        g0_ref[k] = g
        if 2 <= k < 6:
            lap = uz + lz + uy + ly + ux + lx - 6.0 * centre
            base = pltpu.roll(centre + (A * 0.5) * lap, 12, 0)[:8]
            own_ref[1, k - 2] = base + A * own_ref[0, k - 2] * pltpu.roll(g, 12, 0)[:8]
    for z in range(BZ):
        own_ref[2, z] = lab_ref[z]
    for ref, start in ((me_ref, 6 - 6 * py), (mo_ref, 6 * py)):
        ref[:12] = own_ref[...].reshape(12, BY, X).astype(SENT)
        for z in range(BZ):
            ref[12 + 4 * z : 16 + 4 * z] = slope2_ref[z, pl.ds(start, 2)].reshape(4, 8, X).astype(SENT)


def widen(at, me_ref, slope2_ref, re_ref, ro_ref, ma_ref, mb_ref, s2y_ref):
    pz, py = at[2], at[3]
    ma_ref[12:24] = me_ref[:12]
    ma_ref[pl.ds(24 - 24 * py, 12)] = re_ref[:12]
    ma_ref[pl.ds(24 * py, 12)] = ro_ref[:12]
    for z in range(BZ):
        s2y_ref[z, 2 : 2 + BY] = slope2_ref[z].astype(bf16)
        for ref, start in ((re_ref, 10 - 10 * py), (ro_ref, 10 * py)):
            rows = ref[12 + 4 * z : 16 + 4 * z].astype(f32).reshape(2, C, X)
            s2y_ref[z, pl.ds(start, 2)] = rows.astype(bf16)
    for k in range(2):
        rows = s2y_ref[2 - 2 * pz + k].astype(f32).reshape(24, 8, X)
        ma_ref[36 + 24 * k : 60 + 24 * k] = rows.astype(SENT)
        rows = s2y_ref[2 * pz + k].astype(f32).reshape(24, 8, X)
        mb_ref[24 * k : 24 + 24 * k] = rows.astype(SENT)


def relay(at, ma_ref, ra_ref, mb_ref):
    pz = at[2]
    mb_ref[:36] = ma_ref[:36]
    for i in range(3):
        mb_ref[36 + 9 * i : 44 + 9 * i] = ra_ref[12 * i : 12 * i + 8]
        mb_ref[44 + 9 * i] = ra_ref[12 * i + 8 + 3 * pz]


def march(nz, ny, at, own_ref, ye_ref, mate_ref, far_ref, far2_ref, g0_ref, dpre_ref,
          sp, lab, ph, w_s, dz_s, dy_s, dx_s, ag_s, ds, dd):
    iz, iy, pz = at[0], at[1], at[2]
    base = 4 * pz

    def place(start, block):
        for k in range(BZ):
            for ref, f in ((sp, 0), (ph, 1), (lab, 2)):
                plane = jnp.concatenate([block(i, f, k).astype(f32) for i in range(3)], axis=0)
                if f == 1:
                    ph[0, start + k] = plane
                else:
                    ref[start + k] = plane

    def piece(ref, first):
        return lambda i, f, k: ref[first + 12 * i + 4 * f + k]

    def mine(i, f, k):
        return own_ref[f, k] if i == 1 else ye_ref[12 * i + 4 * f + k]

    place(8 + 4 * pz, mine)
    place(12 - 4 * pz, piece(mate_ref, 0))
    place(16 * pz + 4 - 4 * pz, piece(far_ref, 0))
    place(16 - 16 * pz + 4 * pz, piece(far2_ref, 0))

    def beyond(i, f, k):
        return far_ref[44 + 9 * i if f == 2 else 36 + 9 * i + 4 * f + k]

    place(16 * pz + 4 * pz, beyond)

    dd[0, 0] = jnp.zeros((24, X), f32)
    rows_in = inside(iy * BY - 8, (24, X), ny)
    first_plane = (iz - pz) * BZ - 8

    def within(z):
        zg = first_plane + z
        return rows_in & (zg >= 0) & (zg < nz)

    for t in (1, 2, 3):

        def step(i, carry, t=t):
            z = base + i
            centre, uz, lz = ph[t - 1, z], ph[t - 1, z + 1], ph[t - 1, z - 1]
            ly, uy = pltpu.roll(centre, 1, 0), pltpu.roll(centre, 23, 0)
            lx, ux = sides(centre)
            dz, dy, dx = (uz - lz) * 0.5, (uy - ly) * 0.5, (ux - lx) * 0.5
            g = jnp.sqrt(dz * dz + dy * dy + dx * dx + FLOOR)
            lap = uz + lz + uy + ly + ux + lx - 6.0 * centre
            speed = sp[z]
            ag = A * g
            new = jnp.where(within(z), centre + speed * ag + (A * 0.5) * lap, 0.0)
            w_s[t - 1, z] = (A * 0.5) * speed / g
            dz_s[t - 1, z] = dz
            dy_s[t - 1, z] = dy
            dx_s[t - 1, z] = dx
            ag_s[t - 1, z] = ag
            if t < 3:
                ph[t, z] = new
            else:
                dd[0, z] = jnp.where(within(z), jax.nn.sigmoid(new) - lab[z], 0.0)
            return carry

        lax.fori_loop(t, 20 - t, step, 0, unroll=2)

    for n, t in enumerate((3, 2, 1)):
        src, dst = n % 2, (n + 1) % 2

        def back(i, carry, t=t, n=n, src=src, dst=dst):
            l1, a1, a2 = carry
            z = base + i
            d = dd[src, z]
            add = ag_s[t - 1, z] * d
            ds[z] = add if n == 0 else ds[z] + add
            w = w_s[t - 1, z] * d
            e = (A * 0.5) * d
            qz, qy, qx = w * dz_s[t - 1, z], w * dy_s[t - 1, z], w * dx_s[t - 1, z]
            local = (1.0 - 3.0 * A) * d
            local = local + pltpu.roll(e + qy, 1, 0) + pltpu.roll(e - qy, 23, 0)
            local = local + sides(e + qx)[0] + sides(e - qx)[1]
            dd[dst, z - 1] = jnp.where(within(z - 1), l1 + a2 + (e - qz), 0.0)
            return local, e + qz, a1

        zero = dd[0, 0]
        lax.fori_loop(3 + n, 17 - n, back, (zero, zero, zero), unroll=2)

    for k in range(8):
        z = base + 6 + k
        speed = sp[z]
        left = 1.0 - speed * speed
        one = pltpu.roll(ds[z] * left, 20, 0)[:16]
        two = pltpu.roll(dd[1, z] * left, 20, 0)[:16]
        dpre_ref[k] = one + A * two * g0_ref[k]


def backward(at, dpre_ref, slope2_ref, s2y_ref, ra_ref, rb_ref, sw_ref, hx_ref, fx_ref, slope1_ref,
             top_ref, w1_ref, w2_ref, df_ref, grad_ref, dx_ref, ex_ref):
    pz = at[2]
    sw = sw_ref[...]

    def second(z, slope):
        for y in range(BY + 4):
            d = dpre_ref[z, 2 + y : 3 + y, :]
            value = (sw * d * slope(y))[None]
            low, up = sides(value)
            dx_ref[z, y : y + 1, 0] = low.astype(bf16)
            dx_ref[z, y : y + 1, 1] = value.astype(bf16)
            dx_ref[z, y : y + 1, 2] = up.astype(bf16)

    for k in range(BZ):
        def own(y, k=k):
            if 2 <= y < 2 + BY:
                return slope2_ref[k, y - 2]
            return s2y_ref[k, y].astype(f32)

        second(2 + k, own)
    for k in range(2):
        for ref, first, z in ((ra_ref, 36, 6 - 6 * pz), (rb_ref, 0, 6 * pz)):
            def far(y, ref=ref, first=first + 24 * k):
                return ref[first + 2 * y : first + 2 * y + 2].astype(f32).reshape(C, X)

            second(z + k, far)

    w2 = w2_ref[...]
    w1 = w1_ref[...]

    def hidden(z, carry):
        for y in range(0, BY + 2, 2):
            both = two_rows(w2, dx_ref, z, y)
            d = jnp.concatenate([(v * slope1_ref[z, y + j])[None] for j, v in enumerate(both)], axis=0)
            low, up = sides(d)
            ex_ref[z, y : y + 2, 0] = low.astype(bf16)
            ex_ref[z, y : y + 2, 1] = d.astype(bf16)
            ex_ref[z, y : y + 2, 2] = up.astype(bf16)
        return carry

    lax.fori_loop(0, BZ + 2, hidden, 0)

    def features(z, carry):
        rows = []
        for y in range(0, BY, 2):
            a, b = two_rows(w1, ex_ref, z, y)
            rows += [a[None], b[None]]
        plane = jnp.concatenate(rows, axis=0)
        df_ref[:, z] = jnp.transpose(plane, (1, 0, 2)).astype(bf16)
        return carry

    lax.fori_loop(0, BZ, features, 0)

    nt = (((1,), (1,)), ((), ()))

    def weights(z, carry):
        g1, g2, gs = carry
        d2 = jnp.concatenate([dx_ref[z + 2, y + 2, 1] for y in range(BY)], axis=1)
        d1 = jnp.concatenate([ex_ref[z + 1, y + 1, 1] for y in range(BY)], axis=1)
        p2 = [hx_ref[pl.ds(z, 3), y : y + 3].reshape(TAPS, X) for y in range(BY)]
        p1 = [fx_ref[pl.ds(z, 3), y : y + 3].reshape(TAPS, X) for y in range(BY)]
        g2 = g2 + lax.dot_general(d2, jnp.concatenate(p2, axis=1), nt, preferred_element_type=f32)
        g1 = g1 + lax.dot_general(d1, jnp.concatenate(p1, axis=1), nt, preferred_element_type=f32)
        for y in range(BY):
            gs = gs + dpre_ref[z + 2, 4 + y : 5 + y, :] * top_ref[z, y]
        return g1, g2, gs

    zero = jnp.zeros((C, TAPS), f32)
    g1, g2, gs = lax.fori_loop(0, BZ, weights, (zero, zero, jnp.zeros((C, X), f32)))
    grad_ref[...] = jnp.zeros_like(grad_ref)
    for i, g in enumerate((g1, g2)):
        grad_ref[i, :C] = g[:, :256]
        grad_ref[i, C:, : TAPS - 256] = g[:, 256:]
    grad_ref[0, C : C + 1, TAPS - 256 : TAPS - 240] = jnp.sum(jnp.transpose(gs), axis=0, keepdims=True)


def finish(a_ref, b_ref, first_ref, second_ref, speed_ref):
    a, b = a_ref[...], b_ref[...]
    total = jnp.sum(a * a) + jnp.sum(b * b)
    count = 54.0 * C * C + C
    factor = 1.0 / jnp.maximum(jnp.sqrt(jnp.full((1, 1), total)) / jnp.sqrt(f32(count)), 1.0)
    a, b = a * factor, b * factor
    for t in range(27):
        row, lane = C * (t // 16), C * (t % 16)
        first_ref[t] = a[row : row + C, lane : lane + C]
        second_ref[t] = b[row : row + C, lane : lane + C]
    speed_ref[...] = a[C : C + 1, TAPS - 256 : TAPS - 240]


def call(kernel, outs, scratch=(), flops=0):
    smem = pl.BlockSpec(memory_space=pltpu.SMEM)
    vmem = pl.BlockSpec(memory_space=pltpu.VMEM)

    def run(at, *args):
        args = ((at,) if at is not None else ()) + args
        specs = [smem if (i == 0 and at is not None) else vmem for i in range(len(args))]
        many = isinstance(outs, (list, tuple))
        size = sum(a.size * a.dtype.itemsize for a in args)
        return pl.pallas_call(
            kernel,
            out_shape=outs,
            in_specs=specs,
            out_specs=[vmem] * len(outs) if many else vmem,
            scratch_shapes=list(scratch),
            cost_estimate=pl.CostEstimate(flops=flops, bytes_accessed=size, transcendentals=0),
            compiler_params=pltpu.CompilerParams(vmem_limit_bytes=16 * 1024 * 1024),
        )(*args)

    return run


def shape(dims, dtype=bf16):
    return jax.ShapeDtypeStruct(dims, dtype)


def even(value, axis):
    n = lax.axis_size(axis)
    return lax.ppermute(value, axis, [(i, i ^ 1) for i in range(n)])


def odd(value, axis):
    n = lax.axis_size(axis)
    pairs = [(i, i + 1) for i in range(1, n - 1, 2)]
    return lax.ppermute(value, axis, pairs + [(j, i) for i, j in pairs])


def groups(n, unit):
    size = max(1, min(4, n // unit))
    firsts = [i for i in range(n) if (i // unit) % size == 0]
    return [[i + unit * k for k in range(size)] for i in firsts]


def total_of(grad, iz):
    core = iz % 2
    keep = lax.dynamic_index_in_dim(grad, core, 0, keepdims=False)
    give = lax.dynamic_index_in_dim(grad, 1 - core, 0, keepdims=False)
    part = keep + even(give, "gz")
    for axis, unit in (("gy", 1), ("gy", 4), ("gz", 8), ("gz", 2)):
        sets = groups(lax.axis_size(axis), unit)
        if len(sets[0]) > 1:
            copies = jnp.broadcast_to(part[None], (len(sets[0]),) + part.shape)
            part = jnp.sum(lax.all_to_all(copies, axis, 0, 0, axis_index_groups=sets), axis=0)
    other = even(part, "gz")
    return jnp.where(core == 0, part, other), jnp.where(core == 0, other, part)


def on_device(features, labels, sign_map, conv_first, conv_second, speed_weight):
    nz, ny = BZ * lax.axis_size("gz"), BY * lax.axis_size("gy")
    iz, iy = lax.axis_index("gz"), lax.axis_index("gy")
    pz, py = iz % 2, iy % 2
    at = jnp.stack([iz, iy, pz, py]).astype(jnp.int32)
    taps = [w.transpose(2, 3, 4, 0, 1).reshape(27, C, C) for w in (conv_first, conv_second)]
    w1, w2, w1b, w2b, sw, target = call(
        build, [shape((2 * C, 36 * C))] * 4 + [shape((C, X), f32), shape((BZ, BY, X), f32)]
    )(None, *taps, speed_weight.reshape(1, C), labels)

    ft, me, mo = call(prepare, [shape((BZ, BY, C, X)), shape((9, C, X)), shape((9, C, X))])(
        at, features, sign_map
    )
    ro = odd(mo, "gy")
    re = even(me, "gy")
    fy, sy, ma, mb = call(
        extend,
        [shape((BZ, 12, C, X)), shape((BZ, 16, X), f32), shape((27, C, X)), shape((27, C, X))],
    )(at, ft, sign_map, re, ro)
    rb = odd(mb, "gz")
    ra = even(ma, "gz")

    fx, hx, slope1, slope2, top, fe, fo, own, g0 = call(
        lambda *refs: forward(nz, ny, *refs),
        [
            shape((6, 10, 3, C, X)),
            shape((6, 10, 3, C, X)),
            shape((6, 10, C, X), f32),
            shape((BZ, BY, C, X), f32),
            shape((BZ, BY, C, X), f32),
            shape((28, 8, X), SENT),
            shape((28, 8, X), SENT),
            shape((3, BZ, BY, X), f32),
            shape((8, 16, X), f32),
        ],
        [pltpu.VMEM((10, 16, X), f32), pltpu.VMEM((8, 12, 3, C, X), bf16)],
    )(at, fy, sy, ra, rb, target, w1, w2, sw)

    go = odd(fo, "gy")
    ge = even(fe, "gy")
    fa, fs, s2y = call(
        widen, [shape((84, 8, X), SENT), shape((48, 8, X), SENT), shape((BZ, 12, C, X))]
    )(at, fe, slope2, ge, go)
    ha = even(fa, "gz")
    hb = odd(call(relay, shape((63, 8, X), SENT))(at, fa, ha), "gz")
    hb, fs = lax.optimization_barrier((hb, fs))
    hs = odd(fs, "gz")
    hc = even(hb[:36], "gz")

    plane = (24, 24, X)
    dpre = call(
        lambda *refs: march(nz, ny, *refs),
        shape((8, 16, X), f32),
        [
            pltpu.VMEM(plane, f32),
            pltpu.VMEM(plane, f32),
            pltpu.VMEM((3,) + plane, f32),
            pltpu.VMEM((3,) + plane, f32),
            pltpu.VMEM((3,) + plane, f32),
            pltpu.VMEM((3,) + plane, f32),
            pltpu.VMEM((3,) + plane, f32),
            pltpu.VMEM((3,) + plane, f32),
            pltpu.VMEM(plane, f32),
            pltpu.VMEM((2,) + plane, f32),
        ],
    )(at, own, fa, ha, hb, hc, g0)

    d_features, grad = call(
        backward,
        [shape((C, BZ, BY, X)), shape((2, 2 * C, 256), f32)],
        [pltpu.VMEM((8, 12, 3, C, X), bf16), pltpu.VMEM((6, 10, 3, C, X), bf16)],
    )(at, dpre, slope2, s2y, ha, hs, sw, hx, fx, slope1, top, w1b, w2b)

    a, b = total_of(grad, iz)
    tap_major = shape((27, C, C), f32)
    first, second, speed = call(finish, [tap_major, tap_major, shape((1, C), f32)])(None, a, b)
    first, second = (
        g.reshape(3, 3, 3, C, C).transpose(3, 4, 0, 1, 2) for g in (first, second)
    )
    return d_features, first, second, speed.reshape(C)


def solution(mesh):
    in_specs = (P(None, "gz", "gy", None), P("gz", "gy", None), P("gz", "gy", None), P(), P(), P())
    out_specs = (P(None, "gz", "gy", None), P(), P(), P())

    return jax.shard_map(
        on_device, mesh=mesh, in_specs=in_specs, out_specs=out_specs, check_vma=False
    )
```

```python
import jax
import jax.numpy as jnp
from jax import lax
from jax.experimental import pallas as pl
from jax.experimental.pallas import tpu as pltpu
from jax.sharding import PartitionSpec as P


C = 16
BZ = 4
BY = 8
X = 128
TAPS = 27 * C
A = 0.25
FLOOR = 0.1
SENT = jnp.bfloat16
f32 = jnp.float32
bf16 = jnp.bfloat16


def sides(v):
    axis = v.ndim - 1
    lane = lax.broadcasted_iota(jnp.int32, v.shape, axis)
    low = jnp.where(lane == 0, 0.0, pltpu.roll(v, 1, axis))
    up = jnp.where(lane == X - 1, 0.0, pltpu.roll(v, X - 1, axis))
    return low, up


def put_taps(ref, index, v):
    low, up = sides(v)
    ref[index, :, 0] = low.astype(bf16)
    ref[index, :, 1] = v.astype(bf16)
    ref[index, :, 2] = up.astype(bf16)


def two_rows(weight, taps_ref, z, y):
    patch = taps_ref[pl.ds(z, 3), y : y + 4].reshape(4 * 9 * C, X)
    out = jnp.dot(weight, patch, preferred_element_type=f32)
    return out[:C], out[C:]


def inside(start, shape, limit):
    row = start + lax.broadcasted_iota(jnp.int32, shape, 0)
    return (row >= 0) & (row < limit)


def build(c1_ref, c2_ref, sp_ref, lab_ref, w1_ref, w2_ref, w1b_ref, w2b_ref, sw_ref, labf_ref):
    sw_ref[...] = jnp.transpose(jnp.broadcast_to(sp_ref[...], (X, C)))
    labf_ref[...] = lab_ref[...].astype(f32)
    zero = jnp.zeros((C, C), f32)
    for src, fwd, adj in ((c1_ref, w1_ref, w1b_ref), (c2_ref, w2_ref, w2b_ref)):
        for j in range(2):
            one, two = [], []
            for a in range(3):
                for b in range(4):
                    for c in range(3):
                        tap = (a * 3 + b - j) * 3 + c
                        ok = 0 <= b - j < 3
                        one.append(src[tap].astype(f32) if ok else zero)
                        two.append(src[26 - tap].astype(f32).T if ok else zero)
            fwd[C * j : C * j + C] = jnp.concatenate(one, axis=1).astype(bf16)
            adj[C * j : C * j + C] = jnp.concatenate(two, axis=1).astype(bf16)


def prepare(at, f_ref, s_ref, ft_ref, me_ref, mo_ref):
    py = at[3]
    row = lax.broadcasted_iota(jnp.int32, (BY, X), 0)
    for z in range(BZ):
        ft_ref[z] = jnp.transpose(f_ref[:, z].astype(f32), (1, 0, 2)).astype(bf16)
    for ref, start, high in ((me_ref, 6 - 6 * py, py == 0), (mo_ref, 6 * py, py == 1)):
        for z in range(BZ):
            ref[2 * z : 2 * z + 2] = ft_ref[z, pl.ds(start, 2)]
        parts = []
        for z in range(BZ):
            own = s_ref[z].astype(f32)
            parts.append(jnp.where(high, pltpu.roll(own, 4, 0), own))
        halves = [jnp.where(row < 4, parts[i], pltpu.roll(parts[i + 1], 4, 0)) for i in (0, 2)]
        ref[2 * BZ] = jnp.concatenate(halves, axis=0).astype(bf16)


def extend(at, ft_ref, s_ref, re_ref, ro_ref, fy_ref, sy_ref, ma_ref, mb_ref):
    pz, py = at[2], at[3]
    row = lax.broadcasted_iota(jnp.int32, (BY, X), 0)
    te = re_ref[2 * BZ].astype(f32)
    to = ro_ref[2 * BZ].astype(f32)
    before = jnp.where(py == 0, to, te)
    after = jnp.where(py == 0, te, to)
    for z in range(BZ):
        fy_ref[z, 2 : 2 + BY] = ft_ref[z]
        fy_ref[z, pl.ds(10 - 10 * py, 2)] = re_ref[2 * z : 2 * z + 2]
        fy_ref[z, pl.ds(10 * py, 2)] = ro_ref[2 * z : 2 * z + 2]
        half, low = (z // 2) * 8, (z % 2) * 4
        own = pltpu.roll(s_ref[z].astype(f32), 4, 0)
        b = before[half : half + 8]
        a = after[half : half + 8]
        b = pltpu.roll(b, 4, 0) if low else b
        a = a if low else pltpu.roll(a, 4, 0)
        sy_ref[z] = jnp.concatenate([jnp.where(row < 4, b, own), jnp.where(row < 4, own, a)], axis=0)
    for ref, start, sign in ((ma_ref, 2 - 2 * pz, 1 - pz), (mb_ref, 2 * pz, pz)):
        for k in range(2):
            ref[12 * k : 12 * k + 12] = fy_ref[start + k]
        for k in range(3):
            ref[24 + k] = sy_ref[sign + k].astype(bf16)


def forward(nz, ny, at, fy_ref, sy_ref, ma_ref, mb_ref, lab_ref, w1_ref, w2_ref, sw_ref,
            fc_ref, hx_ref, slope1_ref, slope2_ref, top_ref, me_ref, mo_ref, own_ref, g0_ref, p_ref, fx_ref):
    iz, iy, pz, py = at[0], at[1], at[2], at[3]
    for k in range(BZ):
        put_taps(fx_ref, 2 + k, fy_ref[k].astype(f32))
    for k in range(2):
        put_taps(fx_ref, 6 - 6 * pz + k, ma_ref[12 * k : 12 * k + 12].astype(f32))
        put_taps(fx_ref, 6 * pz + k, mb_ref[12 * k : 12 * k + 12].astype(f32))
    fc_ref[...] = fx_ref[1:7, 1:11]
    w1 = w1_ref[...]
    w2 = w2_ref[...]

    def first(z, carry):
        zg = iz * BZ - 1 + z
        zin = (zg >= 0) & (zg < nz)
        for y in range(0, BY + 2, 2):
            acts = two_rows(w1, fx_ref, z, y)
            hid = []
            for j, act in enumerate(acts):
                yg = iy * BY - 1 + y + j
                keep = jnp.where(zin & (yg >= 0) & (yg < ny), 1.0, 0.0)
                sig = jax.nn.sigmoid(act)
                slope1_ref[z, y + j] = sig * (1.0 + act * (1.0 - sig)) * keep
                hid.append((act * sig * keep)[None])
            hid = jnp.concatenate(hid, axis=0)
            low, up = sides(hid)
            hx_ref[z, y : y + 2, 0] = low.astype(bf16)
            hx_ref[z, y : y + 2, 1] = hid.astype(bf16)
            hx_ref[z, y : y + 2, 2] = up.astype(bf16)
        return carry

    lax.fori_loop(0, BZ + 2, first, 0, unroll=2)
    sw = sw_ref[...]

    def second(z, carry):
        rows = []
        for y in range(0, BY, 2):
            for j, act in enumerate(two_rows(w2, hx_ref, z, y)):
                sig = jax.nn.sigmoid(act)
                top = act * sig
                top_ref[z, y + j] = top
                slope2_ref[z, y + j] = sig * (1.0 + act * (1.0 - sig))
                rows.append(jnp.sum(top * sw, axis=0, keepdims=True))
        own_ref[0, z] = jnp.tanh(jnp.concatenate(rows, axis=0))
        return carry

    lax.fori_loop(0, BZ, second, 0, unroll=2)

    for k in range(BZ):
        p_ref[3 + k] = sy_ref[k]
    for k in range(3):
        p_ref[7 - 7 * pz + k] = ma_ref[24 + k].astype(f32)
        p_ref[7 * pz + k] = mb_ref[24 + k].astype(f32)
    rows_in = inside(iy * BY - 4, (16, X), ny)
    for k in range(10):
        zg = iz * BZ - 3 + k
        p_ref[k] = jnp.where(rows_in & (zg >= 0) & (zg < nz), 2.0 * p_ref[k] - 1.0, 0.0)
    for k in range(8):
        centre, uz, lz = p_ref[k + 1], p_ref[k + 2], p_ref[k]
        ly, uy = pltpu.roll(centre, 1, 0), pltpu.roll(centre, 15, 0)
        lx, ux = sides(centre)
        dz, dy, dx = (uz - lz) * 0.5, (uy - ly) * 0.5, (ux - lx) * 0.5
        g = jnp.sqrt(dz * dz + dy * dy + dx * dx + FLOOR)
        g0_ref[k] = g
        if 2 <= k < 6:
            lap = uz + lz + uy + ly + ux + lx - 6.0 * centre
            base = pltpu.roll(centre + (A * 0.5) * lap, 12, 0)[:8]
            own_ref[1, k - 2] = base + A * own_ref[0, k - 2] * pltpu.roll(g, 12, 0)[:8]
    for z in range(BZ):
        own_ref[2, z] = lab_ref[z]
    for ref, start in ((me_ref, 6 - 6 * py), (mo_ref, 6 * py)):
        ref[:12] = own_ref[...].reshape(12, BY, X).astype(SENT)
        for z in range(BZ):
            ref[12 + 4 * z : 16 + 4 * z] = slope2_ref[z, pl.ds(start, 2)].reshape(4, 8, X).astype(SENT)


def widen(at, me_ref, slope2_ref, re_ref, ro_ref, ma_ref, mb_ref, s2y_ref):
    pz, py = at[2], at[3]
    ma_ref[12:24] = me_ref[:12]
    ma_ref[pl.ds(24 - 24 * py, 12)] = re_ref[:12]
    ma_ref[pl.ds(24 * py, 12)] = ro_ref[:12]
    for z in range(BZ):
        s2y_ref[z, 2 : 2 + BY] = slope2_ref[z].astype(bf16)
        for ref, start in ((re_ref, 10 - 10 * py), (ro_ref, 10 * py)):
            rows = ref[12 + 4 * z : 16 + 4 * z].astype(f32).reshape(2, C, X)
            s2y_ref[z, pl.ds(start, 2)] = rows.astype(bf16)
    for k in range(2):
        rows = s2y_ref[2 - 2 * pz + k].astype(f32).reshape(24, 8, X)
        ma_ref[36 + 24 * k : 60 + 24 * k] = rows.astype(SENT)
        rows = s2y_ref[2 * pz + k].astype(f32).reshape(24, 8, X)
        mb_ref[24 * k : 24 + 24 * k] = rows.astype(SENT)


def relay(at, ma_ref, ra_ref, mb_ref):
    pz = at[2]
    mb_ref[:36] = ma_ref[:36]
    for i in range(3):
        mb_ref[36 + 9 * i : 44 + 9 * i] = ra_ref[12 * i : 12 * i + 8]
        mb_ref[44 + 9 * i] = ra_ref[12 * i + 8 + 3 * pz]


def march(nz, ny, at, own_ref, ye_ref, mate_ref, far_ref, far2_ref, g0_ref, dpre_ref,
          sp, lab, ph, w_s, dz_s, dy_s, dx_s, ag_s, ds, dd):
    iz, iy, pz = at[0], at[1], at[2]
    base = 4 * pz

    def place(start, block):
        for k in range(BZ):
            for ref, f in ((sp, 0), (ph, 1), (lab, 2)):
                plane = jnp.concatenate([block(i, f, k).astype(f32) for i in range(3)], axis=0)
                if f == 1:
                    ph[0, start + k] = plane
                else:
                    ref[start + k] = plane

    def piece(ref, first):
        return lambda i, f, k: ref[first + 12 * i + 4 * f + k]

    def mine(i, f, k):
        return own_ref[f, k] if i == 1 else ye_ref[12 * i + 4 * f + k]

    place(8 + 4 * pz, mine)
    place(12 - 4 * pz, piece(mate_ref, 0))
    place(16 * pz + 4 - 4 * pz, piece(far_ref, 0))
    place(16 - 16 * pz + 4 * pz, piece(far2_ref, 0))

    def beyond(i, f, k):
        return far_ref[44 + 9 * i if f == 2 else 36 + 9 * i + 4 * f + k]

    place(16 * pz + 4 * pz, beyond)

    dd[0, 0] = jnp.zeros((24, X), f32)
    rows_in = inside(iy * BY - 8, (24, X), ny)
    first_plane = (iz - pz) * BZ - 8

    def within(z):
        zg = first_plane + z
        return rows_in & (zg >= 0) & (zg < nz)

    for t in (1, 2, 3):

        def step(i, carry, t=t):
            z = base + i
            centre, uz, lz = ph[t - 1, z], ph[t - 1, z + 1], ph[t - 1, z - 1]
            ly, uy = pltpu.roll(centre, 1, 0), pltpu.roll(centre, 23, 0)
            lx, ux = sides(centre)
            dz, dy, dx = (uz - lz) * 0.5, (uy - ly) * 0.5, (ux - lx) * 0.5
            g = jnp.sqrt(dz * dz + dy * dy + dx * dx + FLOOR)
            lap = uz + lz + uy + ly + ux + lx - 6.0 * centre
            speed = sp[z]
            ag = A * g
            new = jnp.where(within(z), centre + speed * ag + (A * 0.5) * lap, 0.0)
            w_s[t - 1, z] = (A * 0.5) * speed / g
            dz_s[t - 1, z] = dz
            dy_s[t - 1, z] = dy
            dx_s[t - 1, z] = dx
            ag_s[t - 1, z] = ag
            if t < 3:
                ph[t, z] = new
            else:
                dd[0, z] = jnp.where(within(z), jax.nn.sigmoid(new) - lab[z], 0.0)
            return carry

        lax.fori_loop(t, 20 - t, step, 0, unroll=2)

    for n, t in enumerate((3, 2, 1)):
        src, dst = n % 2, (n + 1) % 2

        def back(i, carry, t=t, n=n, src=src, dst=dst):
            l1, a1, a2 = carry
            z = base + i
            d = dd[src, z]
            add = ag_s[t - 1, z] * d
            ds[z] = add if n == 0 else ds[z] + add
            w = w_s[t - 1, z] * d
            e = (A * 0.5) * d
            qz, qy, qx = w * dz_s[t - 1, z], w * dy_s[t - 1, z], w * dx_s[t - 1, z]
            local = (1.0 - 3.0 * A) * d
            local = local + pltpu.roll(e + qy, 1, 0) + pltpu.roll(e - qy, 23, 0)
            local = local + sides(e + qx)[0] + sides(e - qx)[1]
            dd[dst, z - 1] = jnp.where(within(z - 1), l1 + a2 + (e - qz), 0.0)
            return local, e + qz, a1

        zero = dd[0, 0]
        lax.fori_loop(3 + n, 17 - n, back, (zero, zero, zero), unroll=2)

    for k in range(8):
        z = base + 6 + k
        speed = sp[z]
        left = 1.0 - speed * speed
        one = pltpu.roll(ds[z] * left, 20, 0)[:16]
        two = pltpu.roll(dd[1, z] * left, 20, 0)[:16]
        dpre_ref[k] = one + A * two * g0_ref[k]


def backward(at, dpre_ref, slope2_ref, s2y_ref, ra_ref, rb_ref, sw_ref, hx_ref, fx_ref, slope1_ref,
             top_ref, w1_ref, w2_ref, df_ref, grad_ref, dx_ref, ex_ref):
    pz = at[2]
    sw = sw_ref[...]

    def second(z, slope):
        for y in range(BY + 4):
            d = dpre_ref[z, 2 + y : 3 + y, :]
            value = (sw * d * slope(y))[None]
            low, up = sides(value)
            dx_ref[z, y : y + 1, 0] = low.astype(bf16)
            dx_ref[z, y : y + 1, 1] = value.astype(bf16)
            dx_ref[z, y : y + 1, 2] = up.astype(bf16)

    for k in range(BZ):
        def own(y, k=k):
            if 2 <= y < 2 + BY:
                return slope2_ref[k, y - 2]
            return s2y_ref[k, y].astype(f32)

        second(2 + k, own)
    for k in range(2):
        for ref, first, z in ((ra_ref, 36, 6 - 6 * pz), (rb_ref, 0, 6 * pz)):
            def far(y, ref=ref, first=first + 24 * k):
                return ref[first + 2 * y : first + 2 * y + 2].astype(f32).reshape(C, X)

            second(z + k, far)

    w2 = w2_ref[...]
    w1 = w1_ref[...]

    def hidden(z, carry):
        for y in range(0, BY + 2, 2):
            both = two_rows(w2, dx_ref, z, y)
            d = jnp.concatenate([(v * slope1_ref[z, y + j])[None] for j, v in enumerate(both)], axis=0)
            low, up = sides(d)
            ex_ref[z, y : y + 2, 0] = low.astype(bf16)
            ex_ref[z, y : y + 2, 1] = d.astype(bf16)
            ex_ref[z, y : y + 2, 2] = up.astype(bf16)
        return carry

    lax.fori_loop(0, BZ + 2, hidden, 0, unroll=2)

    def features(z, carry):
        rows = []
        for y in range(0, BY, 2):
            a, b = two_rows(w1, ex_ref, z, y)
            rows += [a[None], b[None]]
        plane = jnp.concatenate(rows, axis=0)
        df_ref[:, z] = jnp.transpose(plane, (1, 0, 2)).astype(bf16)
        return carry

    lax.fori_loop(0, BZ, features, 0, unroll=2)

    nt = (((1,), (1,)), ((), ()))

    def weights(z, carry):
        g1, g2, gs = carry
        d2 = jnp.concatenate([dx_ref[z + 2, y + 2, 1] for y in range(BY)], axis=1)
        d1 = jnp.concatenate([ex_ref[z + 1, y + 1, 1] for y in range(BY)], axis=1)
        p2 = [hx_ref[pl.ds(z, 3), y : y + 3].reshape(TAPS, X) for y in range(BY)]
        p1 = [fx_ref[pl.ds(z, 3), y : y + 3].reshape(TAPS, X) for y in range(BY)]
        g2 = g2 + lax.dot_general(d2, jnp.concatenate(p2, axis=1), nt, preferred_element_type=f32)
        g1 = g1 + lax.dot_general(d1, jnp.concatenate(p1, axis=1), nt, preferred_element_type=f32)
        for y in range(BY):
            gs = gs + dpre_ref[z + 2, 4 + y : 5 + y, :] * top_ref[z, y]
        return g1, g2, gs

    zero = jnp.zeros((C, TAPS), f32)
    g1, g2, gs = lax.fori_loop(0, BZ, weights, (zero, zero, jnp.zeros((C, X), f32)))
    grad_ref[...] = jnp.zeros_like(grad_ref)
    for i, g in enumerate((g1, g2)):
        for k in range(3):
            grad_ref[i, C * k : C * k + C] = g[:, X * k : X * k + X]
        grad_ref[i, 48:, :48] = g[:8, 3 * X :]
        grad_ref[i, 48:, 64:112] = g[8:, 3 * X :]
    grad_ref[0, 48:49, 48:64] = jnp.sum(jnp.transpose(gs), axis=0, keepdims=True)


def finish(a_ref, b_ref, first_ref, second_ref, speed_ref):
    a, b = a_ref[...], b_ref[...]
    total = jnp.sum(a * a) + jnp.sum(b * b)
    count = 54.0 * C * C + C
    factor = 1.0 / jnp.maximum(jnp.sqrt(jnp.full((1, 1), total)) / jnp.sqrt(f32(count)), 1.0)
    a, b = a * factor, b * factor
    for out, g in ((first_ref, a), (second_ref, b)):
        for t in range(27):
            row, lane = C * (t // 8), C * (t % 8)
            if t < 24:
                out[t] = g[row : row + C, lane : lane + C]
            else:
                out[t, :8] = g[48:, lane : lane + C]
                out[t, 8:] = g[48:, 64 + lane : 64 + lane + C]
    speed_ref[...] = a[48:49, 48:64]


def call(kernel, outs, scratch=(), flops=0):
    smem = pl.BlockSpec(memory_space=pltpu.SMEM)
    vmem = pl.BlockSpec(memory_space=pltpu.VMEM)

    def run(at, *args):
        args = ((at,) if at is not None else ()) + args
        specs = [smem if (i == 0 and at is not None) else vmem for i in range(len(args))]
        many = isinstance(outs, (list, tuple))
        size = sum(a.size * a.dtype.itemsize for a in args)
        return pl.pallas_call(
            kernel,
            out_shape=outs,
            in_specs=specs,
            out_specs=[vmem] * len(outs) if many else vmem,
            scratch_shapes=list(scratch),
            cost_estimate=pl.CostEstimate(flops=flops, bytes_accessed=size, transcendentals=0),
            compiler_params=pltpu.CompilerParams(vmem_limit_bytes=16 * 1024 * 1024),
        )(*args)

    return run


def shape(dims, dtype=bf16):
    return jax.ShapeDtypeStruct(dims, dtype)


def even(value, axis):
    n = lax.axis_size(axis)
    return lax.ppermute(value, axis, [(i, i ^ 1) for i in range(n)])


def odd(value, axis):
    n = lax.axis_size(axis)
    pairs = [(i, i + 1) for i in range(1, n - 1, 2)]
    return lax.ppermute(value, axis, pairs + [(j, i) for i, j in pairs])


def groups(n, unit):
    size = max(1, min(4, n // unit))
    firsts = [i for i in range(n) if (i // unit) % size == 0]
    return [[i + unit * k for k in range(size)] for i in firsts]


def total_of(grad, iz):
    core = iz % 2
    keep = lax.dynamic_index_in_dim(grad, core, 0, keepdims=False)
    give = lax.dynamic_index_in_dim(grad, 1 - core, 0, keepdims=False)
    part = keep + even(give, "gz")
    for axis, unit in (("gy", 1), ("gy", 4), ("gz", 8), ("gz", 2)):
        sets = groups(lax.axis_size(axis), unit)
        if len(sets[0]) > 1:
            sent = part.astype(bf16) if unit == 2 else part
            copies = jnp.broadcast_to(sent[None], (len(sets[0]),) + part.shape)
            got = lax.all_to_all(copies, axis, 0, 0, axis_index_groups=sets)
            part = jnp.sum(got.astype(f32), axis=0)
    other = even(part, "gz")
    return jnp.where(core == 0, part, other), jnp.where(core == 0, other, part)


def on_device(features, labels, sign_map, conv_first, conv_second, speed_weight):
    nz, ny = BZ * lax.axis_size("gz"), BY * lax.axis_size("gy")
    iz, iy = lax.axis_index("gz"), lax.axis_index("gy")
    pz, py = iz % 2, iy % 2
    at = jnp.stack([iz, iy, pz, py]).astype(jnp.int32)
    taps = [w.transpose(2, 3, 4, 0, 1).reshape(27, C, C) for w in (conv_first, conv_second)]
    w1, w2, w1b, w2b, sw, target = call(
        build, [shape((2 * C, 36 * C))] * 4 + [shape((C, X), f32), shape((BZ, BY, X), f32)]
    )(None, *taps, speed_weight.reshape(1, C), labels)

    ft, me, mo = call(prepare, [shape((BZ, BY, C, X)), shape((9, C, X)), shape((9, C, X))])(
        at, features, sign_map
    )
    ro = odd(mo, "gy")
    re = even(me, "gy")
    fy, sy, ma, mb = call(
        extend,
        [shape((BZ, 12, C, X)), shape((BZ, 16, X), f32), shape((27, C, X)), shape((27, C, X))],
    )(at, ft, sign_map, re, ro)
    rb = odd(mb, "gz")
    ra = even(ma, "gz")

    fx, hx, slope1, slope2, top, fe, fo, own, g0 = call(
        lambda *refs: forward(nz, ny, *refs),
        [
            shape((6, 10, 3, C, X)),
            shape((6, 10, 3, C, X)),
            shape((6, 10, C, X), f32),
            shape((BZ, BY, C, X), f32),
            shape((BZ, BY, C, X), f32),
            shape((28, 8, X), SENT),
            shape((28, 8, X), SENT),
            shape((3, BZ, BY, X), f32),
            shape((8, 16, X), f32),
        ],
        [pltpu.VMEM((10, 16, X), f32), pltpu.VMEM((8, 12, 3, C, X), bf16)],
    )(at, fy, sy, ra, rb, target, w1, w2, sw)

    go = odd(fo, "gy")
    ge = even(fe, "gy")
    fa, fs, s2y = call(
        widen, [shape((84, 8, X), SENT), shape((48, 8, X), SENT), shape((BZ, 12, C, X))]
    )(at, fe, slope2, ge, go)
    ha = even(fa, "gz")
    hb = odd(call(relay, shape((63, 8, X), SENT))(at, fa, ha), "gz")
    hb, fs = lax.optimization_barrier((hb, fs))
    hs = odd(fs, "gz")
    hc = even(hb, "gz")

    plane = (24, 24, X)
    dpre = call(
        lambda *refs: march(nz, ny, *refs),
        shape((8, 16, X), f32),
        [
            pltpu.VMEM(plane, f32),
            pltpu.VMEM(plane, f32),
            pltpu.VMEM((3,) + plane, f32),
            pltpu.VMEM((3,) + plane, f32),
            pltpu.VMEM((3,) + plane, f32),
            pltpu.VMEM((3,) + plane, f32),
            pltpu.VMEM((3,) + plane, f32),
            pltpu.VMEM((3,) + plane, f32),
            pltpu.VMEM(plane, f32),
            pltpu.VMEM((2,) + plane, f32),
        ],
    )(at, own, fa, ha, hb, hc, g0)

    d_features, grad = call(
        backward,
        [shape((C, BZ, BY, X)), shape((2, 56, X), f32)],
        [pltpu.VMEM((8, 12, 3, C, X), bf16), pltpu.VMEM((6, 10, 3, C, X), bf16)],
    )(at, dpre, slope2, s2y, ha, hs, sw, hx, fx, slope1, top, w1b, w2b)

    a, b = total_of(grad, iz)
    tap_major = shape((27, C, C), f32)
    first, second, speed = call(finish, [tap_major, tap_major, shape((1, C), f32)])(None, a, b)
    first, second = (
        g.reshape(3, 3, 3, C, C).transpose(3, 4, 0, 1, 2) for g in (first, second)
    )
    return d_features, first, second, speed.reshape(C)


def solution(mesh):
    in_specs = (P(None, "gz", "gy", None), P("gz", "gy", None), P("gz", "gy", None), P(), P(), P())
    out_specs = (P(None, "gz", "gy", None), P(), P(), P())

    return jax.shard_map(
        on_device, mesh=mesh, in_specs=in_specs, out_specs=out_specs, check_vma=False
    )
```

```python
import jax
import jax.numpy as jnp
from jax import lax
from jax.experimental import pallas as pl
from jax.experimental.pallas import tpu as pltpu
from jax.sharding import PartitionSpec as P

C = 16
BZ = 4
BY = 8
X = 128
TAPS = 27 * C
A = 0.25
FLOOR = 0.1
SENT = jnp.bfloat16
f32 = jnp.float32
bf16 = jnp.bfloat16


def sides(v):
    axis = v.ndim - 1
    lane = lax.broadcasted_iota(jnp.int32, v.shape, axis)
    low = jnp.where(lane == 0, 0.0, pltpu.roll(v, 1, axis))
    up = jnp.where(lane == X - 1, 0.0, pltpu.roll(v, X - 1, axis))
    return low, up


def put_taps(ref, index, v):
    low, up = sides(v)
    ref[index, :, 0] = low.astype(bf16)
    ref[index, :, 1] = v.astype(bf16)
    ref[index, :, 2] = up.astype(bf16)


def two_rows(weight, taps_ref, z, y):
    patch = taps_ref[pl.ds(z, 3), y : y + 4].reshape(4 * 9 * C, X)
    out = jnp.dot(weight, patch, preferred_element_type=f32)
    return out[:C], out[C:]


def inside(start, shape, limit):
    row = start + lax.broadcasted_iota(jnp.int32, shape, 0)
    return (row >= 0) & (row < limit)


def build(c1_ref, c2_ref, sp_ref, lab_ref, w1_ref, w2_ref, w1b_ref, w2b_ref, sw_ref, labf_ref):
    sw_ref[...] = jnp.transpose(jnp.broadcast_to(sp_ref[...], (X, C)))
    labf_ref[...] = lab_ref[...].astype(f32)
    zero = jnp.zeros((C, C), f32)
    for src, fwd, adj in ((c1_ref, w1_ref, w1b_ref), (c2_ref, w2_ref, w2b_ref)):
        for j in range(2):
            one, two = [], []
            for a in range(3):
                for b in range(4):
                    for c in range(3):
                        tap = (a * 3 + b - j) * 3 + c
                        ok = 0 <= b - j < 3
                        one.append(src[tap].astype(f32) if ok else zero)
                        two.append(src[26 - tap].astype(f32).T if ok else zero)
            fwd[C * j : C * j + C] = jnp.concatenate(one, axis=1).astype(bf16)
            adj[C * j : C * j + C] = jnp.concatenate(two, axis=1).astype(bf16)


def prepare(at, f_ref, s_ref, ft_ref, me_ref, mo_ref):
    py = at[3]
    row = lax.broadcasted_iota(jnp.int32, (BY, X), 0)
    for z in range(BZ):
        ft_ref[z] = jnp.transpose(f_ref[:, z].astype(f32), (1, 0, 2)).astype(bf16)
    for ref, start, high in ((me_ref, 6 - 6 * py, py == 0), (mo_ref, 6 * py, py == 1)):
        for z in range(BZ):
            ref[2 * z : 2 * z + 2] = ft_ref[z, pl.ds(start, 2)]
        parts = []
        for z in range(BZ):
            own = s_ref[z].astype(f32)
            parts.append(jnp.where(high, pltpu.roll(own, 4, 0), own))
        halves = [jnp.where(row < 4, parts[i], pltpu.roll(parts[i + 1], 4, 0)) for i in (0, 2)]
        ref[2 * BZ] = jnp.concatenate(halves, axis=0).astype(bf16)


def extend(at, ft_ref, s_ref, re_ref, ro_ref, fy_ref, sy_ref, ma_ref, mb_ref):
    pz, py = at[2], at[3]
    row = lax.broadcasted_iota(jnp.int32, (BY, X), 0)
    te = re_ref[2 * BZ].astype(f32)
    to = ro_ref[2 * BZ].astype(f32)
    before = jnp.where(py == 0, to, te)
    after = jnp.where(py == 0, te, to)
    for z in range(BZ):
        fy_ref[z, 2 : 2 + BY] = ft_ref[z]
        fy_ref[z, pl.ds(10 - 10 * py, 2)] = re_ref[2 * z : 2 * z + 2]
        fy_ref[z, pl.ds(10 * py, 2)] = ro_ref[2 * z : 2 * z + 2]
        half, low = (z // 2) * 8, (z % 2) * 4
        own = pltpu.roll(s_ref[z].astype(f32), 4, 0)
        b = before[half : half + 8]
        a = after[half : half + 8]
        b = pltpu.roll(b, 4, 0) if low else b
        a = a if low else pltpu.roll(a, 4, 0)
        sy_ref[z] = jnp.concatenate([jnp.where(row < 4, b, own), jnp.where(row < 4, own, a)], axis=0)
    for ref, start, sign in ((ma_ref, 2 - 2 * pz, 1 - pz), (mb_ref, 2 * pz, pz)):
        for k in range(2):
            ref[12 * k : 12 * k + 12] = fy_ref[start + k]
        for k in range(3):
            ref[24 + k] = sy_ref[sign + k].astype(bf16)


def forward(nz, ny, at, fy_ref, sy_ref, ma_ref, mb_ref, lab_ref, w1_ref, w2_ref, sw_ref,
            fc_ref, hx_ref, slope1_ref, slope2_ref, top_ref, me_ref, mo_ref, own_ref, g0_ref, p_ref, fx_ref):
    iz, iy, pz, py = at[0], at[1], at[2], at[3]
    for k in range(BZ):
        put_taps(fx_ref, 2 + k, fy_ref[k].astype(f32))
    for k in range(2):
        put_taps(fx_ref, 6 - 6 * pz + k, ma_ref[12 * k : 12 * k + 12].astype(f32))
        put_taps(fx_ref, 6 * pz + k, mb_ref[12 * k : 12 * k + 12].astype(f32))
    fc_ref[...] = fx_ref[1:7, 1:11]
    w1 = w1_ref[...]
    w2 = w2_ref[...]

    def first(z, carry):
        zg = iz * BZ - 1 + z
        zin = (zg >= 0) & (zg < nz)
        for y in range(0, BY + 2, 2):
            acts = two_rows(w1, fx_ref, z, y)
            hid = []
            for j, act in enumerate(acts):
                yg = iy * BY - 1 + y + j
                keep = jnp.where(zin & (yg >= 0) & (yg < ny), 1.0, 0.0)
                sig = jax.nn.sigmoid(act)
                slope1_ref[z, y + j] = sig * (1.0 + act * (1.0 - sig)) * keep
                hid.append((act * sig * keep)[None])
            hid = jnp.concatenate(hid, axis=0)
            low, up = sides(hid)
            hx_ref[z, y : y + 2, 0] = low.astype(bf16)
            hx_ref[z, y : y + 2, 1] = hid.astype(bf16)
            hx_ref[z, y : y + 2, 2] = up.astype(bf16)
        return carry

    lax.fori_loop(0, BZ + 2, first, 0, unroll=2)
    sw = sw_ref[...]

    def second(z, carry):
        rows = []
        for y in range(0, BY, 2):
            for j, act in enumerate(two_rows(w2, hx_ref, z, y)):
                sig = jax.nn.sigmoid(act)
                top = act * sig
                top_ref[z, y + j] = top
                slope2_ref[z, y + j] = sig * (1.0 + act * (1.0 - sig))
                rows.append(jnp.sum(top * sw, axis=0, keepdims=True))
        own_ref[0, z] = jnp.tanh(jnp.concatenate(rows, axis=0))
        return carry

    lax.fori_loop(0, BZ, second, 0, unroll=2)

    for k in range(BZ):
        p_ref[3 + k] = sy_ref[k]
    for k in range(3):
        p_ref[7 - 7 * pz + k] = ma_ref[24 + k].astype(f32)
        p_ref[7 * pz + k] = mb_ref[24 + k].astype(f32)
    rows_in = inside(iy * BY - 4, (16, X), ny)
    for k in range(10):
        zg = iz * BZ - 3 + k
        p_ref[k] = jnp.where(rows_in & (zg >= 0) & (zg < nz), 2.0 * p_ref[k] - 1.0, 0.0)
    for k in range(8):
        centre, uz, lz = p_ref[k + 1], p_ref[k + 2], p_ref[k]
        ly, uy = pltpu.roll(centre, 1, 0), pltpu.roll(centre, 15, 0)
        lx, ux = sides(centre)
        dz, dy, dx = (uz - lz) * 0.5, (uy - ly) * 0.5, (ux - lx) * 0.5
        g = jnp.sqrt(dz * dz + dy * dy + dx * dx + FLOOR)
        g0_ref[k] = g
        if 2 <= k < 6:
            lap = uz + lz + uy + ly + ux + lx - 6.0 * centre
            base = pltpu.roll(centre + (A * 0.5) * lap, 12, 0)[:8]
            own_ref[1, k - 2] = base + A * own_ref[0, k - 2] * pltpu.roll(g, 12, 0)[:8]
    for z in range(BZ):
        own_ref[2, z] = lab_ref[z]
    for ref, start in ((me_ref, 6 - 6 * py), (mo_ref, 6 * py)):
        ref[:12] = own_ref[...].reshape(12, BY, X).astype(SENT)
        for z in range(BZ):
            ref[12 + 4 * z : 16 + 4 * z] = slope2_ref[z, pl.ds(start, 2)].reshape(4, 8, X).astype(SENT)


def widen(at, me_ref, slope2_ref, re_ref, ro_ref, ma_ref, mb_ref, s2y_ref):
    pz, py = at[2], at[3]
    ma_ref[12:24] = me_ref[:12]
    ma_ref[pl.ds(24 - 24 * py, 12)] = re_ref[:12]
    ma_ref[pl.ds(24 * py, 12)] = ro_ref[:12]
    for z in range(BZ):
        s2y_ref[z, 2 : 2 + BY] = slope2_ref[z].astype(bf16)
        for ref, start in ((re_ref, 10 - 10 * py), (ro_ref, 10 * py)):
            rows = ref[12 + 4 * z : 16 + 4 * z].astype(f32).reshape(2, C, X)
            s2y_ref[z, pl.ds(start, 2)] = rows.astype(bf16)
    for k in range(2):
        rows = s2y_ref[2 - 2 * pz + k].astype(f32).reshape(24, 8, X)
        ma_ref[36 + 24 * k : 60 + 24 * k] = rows.astype(SENT)
        rows = s2y_ref[2 * pz + k].astype(f32).reshape(24, 8, X)
        mb_ref[24 * k : 24 + 24 * k] = rows.astype(SENT)


def relay(at, ma_ref, ra_ref, mb_ref):
    pz = at[2]
    mb_ref[:36] = ma_ref[:36]
    for i in range(3):
        mb_ref[36 + 9 * i : 44 + 9 * i] = ra_ref[12 * i : 12 * i + 8]
        mb_ref[44 + 9 * i] = ra_ref[12 * i + 8 + 3 * pz]


def march(nz, ny, at, own_ref, ye_ref, mate_ref, far_ref, far2_ref, g0_ref, dpre_ref,
          sp, lab, ph, w_s, dz_s, dy_s, dx_s, ag_s, ds, dd):
    iz, iy, pz, py = at[0], at[1], at[2], at[3]
    base = 4 * pz

    def place(start, block):
        for k in range(BZ):
            for ref, f in ((sp, 0), (ph, 1), (lab, 2)):
                plane = jnp.concatenate([block(i, f, k).astype(f32) for i in range(3)], axis=0)
                if f == 1:
                    ph[0, start + k] = plane
                else:
                    ref[start + k] = plane

    def piece(ref, first):
        return lambda i, f, k: ref[first + 12 * i + 4 * f + k]

    def mine(i, f, k):
        return own_ref[f, k] if i == 1 else ye_ref[12 * i + 4 * f + k]

    place(8 + 4 * pz, mine)
    place(12 - 4 * pz, piece(mate_ref, 0))
    place(16 * pz + 4 - 4 * pz, piece(far_ref, 0))
    place(16 - 16 * pz + 4 * pz, piece(far2_ref, 0))

    def beyond(i, f, k):
        return far_ref[44 + 9 * i if f == 2 else 36 + 9 * i + 4 * f + k]

    place(16 * pz + 4 * pz, beyond)

    dd[0, 0] = jnp.zeros((24, X), f32)
    rows_in = inside(iy * BY - 8, (24, X), ny)
    first_plane = (iz - pz) * BZ - 8

    def within(z):
        zg = first_plane + z
        return rows_in & (zg >= 0) & (zg < nz)

    for t in (1, 2, 3):

        def step(i, carry, t=t):
            z = base + i
            centre, uz, lz = ph[t - 1, z], ph[t - 1, z + 1], ph[t - 1, z - 1]
            ly, uy = pltpu.roll(centre, 1, 0), pltpu.roll(centre, 23, 0)
            lx, ux = sides(centre)
            dz, dy, dx = (uz - lz) * 0.5, (uy - ly) * 0.5, (ux - lx) * 0.5
            square = dz * dz + dy * dy + dx * dx + FLOOR
            root = lax.rsqrt(square)
            lap = uz + lz + uy + ly + ux + lx - 6.0 * centre
            speed = sp[z]
            ag = A * square * root
            new = jnp.where(within(z), centre + speed * ag + (A * 0.5) * lap, 0.0)
            w_s[t - 1, z] = (A * 0.5) * speed * root
            dz_s[t - 1, z] = dz
            dy_s[t - 1, z] = dy
            dx_s[t - 1, z] = dx
            ag_s[t - 1, z] = ag
            if t < 3:
                ph[t, z] = new
            else:
                dd[0, z] = jnp.where(within(z), jax.nn.sigmoid(new) - lab[z], 0.0)
            return carry

        lax.fori_loop(t, 20 - t, step, 0, unroll=2)

    for n, t in enumerate((3, 2, 1)):
        src, dst = n % 2, (n + 1) % 2

        def back(i, carry, t=t, n=n, src=src, dst=dst):
            l1, a1, a2 = carry
            z = base + i
            d = dd[src, z]
            add = ag_s[t - 1, z] * d
            ds[z] = add if n == 0 else ds[z] + add
            w = w_s[t - 1, z] * d
            e = (A * 0.5) * d
            qz, qy, qx = w * dz_s[t - 1, z], w * dy_s[t - 1, z], w * dx_s[t - 1, z]
            local = (1.0 - 3.0 * A) * d
            local = local + pltpu.roll(e + qy, 1, 0) + pltpu.roll(e - qy, 23, 0)
            local = local + sides(e + qx)[0] + sides(e - qx)[1]
            dd[dst, z - 1] = jnp.where(within(z - 1), l1 + a2 + (e - qz), 0.0)
            return local, e + qz, a1

        zero = dd[0, 0]
        lax.fori_loop(3 + n, 17 - n, back, (zero, zero, zero), unroll=2)

    for k in range(8):
        z = base + 6 + k
        speed = sp[z]
        left = 1.0 - speed * speed
        one = pltpu.roll(ds[z] * left, 20, 0)[:16]
        two = pltpu.roll(dd[1, z] * left, 20, 0)[:16]
        dpre_ref[k] = one + A * two * g0_ref[k]


def backward(at, dpre_ref, slope2_ref, s2y_ref, ra_ref, rb_ref, sw_ref, hx_ref, fx_ref, slope1_ref,
             top_ref, w1_ref, w2_ref, df_ref, grad_ref, dx_ref, ex_ref):
    pz = at[2]
    sw = sw_ref[...]

    def second(z, k, slope):
        for y in range(BY + 4):
            d = dpre_ref[z, 2 + y : 3 + y, :]
            value = (sw * d * slope(y))[None]
            low, up = sides(value)
            dx_ref[z, y : y + 1, 0] = low.astype(bf16)
            dx_ref[z, y : y + 1, 1] = value.astype(bf16)
            dx_ref[z, y : y + 1, 2] = up.astype(bf16)

    for k in range(BZ):
        def own(y, k=k):
            if 2 <= y < 2 + BY:
                return slope2_ref[k, y - 2]
            return s2y_ref[k, y].astype(f32)
        second(2 + k, k, own)
    for k in range(2):
        for ref, first, z in ((ra_ref, 36, 6 - 6 * pz), (rb_ref, 0, 6 * pz)):
            def far(y, ref=ref, first=first + 24 * k):
                return ref[first + 2 * y : first + 2 * y + 2].astype(f32).reshape(C, X)
            second(z + k, k, far)

    w2 = w2_ref[...]
    w1 = w1_ref[...]

    def hidden(z, carry):
        for y in range(0, BY + 2, 2):
            both = two_rows(w2, dx_ref, z, y)
            d = jnp.concatenate([(v * slope1_ref[z, y + j])[None] for j, v in enumerate(both)], axis=0)
            low, up = sides(d)
            ex_ref[z, y : y + 2, 0] = low.astype(bf16)
            ex_ref[z, y : y + 2, 1] = d.astype(bf16)
            ex_ref[z, y : y + 2, 2] = up.astype(bf16)
        return carry

    lax.fori_loop(0, BZ + 2, hidden, 0, unroll=2)

    def features(z, carry):
        rows = []
        for y in range(0, BY, 2):
            a, b = two_rows(w1, ex_ref, z, y)
            rows += [a[None], b[None]]
        plane = jnp.concatenate(rows, axis=0)
        df_ref[:, z] = jnp.transpose(plane, (1, 0, 2)).astype(bf16)
        return carry

    lax.fori_loop(0, BZ, features, 0, unroll=2)

    nt = (((1,), (1,)), ((), ()))

    def weights(z, carry):
        g1, g2, gs = carry
        d2 = jnp.concatenate([dx_ref[z + 2, y + 2, 1] for y in range(BY)], axis=1)
        d1 = jnp.concatenate([ex_ref[z + 1, y + 1, 1] for y in range(BY)], axis=1)
        p2 = [hx_ref[pl.ds(z, 3), y : y + 3].reshape(TAPS, X) for y in range(BY)]
        p1 = [fx_ref[pl.ds(z, 3), y : y + 3].reshape(TAPS, X) for y in range(BY)]
        g2 = g2 + lax.dot_general(d2, jnp.concatenate(p2, axis=1), nt, preferred_element_type=f32)
        g1 = g1 + lax.dot_general(d1, jnp.concatenate(p1, axis=1), nt, preferred_element_type=f32)
        for y in range(BY):
            gs = gs + dpre_ref[z + 2, 4 + y : 5 + y, :] * top_ref[z, y]
        return g1, g2, gs

    zero = jnp.zeros((C, TAPS), f32)
    g1, g2, gs = lax.fori_loop(0, BZ, weights, (zero, zero, jnp.zeros((C, X), f32)))
    grad_ref[...] = jnp.zeros_like(grad_ref)
    for i, g in enumerate((g1, g2)):
        for k in range(3):
            grad_ref[i, C * k : C * k + C] = g[:, X * k : X * k + X]
        grad_ref[i, 48:, :48] = g[:8, 3 * X :]
        grad_ref[i, 48:, 64:112] = g[8:, 3 * X :]
    grad_ref[0, 48:49, 48:64] = jnp.sum(jnp.transpose(gs), axis=0, keepdims=True)


def finish(a_ref, b_ref, first_ref, second_ref, speed_ref):
    a, b = a_ref[...], b_ref[...]
    total = jnp.sum(a * a) + jnp.sum(b * b)
    count = 54.0 * C * C + C
    factor = 1.0 / jnp.maximum(jnp.sqrt(jnp.full((1, 1), total)) / jnp.sqrt(f32(count)), 1.0)
    a, b = a * factor, b * factor
    for out, g in ((first_ref, a), (second_ref, b)):
        for t in range(27):
            row, lane = C * (t // 8), C * (t % 8)
            if t < 24:
                out[t] = g[row : row + C, lane : lane + C]
            else:
                out[t, :8] = g[48:, lane : lane + C]
                out[t, 8:] = g[48:, 64 + lane : 64 + lane + C]
    speed_ref[...] = a[48:49, 48:64]


def call(kernel, outs, scratch=(), flops=0):
    smem = pl.BlockSpec(memory_space=pltpu.SMEM)
    vmem = pl.BlockSpec(memory_space=pltpu.VMEM)

    def run(at, *args):
        args = ((at,) if at is not None else ()) + args
        specs = [smem if (i == 0 and at is not None) else vmem for i in range(len(args))]
        many = isinstance(outs, (list, tuple))
        size = sum(a.size * a.dtype.itemsize for a in args)
        return pl.pallas_call(
            kernel,
            out_shape=outs,
            in_specs=specs,
            out_specs=[vmem] * len(outs) if many else vmem,
            scratch_shapes=list(scratch),
            cost_estimate=pl.CostEstimate(flops=flops, bytes_accessed=size, transcendentals=0),
            compiler_params=pltpu.CompilerParams(vmem_limit_bytes=16 * 1024 * 1024),
        )(*args)

    return run


def shape(dims, dtype=bf16):
    return jax.ShapeDtypeStruct(dims, dtype)


def even(value, axis):
    n = lax.axis_size(axis)
    return lax.ppermute(value, axis, [(i, i ^ 1) for i in range(n)])


def odd(value, axis):
    n = lax.axis_size(axis)
    pairs = [(i, i + 1) for i in range(1, n - 1, 2)]
    return lax.ppermute(value, axis, pairs + [(j, i) for i, j in pairs])


def groups(n, unit):
    size = max(1, min(4, n // unit))
    firsts = [i for i in range(n) if (i // unit) % size == 0]
    return [[i + unit * k for k in range(size)] for i in firsts]


def total_of(grad, iz):
    core = iz % 2
    keep = lax.dynamic_index_in_dim(grad, core, 0, keepdims=False)
    give = lax.dynamic_index_in_dim(grad, 1 - core, 0, keepdims=False)
    part = keep + even(give, "gz")
    for axis, unit in (("gy", 1), ("gy", 4), ("gz", 8), ("gz", 2)):
        sets = groups(lax.axis_size(axis), unit)
        if len(sets[0]) > 1:
            copies = jnp.broadcast_to(part[None], (len(sets[0]),) + part.shape)
            part = jnp.sum(lax.all_to_all(copies, axis, 0, 0, axis_index_groups=sets), axis=0)
    other = even(part, "gz")
    return jnp.where(core == 0, part, other), jnp.where(core == 0, other, part)


def on_device(features, labels, sign_map, conv_first, conv_second, speed_weight):
    nz, ny = BZ * lax.axis_size("gz"), BY * lax.axis_size("gy")
    iz, iy = lax.axis_index("gz"), lax.axis_index("gy")
    pz, py = iz % 2, iy % 2
    at = jnp.stack([iz, iy, pz, py]).astype(jnp.int32)
    taps = [w.transpose(2, 3, 4, 0, 1).reshape(27, C, C) for w in (conv_first, conv_second)]
    w1, w2, w1b, w2b, sw, target = call(
        build, [shape((2 * C, 36 * C))] * 4 + [shape((C, X), f32), shape((BZ, BY, X), f32)]
    )(None, *taps, speed_weight.reshape(1, C), labels)

    ft, me, mo = call(prepare, [shape((BZ, BY, C, X)), shape((9, C, X)), shape((9, C, X))])(
        at, features, sign_map
    )
    ro = odd(mo, "gy")
    re = even(me, "gy")
    fy, sy, ma, mb = call(
        extend,
        [shape((BZ, 12, C, X)), shape((BZ, 16, X), f32), shape((27, C, X)), shape((27, C, X))],
    )(at, ft, sign_map, re, ro)
    rb = odd(mb, "gz")
    ra = even(ma, "gz")

    fx, hx, slope1, slope2, top, fe, fo, own, g0 = call(
        lambda *refs: forward(nz, ny, *refs),
        [
            shape((6, 10, 3, C, X)),
            shape((6, 10, 3, C, X)),
            shape((6, 10, C, X), f32),
            shape((BZ, BY, C, X), f32),
            shape((BZ, BY, C, X), f32),
            shape((28, 8, X), SENT),
            shape((28, 8, X), SENT),
            shape((3, BZ, BY, X), f32),
            shape((8, 16, X), f32),
        ],
        [pltpu.VMEM((10, 16, X), f32), pltpu.VMEM((8, 12, 3, C, X), bf16)],
    )(at, fy, sy, ra, rb, target, w1, w2, sw)

    go = odd(fo, "gy")
    ge = even(fe, "gy")
    fa, fs, s2y = call(
        widen, [shape((84, 8, X), SENT), shape((48, 8, X), SENT), shape((BZ, 12, C, X))]
    )(at, fe, slope2, ge, go)
    ha = even(fa, "gz")
    hb = odd(call(relay, shape((63, 8, X), SENT))(at, fa, ha), "gz")
    hb, fs = lax.optimization_barrier((hb, fs))
    hc = even(hb, "gz")
    hs = odd(fs, "gz")

    plane = (24, 24, X)
    dpre = call(
        lambda *refs: march(nz, ny, *refs),
        shape((8, 16, X), f32),
        [
            pltpu.VMEM(plane, f32),
            pltpu.VMEM(plane, f32),
            pltpu.VMEM((3,) + plane, f32),
            pltpu.VMEM((3,) + plane, f32),
            pltpu.VMEM((3,) + plane, f32),
            pltpu.VMEM((3,) + plane, f32),
            pltpu.VMEM((3,) + plane, f32),
            pltpu.VMEM((3,) + plane, f32),
            pltpu.VMEM(plane, f32),
            pltpu.VMEM((2,) + plane, f32),
        ],
    )(at, own, fa, ha, hb, hc, g0)

    d_features, grad = call(
        backward,
        [shape((C, BZ, BY, X)), shape((2, 56, X), f32)],
        [pltpu.VMEM((8, 12, 3, C, X), bf16), pltpu.VMEM((6, 10, 3, C, X), bf16)],
    )(at, dpre, slope2, s2y, ha, hs, sw, hx, fx, slope1, top, w1b, w2b)

    a, b = total_of(grad, iz)
    tap_major = shape((27, C, C), f32)
    first, second, speed = call(finish, [tap_major, tap_major, shape((1, C), f32)])(None, a, b)
    first, second = (
        g.reshape(3, 3, 3, C, C).transpose(3, 4, 0, 1, 2) for g in (first, second)
    )
    return d_features, first, second, speed.reshape(C)


def solution(mesh):
    in_specs = (P(None, "gz", "gy", None), P("gz", "gy", None), P("gz", "gy", None), P(), P(), P())
    out_specs = (P(None, "gz", "gy", None), P(), P(), P())
    return jax.shard_map(
        on_device, mesh=mesh, in_specs=in_specs, out_specs=out_specs, check_vma=False
    )
```

```python
import jax
import jax.numpy as jnp
from jax import lax
from jax.experimental import pallas as pl
from jax.experimental.pallas import tpu as pltpu
from jax.sharding import PartitionSpec as P


C = 16
BZ = 4
BY = 8
X = 128
TAPS = 27 * C
A = 0.25
FLOOR = 0.1
SENT = jnp.bfloat16
f32 = jnp.float32
bf16 = jnp.bfloat16


def sides(v):
    axis = v.ndim - 1
    lane = lax.broadcasted_iota(jnp.int32, v.shape, axis)
    low = jnp.where(lane == 0, 0.0, pltpu.roll(v, 1, axis))
    up = jnp.where(lane == X - 1, 0.0, pltpu.roll(v, X - 1, axis))
    return low, up


def put_taps(ref, index, v):
    low, up = sides(v)
    ref[index, :, 0] = low.astype(bf16)
    ref[index, :, 1] = v.astype(bf16)
    ref[index, :, 2] = up.astype(bf16)


def two_rows(weight, taps_ref, z, y):
    patch = taps_ref[pl.ds(z, 3), y : y + 4].reshape(4 * 9 * C, X)
    out = jnp.dot(weight, patch, preferred_element_type=f32)
    return out[:C], out[C:]


def inside(start, shape, limit):
    row = start + lax.broadcasted_iota(jnp.int32, shape, 0)
    return (row >= 0) & (row < limit)


def build(c1_ref, c2_ref, sp_ref, lab_ref, w1_ref, w2_ref, w1b_ref, w2b_ref, sw_ref, labf_ref):
    sw_ref[...] = jnp.transpose(jnp.broadcast_to(sp_ref[...], (X, C)))
    labf_ref[...] = lab_ref[...].astype(f32)
    zero = jnp.zeros((C, C), f32)
    for src, fwd, adj in ((c1_ref, w1_ref, w1b_ref), (c2_ref, w2_ref, w2b_ref)):
        for j in range(2):
            one, two = [], []
            for a in range(3):
                for b in range(4):
                    for c in range(3):
                        tap = (a * 3 + b - j) * 3 + c
                        ok = 0 <= b - j < 3
                        one.append(src[tap].astype(f32) if ok else zero)
                        two.append(src[26 - tap].astype(f32).T if ok else zero)
            fwd[C * j : C * j + C] = jnp.concatenate(one, axis=1).astype(bf16)
            adj[C * j : C * j + C] = jnp.concatenate(two, axis=1).astype(bf16)


def prepare(at, f_ref, s_ref, ft_ref, me_ref, mo_ref):
    py = at[3]
    row = lax.broadcasted_iota(jnp.int32, (BY, X), 0)
    for z in range(BZ):
        ft_ref[z] = jnp.transpose(f_ref[:, z].astype(f32), (1, 0, 2)).astype(bf16)
    for ref, start, high in ((me_ref, 6 - 6 * py, py == 0), (mo_ref, 6 * py, py == 1)):
        for z in range(BZ):
            ref[2 * z : 2 * z + 2] = ft_ref[z, pl.ds(start, 2)]
        parts = []
        for z in range(BZ):
            own = s_ref[z].astype(f32)
            parts.append(jnp.where(high, pltpu.roll(own, 4, 0), own))
        halves = [jnp.where(row < 4, parts[i], pltpu.roll(parts[i + 1], 4, 0)) for i in (0, 2)]
        ref[2 * BZ] = jnp.concatenate(halves, axis=0).astype(bf16)


def extend(at, ft_ref, s_ref, re_ref, ro_ref, fy_ref, sy_ref, ma_ref, mb_ref):
    pz, py = at[2], at[3]
    row = lax.broadcasted_iota(jnp.int32, (BY, X), 0)
    te = re_ref[2 * BZ].astype(f32)
    to = ro_ref[2 * BZ].astype(f32)
    before = jnp.where(py == 0, to, te)
    after = jnp.where(py == 0, te, to)
    for z in range(BZ):
        fy_ref[z, 2 : 2 + BY] = ft_ref[z]
        fy_ref[z, pl.ds(10 - 10 * py, 2)] = re_ref[2 * z : 2 * z + 2]
        fy_ref[z, pl.ds(10 * py, 2)] = ro_ref[2 * z : 2 * z + 2]
        half, low = (z // 2) * 8, (z % 2) * 4
        own = pltpu.roll(s_ref[z].astype(f32), 4, 0)
        b = before[half : half + 8]
        a = after[half : half + 8]
        b = pltpu.roll(b, 4, 0) if low else b
        a = a if low else pltpu.roll(a, 4, 0)
        sy_ref[z] = jnp.concatenate([jnp.where(row < 4, b, own), jnp.where(row < 4, own, a)], axis=0)
    for ref, start, sign in ((ma_ref, 2 - 2 * pz, 1 - pz), (mb_ref, 2 * pz, pz)):
        for k in range(2):
            ref[12 * k : 12 * k + 12] = fy_ref[start + k]
        for k in range(3):
            ref[24 + k] = sy_ref[sign + k].astype(bf16)


def forward(nz, ny, at, fy_ref, sy_ref, ma_ref, mb_ref, lab_ref, w1_ref, w2_ref, sw_ref,
            fc_ref, hx_ref, slope1_ref, slope2_ref, top_ref, me_ref, mo_ref, own_ref, g0_ref, p_ref, fx_ref):
    iz, iy, pz, py = at[0], at[1], at[2], at[3]
    for k in range(BZ):
        put_taps(fx_ref, 2 + k, fy_ref[k].astype(f32))
    for k in range(2):
        put_taps(fx_ref, 6 - 6 * pz + k, ma_ref[12 * k : 12 * k + 12].astype(f32))
        put_taps(fx_ref, 6 * pz + k, mb_ref[12 * k : 12 * k + 12].astype(f32))
    fc_ref[...] = fx_ref[1:7, 1:11]
    w1 = w1_ref[...]
    w2 = w2_ref[...]

    def first(z, carry):
        zg = iz * BZ - 1 + z
        zin = (zg >= 0) & (zg < nz)
        for y in range(0, BY + 2, 2):
            acts = two_rows(w1, fx_ref, z, y)
            hid = []
            for j, act in enumerate(acts):
                yg = iy * BY - 1 + y + j
                keep = jnp.where(zin & (yg >= 0) & (yg < ny), 1.0, 0.0)
                sig = jax.nn.sigmoid(act)
                slope1_ref[z, y + j] = sig * (1.0 + act * (1.0 - sig)) * keep
                hid.append((act * sig * keep)[None])
            hid = jnp.concatenate(hid, axis=0)
            low, up = sides(hid)
            hx_ref[z, y : y + 2, 0] = low.astype(bf16)
            hx_ref[z, y : y + 2, 1] = hid.astype(bf16)
            hx_ref[z, y : y + 2, 2] = up.astype(bf16)
        return carry

    lax.fori_loop(0, BZ + 2, first, 0, unroll=2)
    sw = sw_ref[...]

    def second(z, carry):
        rows = []
        for y in range(0, BY, 2):
            for j, act in enumerate(two_rows(w2, hx_ref, z, y)):
                sig = jax.nn.sigmoid(act)
                top = act * sig
                top_ref[z, y + j] = top
                slope2_ref[z, y + j] = sig * (1.0 + act * (1.0 - sig))
                rows.append(jnp.sum(top * sw, axis=0, keepdims=True))
        own_ref[0, z] = jnp.tanh(jnp.concatenate(rows, axis=0))
        return carry

    lax.fori_loop(0, BZ, second, 0, unroll=2)

    for k in range(BZ):
        p_ref[3 + k] = sy_ref[k]
    for k in range(3):
        p_ref[7 - 7 * pz + k] = ma_ref[24 + k].astype(f32)
        p_ref[7 * pz + k] = mb_ref[24 + k].astype(f32)
    rows_in = inside(iy * BY - 4, (16, X), ny)
    for k in range(10):
        zg = iz * BZ - 3 + k
        p_ref[k] = jnp.where(rows_in & (zg >= 0) & (zg < nz), 2.0 * p_ref[k] - 1.0, 0.0)
    for k in range(8):
        centre, uz, lz = p_ref[k + 1], p_ref[k + 2], p_ref[k]
        ly, uy = pltpu.roll(centre, 1, 0), pltpu.roll(centre, 15, 0)
        lx, ux = sides(centre)
        dz, dy, dx = (uz - lz) * 0.5, (uy - ly) * 0.5, (ux - lx) * 0.5
        g = jnp.sqrt(dz * dz + dy * dy + dx * dx + FLOOR)
        g0_ref[k] = g
        if 2 <= k < 6:
            lap = uz + lz + uy + ly + ux + lx - 6.0 * centre
            base = pltpu.roll(centre + (A * 0.5) * lap, 12, 0)[:8]
            own_ref[1, k - 2] = base + A * own_ref[0, k - 2] * pltpu.roll(g, 12, 0)[:8]
    for z in range(BZ):
        own_ref[2, z] = lab_ref[z]
    for ref, start in ((me_ref, 6 - 6 * py), (mo_ref, 6 * py)):
        ref[:12] = own_ref[...].reshape(12, BY, X).astype(SENT)
        for z in range(BZ):
            ref[12 + 4 * z : 16 + 4 * z] = slope2_ref[z, pl.ds(start, 2)].reshape(4, 8, X).astype(SENT)


def widen(at, me_ref, slope2_ref, re_ref, ro_ref, ma_ref, mb_ref, s2y_ref):
    pz, py = at[2], at[3]
    ma_ref[12:24] = me_ref[:12]
    ma_ref[pl.ds(24 - 24 * py, 12)] = re_ref[:12]
    ma_ref[pl.ds(24 * py, 12)] = ro_ref[:12]
    for z in range(BZ):
        s2y_ref[z, 2 : 2 + BY] = slope2_ref[z].astype(bf16)
        for ref, start in ((re_ref, 10 - 10 * py), (ro_ref, 10 * py)):
            rows = ref[12 + 4 * z : 16 + 4 * z].astype(f32).reshape(2, C, X)
            s2y_ref[z, pl.ds(start, 2)] = rows.astype(bf16)
    for k in range(2):
        rows = s2y_ref[2 - 2 * pz + k].astype(f32).reshape(24, 8, X)
        ma_ref[36 + 24 * k : 60 + 24 * k] = rows.astype(SENT)
        rows = s2y_ref[2 * pz + k].astype(f32).reshape(24, 8, X)
        mb_ref[24 * k : 24 + 24 * k] = rows.astype(SENT)


def relay(at, ma_ref, ra_ref, mb_ref):
    pz = at[2]
    mb_ref[:36] = ma_ref[:36]
    for i in range(3):
        mb_ref[36 + 9 * i : 44 + 9 * i] = ra_ref[12 * i : 12 * i + 8]
        mb_ref[44 + 9 * i] = ra_ref[12 * i + 8 + 3 * pz]


def march(nz, ny, at, own_ref, ye_ref, mate_ref, far_ref, far2_ref, g0_ref, dpre_ref,
          sp, lab, ph, w_s, dz_s, dy_s, dx_s, ag_s, ds, dd):
    iz, iy, pz = at[0], at[1], at[2]
    base = 4 * pz

    def place(start, block):
        for k in range(BZ):
            for ref, f in ((sp, 0), (ph, 1), (lab, 2)):
                plane = jnp.concatenate([block(i, f, k).astype(f32) for i in range(3)], axis=0)
                if f == 1:
                    ph[0, start + k] = plane
                else:
                    ref[start + k] = plane

    def piece(ref, first):
        return lambda i, f, k: ref[first + 12 * i + 4 * f + k]

    def mine(i, f, k):
        return own_ref[f, k] if i == 1 else ye_ref[12 * i + 4 * f + k]

    place(8 + 4 * pz, mine)
    place(12 - 4 * pz, piece(mate_ref, 0))
    place(16 * pz + 4 - 4 * pz, piece(far_ref, 0))
    place(16 - 16 * pz + 4 * pz, piece(far2_ref, 0))

    def beyond(i, f, k):
        return far_ref[44 + 9 * i if f == 2 else 36 + 9 * i + 4 * f + k]

    place(16 * pz + 4 * pz, beyond)

    dd[0, 0] = jnp.zeros((24, X), f32)
    rows_in = inside(iy * BY - 8, (24, X), ny)
    first_plane = (iz - pz) * BZ - 8

    def within(z):
        zg = first_plane + z
        return rows_in & (zg >= 0) & (zg < nz)

    for t in (1, 2, 3):

        def step(i, carry, t=t):
            z = base + i
            centre, uz, lz = ph[t - 1, z], ph[t - 1, z + 1], ph[t - 1, z - 1]
            ly, uy = pltpu.roll(centre, 1, 0), pltpu.roll(centre, 23, 0)
            lx, ux = sides(centre)
            dz, dy, dx = (uz - lz) * 0.5, (uy - ly) * 0.5, (ux - lx) * 0.5
            square = dz * dz + dy * dy + dx * dx + FLOOR
            root = lax.rsqrt(square)
            lap = uz + lz + uy + ly + ux + lx - 6.0 * centre
            speed = sp[z]
            ag = A * square * root
            new = jnp.where(within(z), centre + speed * ag + (A * 0.5) * lap, 0.0)
            w_s[t - 1, z] = (A * 0.5) * speed * root
            dz_s[t - 1, z] = dz
            dy_s[t - 1, z] = dy
            dx_s[t - 1, z] = dx
            ag_s[t - 1, z] = ag
            if t < 3:
                ph[t, z] = new
            else:
                dd[0, z] = jnp.where(within(z), jax.nn.sigmoid(new) - lab[z], 0.0)
            return carry

        lax.fori_loop(t, 20 - t, step, 0, unroll=2)

    for n, t in enumerate((3, 2, 1)):
        src, dst = n % 2, (n + 1) % 2

        def back(i, carry, t=t, n=n, src=src, dst=dst):
            l1, a1, a2 = carry
            z = base + i
            d = dd[src, z]
            add = ag_s[t - 1, z] * d
            ds[z] = add if n == 0 else ds[z] + add
            w = w_s[t - 1, z] * d
            e = (A * 0.5) * d
            qz, qy, qx = w * dz_s[t - 1, z], w * dy_s[t - 1, z], w * dx_s[t - 1, z]
            local = (1.0 - 3.0 * A) * d
            local = local + pltpu.roll(e + qy, 1, 0) + pltpu.roll(e - qy, 23, 0)
            local = local + sides(e + qx)[0] + sides(e - qx)[1]
            dd[dst, z - 1] = jnp.where(within(z - 1), l1 + a2 + (e - qz), 0.0)
            return local, e + qz, a1

        zero = dd[0, 0]
        lax.fori_loop(3 + n, 17 - n, back, (zero, zero, zero), unroll=2)

    for k in range(8):
        z = base + 6 + k
        speed = sp[z]
        left = 1.0 - speed * speed
        one = pltpu.roll(ds[z] * left, 20, 0)[:16]
        two = pltpu.roll(dd[1, z] * left, 20, 0)[:16]
        dpre_ref[k] = one + A * two * g0_ref[k]


def backward(at, dpre_ref, slope2_ref, s2y_ref, ra_ref, rb_ref, sw_ref, hx_ref, fx_ref, slope1_ref,
             top_ref, w1_ref, w2_ref, df_ref, grad_ref, dx_ref, ex_ref):
    pz = at[2]
    sw = sw_ref[...]

    def second(z, slope):
        for y in range(BY + 4):
            d = dpre_ref[z, 2 + y : 3 + y, :]
            value = (sw * d * slope(y))[None]
            low, up = sides(value)
            dx_ref[z, y : y + 1, 0] = low.astype(bf16)
            dx_ref[z, y : y + 1, 1] = value.astype(bf16)
            dx_ref[z, y : y + 1, 2] = up.astype(bf16)

    for k in range(BZ):
        def own(y, k=k):
            if 2 <= y < 2 + BY:
                return slope2_ref[k, y - 2]
            return s2y_ref[k, y].astype(f32)

        second(2 + k, own)
    for k in range(2):
        for ref, first, z in ((ra_ref, 36, 6 - 6 * pz), (rb_ref, 0, 6 * pz)):
            def far(y, ref=ref, first=first + 24 * k):
                return ref[first + 2 * y : first + 2 * y + 2].astype(f32).reshape(C, X)

            second(z + k, far)

    w2 = w2_ref[...]
    w1 = w1_ref[...]

    def hidden(z, carry):
        for y in range(0, BY + 2, 2):
            both = two_rows(w2, dx_ref, z, y)
            d = jnp.concatenate([(v * slope1_ref[z, y + j])[None] for j, v in enumerate(both)], axis=0)
            low, up = sides(d)
            ex_ref[z, y : y + 2, 0] = low.astype(bf16)
            ex_ref[z, y : y + 2, 1] = d.astype(bf16)
            ex_ref[z, y : y + 2, 2] = up.astype(bf16)
        return carry

    lax.fori_loop(0, BZ + 2, hidden, 0, unroll=2)

    def features(z, carry):
        rows = []
        for y in range(0, BY, 2):
            a, b = two_rows(w1, ex_ref, z, y)
            rows += [a[None], b[None]]
        plane = jnp.concatenate(rows, axis=0)
        df_ref[:, z] = jnp.transpose(plane, (1, 0, 2)).astype(bf16)
        return carry

    lax.fori_loop(0, BZ, features, 0, unroll=2)

    nt = (((1,), (1,)), ((), ()))

    def weights(z, carry):
        g1, g2, gs = carry
        d2 = jnp.concatenate([dx_ref[z + 2, y + 2, 1] for y in range(BY)], axis=1)
        d1 = jnp.concatenate([ex_ref[z + 1, y + 1, 1] for y in range(BY)], axis=1)
        p2 = [hx_ref[pl.ds(z, 3), y : y + 3].reshape(TAPS, X) for y in range(BY)]
        p1 = [fx_ref[pl.ds(z, 3), y : y + 3].reshape(TAPS, X) for y in range(BY)]
        g2 = g2 + lax.dot_general(d2, jnp.concatenate(p2, axis=1), nt, preferred_element_type=f32)
        g1 = g1 + lax.dot_general(d1, jnp.concatenate(p1, axis=1), nt, preferred_element_type=f32)
        for y in range(BY):
            gs = gs + dpre_ref[z + 2, 4 + y : 5 + y, :] * top_ref[z, y]
        return g1, g2, gs

    zero = jnp.zeros((C, TAPS), f32)
    g1, g2, gs = lax.fori_loop(0, BZ, weights, (zero, zero, jnp.zeros((C, X), f32)))
    grad_ref[...] = jnp.zeros_like(grad_ref)
    for i, g in enumerate((g1, g2)):
        for k in range(3):
            grad_ref[i, C * k : C * k + C] = g[:, X * k : X * k + X]
        grad_ref[i, 48:, :48] = g[:8, 3 * X :]
        grad_ref[i, 48:, 64:112] = g[8:, 3 * X :]
    grad_ref[0, 48:49, 48:64] = jnp.sum(jnp.transpose(gs), axis=0, keepdims=True)


def finish(a_ref, b_ref, first_ref, second_ref, speed_ref):
    a, b = a_ref[...], b_ref[...]
    total = jnp.sum(a * a) + jnp.sum(b * b)
    count = 54.0 * C * C + C
    factor = 1.0 / jnp.maximum(jnp.sqrt(jnp.full((1, 1), total)) / jnp.sqrt(f32(count)), 1.0)
    a, b = a * factor, b * factor
    for out, g in ((first_ref, a), (second_ref, b)):
        for t in range(27):
            row, lane = C * (t // 8), C * (t % 8)
            if t < 24:
                out[t] = g[row : row + C, lane : lane + C]
            else:
                out[t, :8] = g[48:, lane : lane + C]
                out[t, 8:] = g[48:, 64 + lane : 64 + lane + C]
    speed_ref[...] = a[48:49, 48:64]


def call(kernel, outs, scratch=(), flops=0):
    smem = pl.BlockSpec(memory_space=pltpu.SMEM)
    vmem = pl.BlockSpec(memory_space=pltpu.VMEM)

    def run(at, *args):
        args = ((at,) if at is not None else ()) + args
        specs = [smem if (i == 0 and at is not None) else vmem for i in range(len(args))]
        many = isinstance(outs, (list, tuple))
        size = sum(a.size * a.dtype.itemsize for a in args)
        return pl.pallas_call(
            kernel,
            out_shape=outs,
            in_specs=specs,
            out_specs=[vmem] * len(outs) if many else vmem,
            scratch_shapes=list(scratch),
            cost_estimate=pl.CostEstimate(flops=flops, bytes_accessed=size, transcendentals=0),
            compiler_params=pltpu.CompilerParams(vmem_limit_bytes=16 * 1024 * 1024),
        )(*args)

    return run


def shape(dims, dtype=bf16):
    return jax.ShapeDtypeStruct(dims, dtype)


def even(value, axis):
    n = lax.axis_size(axis)
    return lax.ppermute(value, axis, [(i, i ^ 1) for i in range(n)])


def odd(value, axis):
    n = lax.axis_size(axis)
    pairs = [(i, i + 1) for i in range(1, n - 1, 2)]
    return lax.ppermute(value, axis, pairs + [(j, i) for i, j in pairs])


def groups(n, unit):
    size = max(1, min(4, n // unit))
    firsts = [i for i in range(n) if (i // unit) % size == 0]
    return [[i + unit * k for k in range(size)] for i in firsts]


def total_of(grad, iz):
    core = iz % 2
    keep = lax.dynamic_index_in_dim(grad, core, 0, keepdims=False)
    give = lax.dynamic_index_in_dim(grad, 1 - core, 0, keepdims=False)
    part = keep + even(give, "gz")
    for axis, unit in (("gy", 1), ("gy", 4), ("gz", 8), ("gz", 2)):
        sets = groups(lax.axis_size(axis), unit)
        if len(sets[0]) > 1:
            copies = jnp.broadcast_to(part[None], (len(sets[0]),) + part.shape)
            part = jnp.sum(lax.all_to_all(copies, axis, 0, 0, axis_index_groups=sets), axis=0)
    other = even(part, "gz")
    return jnp.where(core == 0, part, other), jnp.where(core == 0, other, part)


def on_device(features, labels, sign_map, conv_first, conv_second, speed_weight):
    nz, ny = BZ * lax.axis_size("gz"), BY * lax.axis_size("gy")
    iz, iy = lax.axis_index("gz"), lax.axis_index("gy")
    pz, py = iz % 2, iy % 2
    at = jnp.stack([iz, iy, pz, py]).astype(jnp.int32)
    taps = [w.transpose(2, 3, 4, 0, 1).reshape(27, C, C) for w in (conv_first, conv_second)]
    w1, w2, w1b, w2b, sw, target = call(
        build, [shape((2 * C, 36 * C))] * 4 + [shape((C, X), f32), shape((BZ, BY, X), f32)]
    )(None, *taps, speed_weight.reshape(1, C), labels)

    ft, me, mo = call(prepare, [shape((BZ, BY, C, X)), shape((9, C, X)), shape((9, C, X))])(
        at, features, sign_map
    )
    ro = odd(mo, "gy")
    re = even(me, "gy")
    fy, sy, ma, mb = call(
        extend,
        [shape((BZ, 12, C, X)), shape((BZ, 16, X), f32), shape((27, C, X)), shape((27, C, X))],
    )(at, ft, sign_map, re, ro)
    rb = odd(mb, "gz")
    ra = even(ma, "gz")

    fx, hx, slope1, slope2, top, fe, fo, own, g0 = call(
        lambda *refs: forward(nz, ny, *refs),
        [
            shape((6, 10, 3, C, X)),
            shape((6, 10, 3, C, X)),
            shape((6, 10, C, X), f32),
            shape((BZ, BY, C, X), f32),
            shape((BZ, BY, C, X), f32),
            shape((28, 8, X), SENT),
            shape((28, 8, X), SENT),
            shape((3, BZ, BY, X), f32),
            shape((8, 16, X), f32),
        ],
        [pltpu.VMEM((10, 16, X), f32), pltpu.VMEM((8, 12, 3, C, X), bf16)],
    )(at, fy, sy, ra, rb, target, w1, w2, sw)

    go = odd(fo, "gy")
    ge = even(fe, "gy")
    fa, fs, s2y = call(
        widen, [shape((84, 8, X), SENT), shape((48, 8, X), SENT), shape((BZ, 12, C, X))]
    )(at, fe, slope2, ge, go)
    ha = even(fa, "gz")
    fb = call(relay, shape((63, 8, X), SENT))(at, fa, ha)
    hb = odd(fb, "gz")
    hs = odd(fs, "gz")
    hc = even(hb, "gz")

    plane = (24, 24, X)
    dpre = call(
        lambda *refs: march(nz, ny, *refs),
        shape((8, 16, X), f32),
        [
            pltpu.VMEM(plane, f32),
            pltpu.VMEM(plane, f32),
            pltpu.VMEM((3,) + plane, f32),
            pltpu.VMEM((3,) + plane, f32),
            pltpu.VMEM((3,) + plane, f32),
            pltpu.VMEM((3,) + plane, f32),
            pltpu.VMEM((3,) + plane, f32),
            pltpu.VMEM((3,) + plane, f32),
            pltpu.VMEM(plane, f32),
            pltpu.VMEM((2,) + plane, f32),
        ],
    )(at, own, fa, ha, hb, hc, g0)

    d_features, grad = call(
        backward,
        [shape((C, BZ, BY, X)), shape((2, 56, X), f32)],
        [pltpu.VMEM((8, 12, 3, C, X), bf16), pltpu.VMEM((6, 10, 3, C, X), bf16)],
    )(at, dpre, slope2, s2y, ha, hs, sw, hx, fx, slope1, top, w1b, w2b)

    a, b = total_of(grad, iz)
    tap_major = shape((27, C, C), f32)
    first, second, speed = call(finish, [tap_major, tap_major, shape((1, C), f32)])(None, a, b)
    first, second = (
        g.reshape(3, 3, 3, C, C).transpose(3, 4, 0, 1, 2) for g in (first, second)
    )
    return d_features, first, second, speed.reshape(C)


def solution(mesh):
    in_specs = (P(None, "gz", "gy", None), P("gz", "gy", None), P("gz", "gy", None), P(), P(), P())
    out_specs = (P(None, "gz", "gy", None), P(), P(), P())

    return jax.shard_map(
        on_device, mesh=mesh, in_specs=in_specs, out_specs=out_specs, check_vma=False
    )
```

```python
import jax
import jax.numpy as jnp
from jax import lax
from jax.experimental import pallas as pl
from jax.experimental.pallas import tpu as pltpu
from jax.sharding import PartitionSpec as P


C = 16
BZ = 4
BY = 8
X = 128
TAPS = 27 * C
A = 0.25
FLOOR = 0.1
SENT = jnp.bfloat16
f32 = jnp.float32
bf16 = jnp.bfloat16


def sides(v):
    axis = v.ndim - 1
    lane = lax.broadcasted_iota(jnp.int32, v.shape, axis)
    low = jnp.where(lane == 0, 0.0, pltpu.roll(v, 1, axis))
    up = jnp.where(lane == X - 1, 0.0, pltpu.roll(v, X - 1, axis))
    return low, up


def put_taps(ref, index, v):
    low, up = sides(v)
    ref[index, :, 0] = low.astype(bf16)
    ref[index, :, 1] = v.astype(bf16)
    ref[index, :, 2] = up.astype(bf16)


def two_rows(weight, taps_ref, z, y):
    patch = taps_ref[pl.ds(z, 3), y : y + 4].reshape(4 * 9 * C, X)
    out = jnp.dot(weight, patch, preferred_element_type=f32)
    return out[:C], out[C:]


def inside(start, shape, limit):
    row = start + lax.broadcasted_iota(jnp.int32, shape, 0)
    return (row >= 0) & (row < limit)


def build(c1_ref, c2_ref, sp_ref, lab_ref, w1_ref, w2_ref, w1b_ref, w2b_ref, sw_ref, labf_ref):
    sw_ref[...] = jnp.transpose(jnp.broadcast_to(sp_ref[...], (X, C)))
    labf_ref[...] = lab_ref[...].astype(f32)
    zero = jnp.zeros((C, C), f32)
    for src, fwd, adj in ((c1_ref, w1_ref, w1b_ref), (c2_ref, w2_ref, w2b_ref)):
        for j in range(2):
            one, two = [], []
            for a in range(3):
                for b in range(4):
                    for c in range(3):
                        tap = (a * 3 + b - j) * 3 + c
                        ok = 0 <= b - j < 3
                        one.append(src[tap].astype(f32) if ok else zero)
                        two.append(src[26 - tap].astype(f32).T if ok else zero)
            fwd[C * j : C * j + C] = jnp.concatenate(one, axis=1).astype(bf16)
            adj[C * j : C * j + C] = jnp.concatenate(two, axis=1).astype(bf16)


def prepare(at, f_ref, s_ref, ft_ref, me_ref, mo_ref):
    py = at[3]
    row = lax.broadcasted_iota(jnp.int32, (BY, X), 0)
    for z in range(BZ):
        ft_ref[z] = jnp.transpose(f_ref[:, z].astype(f32), (1, 0, 2)).astype(bf16)
    for ref, start, high in ((me_ref, 6 - 6 * py, py == 0), (mo_ref, 6 * py, py == 1)):
        for z in range(BZ):
            ref[2 * z : 2 * z + 2] = ft_ref[z, pl.ds(start, 2)]
        parts = []
        for z in range(BZ):
            own = s_ref[z].astype(f32)
            parts.append(jnp.where(high, pltpu.roll(own, 4, 0), own))
        halves = [jnp.where(row < 4, parts[i], pltpu.roll(parts[i + 1], 4, 0)) for i in (0, 2)]
        ref[2 * BZ] = jnp.concatenate(halves, axis=0).astype(bf16)


def extend(at, ft_ref, s_ref, re_ref, ro_ref, fy_ref, sy_ref, ma_ref, mb_ref):
    pz, py = at[2], at[3]
    row = lax.broadcasted_iota(jnp.int32, (BY, X), 0)
    te = re_ref[2 * BZ].astype(f32)
    to = ro_ref[2 * BZ].astype(f32)
    before = jnp.where(py == 0, to, te)
    after = jnp.where(py == 0, te, to)
    for z in range(BZ):
        fy_ref[z, 2 : 2 + BY] = ft_ref[z]
        fy_ref[z, pl.ds(10 - 10 * py, 2)] = re_ref[2 * z : 2 * z + 2]
        fy_ref[z, pl.ds(10 * py, 2)] = ro_ref[2 * z : 2 * z + 2]
        half, low = (z // 2) * 8, (z % 2) * 4
        own = pltpu.roll(s_ref[z].astype(f32), 4, 0)
        b = before[half : half + 8]
        a = after[half : half + 8]
        b = pltpu.roll(b, 4, 0) if low else b
        a = a if low else pltpu.roll(a, 4, 0)
        sy_ref[z] = jnp.concatenate([jnp.where(row < 4, b, own), jnp.where(row < 4, own, a)], axis=0)
    for ref, start, sign in ((ma_ref, 2 - 2 * pz, 1 - pz), (mb_ref, 2 * pz, pz)):
        for k in range(2):
            ref[12 * k : 12 * k + 12] = fy_ref[start + k]
        for k in range(3):
            ref[24 + k] = sy_ref[sign + k].astype(bf16)


def forward(nz, ny, at, fy_ref, sy_ref, ma_ref, mb_ref, lab_ref, w1_ref, w2_ref, sw_ref,
            fc_ref, hx_ref, slope1_ref, slope2_ref, top_ref, me_ref, mo_ref, own_ref, g0_ref, p_ref, fx_ref):
    iz, iy, pz, py = at[0], at[1], at[2], at[3]
    for k in range(BZ):
        put_taps(fx_ref, 2 + k, fy_ref[k].astype(f32))
    for k in range(2):
        put_taps(fx_ref, 6 - 6 * pz + k, ma_ref[12 * k : 12 * k + 12].astype(f32))
        put_taps(fx_ref, 6 * pz + k, mb_ref[12 * k : 12 * k + 12].astype(f32))
    fc_ref[...] = fx_ref[1:7, 1:11]
    w1 = w1_ref[...]
    w2 = w2_ref[...]

    def first(z, carry):
        zg = iz * BZ - 1 + z
        zin = (zg >= 0) & (zg < nz)
        for y in range(0, BY + 2, 2):
            acts = two_rows(w1, fx_ref, z, y)
            hid = []
            for j, act in enumerate(acts):
                yg = iy * BY - 1 + y + j
                keep = jnp.where(zin & (yg >= 0) & (yg < ny), 1.0, 0.0)
                sig = jax.nn.sigmoid(act)
                slope1_ref[z, y + j] = sig * (1.0 + act * (1.0 - sig)) * keep
                hid.append((act * sig * keep)[None])
            hid = jnp.concatenate(hid, axis=0)
            low, up = sides(hid)
            hx_ref[z, y : y + 2, 0] = low.astype(bf16)
            hx_ref[z, y : y + 2, 1] = hid.astype(bf16)
            hx_ref[z, y : y + 2, 2] = up.astype(bf16)
        return carry

    lax.fori_loop(0, BZ + 2, first, 0, unroll=2)
    sw = sw_ref[...]

    def second(z, carry):
        rows = []
        for y in range(0, BY, 2):
            for j, act in enumerate(two_rows(w2, hx_ref, z, y)):
                sig = jax.nn.sigmoid(act)
                top = act * sig
                top_ref[z, y + j] = top
                slope2_ref[z, y + j] = sig * (1.0 + act * (1.0 - sig))
                rows.append(jnp.sum(top * sw, axis=0, keepdims=True))
        own_ref[0, z] = jnp.tanh(jnp.concatenate(rows, axis=0))
        return carry

    lax.fori_loop(0, BZ, second, 0, unroll=2)

    for k in range(BZ):
        p_ref[3 + k] = sy_ref[k]
    for k in range(3):
        p_ref[7 - 7 * pz + k] = ma_ref[24 + k].astype(f32)
        p_ref[7 * pz + k] = mb_ref[24 + k].astype(f32)
    rows_in = inside(iy * BY - 4, (16, X), ny)
    for k in range(10):
        zg = iz * BZ - 3 + k
        p_ref[k] = jnp.where(rows_in & (zg >= 0) & (zg < nz), 2.0 * p_ref[k] - 1.0, 0.0)
    for k in range(8):
        centre, uz, lz = p_ref[k + 1], p_ref[k + 2], p_ref[k]
        ly, uy = pltpu.roll(centre, 1, 0), pltpu.roll(centre, 15, 0)
        lx, ux = sides(centre)
        dz, dy, dx = (uz - lz) * 0.5, (uy - ly) * 0.5, (ux - lx) * 0.5
        g = jnp.sqrt(dz * dz + dy * dy + dx * dx + FLOOR)
        g0_ref[k] = g
        if 2 <= k < 6:
            lap = uz + lz + uy + ly + ux + lx - 6.0 * centre
            base = pltpu.roll(centre + (A * 0.5) * lap, 12, 0)[:8]
            own_ref[1, k - 2] = base + A * own_ref[0, k - 2] * pltpu.roll(g, 12, 0)[:8]
    for z in range(BZ):
        own_ref[2, z] = lab_ref[z]
    for ref, start in ((me_ref, 6 - 6 * py), (mo_ref, 6 * py)):
        ref[:12] = own_ref[...].reshape(12, BY, X).astype(SENT)
        for z in range(BZ):
            ref[12 + 4 * z : 16 + 4 * z] = slope2_ref[z, pl.ds(start, 2)].reshape(4, 8, X).astype(SENT)


def widen(at, me_ref, re_ref, ro_ref, ma_ref):
    py = at[3]
    ma_ref[12:24] = me_ref[:12]
    ma_ref[pl.ds(24 - 24 * py, 12)] = re_ref[:12]
    ma_ref[pl.ds(24 * py, 12)] = ro_ref[:12]


def spread(at, slope2_ref, re_ref, ro_ref, ma_ref, mb_ref, s2y_ref):
    pz, py = at[2], at[3]
    for z in range(BZ):
        s2y_ref[z, 2 : 2 + BY] = slope2_ref[z].astype(bf16)
        for ref, start in ((re_ref, 10 - 10 * py), (ro_ref, 10 * py)):
            rows = ref[12 + 4 * z : 16 + 4 * z].astype(f32).reshape(2, C, X)
            s2y_ref[z, pl.ds(start, 2)] = rows.astype(bf16)
    for k in range(2):
        for ref, start in ((ma_ref, 2 - 2 * pz), (mb_ref, 2 * pz)):
            rows = s2y_ref[start + k].astype(f32).reshape(24, 8, X)
            ref[24 * k : 24 + 24 * k] = rows.astype(SENT)


def relay(at, ma_ref, ra_ref, mb_ref):
    pz = at[2]
    mb_ref[:36] = ma_ref[:36]
    for i in range(3):
        mb_ref[36 + 9 * i : 44 + 9 * i] = ra_ref[12 * i : 12 * i + 8]
        mb_ref[44 + 9 * i] = ra_ref[12 * i + 8 + 3 * pz]


def march(nz, ny, at, own_ref, ye_ref, mate_ref, far_ref, far2_ref, g0_ref, dpre_ref,
          sp, lab, ph, w_s, dz_s, dy_s, dx_s, ag_s, ds, dd):
    iz, iy, pz = at[0], at[1], at[2]
    base = 4 * pz

    def place(start, block):
        for k in range(BZ):
            for ref, f in ((sp, 0), (ph, 1), (lab, 2)):
                plane = jnp.concatenate([block(i, f, k).astype(f32) for i in range(3)], axis=0)
                if f == 1:
                    ph[0, start + k] = plane
                else:
                    ref[start + k] = plane

    def piece(ref, first):
        return lambda i, f, k: ref[first + 12 * i + 4 * f + k]

    def mine(i, f, k):
        return own_ref[f, k] if i == 1 else ye_ref[12 * i + 4 * f + k]

    place(8 + 4 * pz, mine)
    place(12 - 4 * pz, piece(mate_ref, 0))
    place(16 * pz + 4 - 4 * pz, piece(far_ref, 0))
    place(16 - 16 * pz + 4 * pz, piece(far2_ref, 0))

    def beyond(i, f, k):
        return far_ref[44 + 9 * i if f == 2 else 36 + 9 * i + 4 * f + k]

    place(16 * pz + 4 * pz, beyond)

    dd[0, 0] = jnp.zeros((24, X), f32)
    rows_in = inside(iy * BY - 8, (24, X), ny)
    first_plane = (iz - pz) * BZ - 8

    def within(z):
        zg = first_plane + z
        return rows_in & (zg >= 0) & (zg < nz)

    for t in (1, 2, 3):

        def step(i, carry, t=t):
            z = base + i
            centre, uz, lz = ph[t - 1, z], ph[t - 1, z + 1], ph[t - 1, z - 1]
            ly, uy = pltpu.roll(centre, 1, 0), pltpu.roll(centre, 23, 0)
            lx, ux = sides(centre)
            dz, dy, dx = (uz - lz) * 0.5, (uy - ly) * 0.5, (ux - lx) * 0.5
            square = dz * dz + dy * dy + dx * dx + FLOOR
            root = lax.rsqrt(square)
            lap = uz + lz + uy + ly + ux + lx - 6.0 * centre
            speed = sp[z]
            ag = A * square * root
            new = jnp.where(within(z), centre + speed * ag + (A * 0.5) * lap, 0.0)
            w_s[t - 1, z] = (A * 0.5) * speed * root
            dz_s[t - 1, z] = dz
            dy_s[t - 1, z] = dy
            dx_s[t - 1, z] = dx
            ag_s[t - 1, z] = ag
            if t < 3:
                ph[t, z] = new
            else:
                dd[0, z] = jnp.where(within(z), jax.nn.sigmoid(new) - lab[z], 0.0)
            return carry

        lax.fori_loop(t, 20 - t, step, 0, unroll=2)

    for n, t in enumerate((3, 2, 1)):
        src, dst = n % 2, (n + 1) % 2

        def back(i, carry, t=t, n=n, src=src, dst=dst):
            l1, a1, a2 = carry
            z = base + i
            d = dd[src, z]
            add = ag_s[t - 1, z] * d
            ds[z] = add if n == 0 else ds[z] + add
            w = w_s[t - 1, z] * d
            e = (A * 0.5) * d
            qz, qy, qx = w * dz_s[t - 1, z], w * dy_s[t - 1, z], w * dx_s[t - 1, z]
            local = (1.0 - 3.0 * A) * d
            local = local + pltpu.roll(e + qy, 1, 0) + pltpu.roll(e - qy, 23, 0)
            local = local + sides(e + qx)[0] + sides(e - qx)[1]
            dd[dst, z - 1] = jnp.where(within(z - 1), l1 + a2 + (e - qz), 0.0)
            return local, e + qz, a1

        zero = dd[0, 0]
        lax.fori_loop(3 + n, 17 - n, back, (zero, zero, zero), unroll=2)

    for k in range(8):
        z = base + 6 + k
        speed = sp[z]
        left = 1.0 - speed * speed
        one = pltpu.roll(ds[z] * left, 20, 0)[:16]
        two = pltpu.roll(dd[1, z] * left, 20, 0)[:16]
        dpre_ref[k] = one + A * two * g0_ref[k]


def backward(at, dpre_ref, slope2_ref, s2y_ref, ra_ref, rb_ref, sw_ref, hx_ref, fx_ref, slope1_ref,
             top_ref, w1_ref, w2_ref, df_ref, grad_ref, dx_ref, ex_ref):
    pz = at[2]
    sw = sw_ref[...]

    def second(z, slope):
        for y in range(BY + 4):
            d = dpre_ref[z, 2 + y : 3 + y, :]
            value = (sw * d * slope(y))[None]
            low, up = sides(value)
            dx_ref[z, y : y + 1, 0] = low.astype(bf16)
            dx_ref[z, y : y + 1, 1] = value.astype(bf16)
            dx_ref[z, y : y + 1, 2] = up.astype(bf16)

    for k in range(BZ):
        def own(y, k=k):
            if 2 <= y < 2 + BY:
                return slope2_ref[k, y - 2]
            return s2y_ref[k, y].astype(f32)

        second(2 + k, own)
    for k in range(2):
        for ref, first, z in ((ra_ref, 0, 6 - 6 * pz), (rb_ref, 0, 6 * pz)):
            def far(y, ref=ref, first=first + 24 * k):
                return ref[first + 2 * y : first + 2 * y + 2].astype(f32).reshape(C, X)

            second(z + k, far)

    w2 = w2_ref[...]
    w1 = w1_ref[...]

    def hidden(z, carry):
        for y in range(0, BY + 2, 2):
            both = two_rows(w2, dx_ref, z, y)
            d = jnp.concatenate([(v * slope1_ref[z, y + j])[None] for j, v in enumerate(both)], axis=0)
            low, up = sides(d)
            ex_ref[z, y : y + 2, 0] = low.astype(bf16)
            ex_ref[z, y : y + 2, 1] = d.astype(bf16)
            ex_ref[z, y : y + 2, 2] = up.astype(bf16)
        return carry

    lax.fori_loop(0, BZ + 2, hidden, 0, unroll=2)

    def features(z, carry):
        rows = []
        for y in range(0, BY, 2):
            a, b = two_rows(w1, ex_ref, z, y)
            rows += [a[None], b[None]]
        plane = jnp.concatenate(rows, axis=0)
        df_ref[:, z] = jnp.transpose(plane, (1, 0, 2)).astype(bf16)
        return carry

    lax.fori_loop(0, BZ, features, 0, unroll=2)

    nt = (((1,), (1,)), ((), ()))

    def weights(z, carry):
        g1, g2, gs = carry
        d2 = jnp.concatenate([dx_ref[z + 2, y + 2, 1] for y in range(BY)], axis=1)
        d1 = jnp.concatenate([ex_ref[z + 1, y + 1, 1] for y in range(BY)], axis=1)
        p2 = [hx_ref[pl.ds(z, 3), y : y + 3].reshape(TAPS, X) for y in range(BY)]
        p1 = [fx_ref[pl.ds(z, 3), y : y + 3].reshape(TAPS, X) for y in range(BY)]
        g2 = g2 + lax.dot_general(d2, jnp.concatenate(p2, axis=1), nt, preferred_element_type=f32)
        g1 = g1 + lax.dot_general(d1, jnp.concatenate(p1, axis=1), nt, preferred_element_type=f32)
        for y in range(BY):
            gs = gs + dpre_ref[z + 2, 4 + y : 5 + y, :] * top_ref[z, y]
        return g1, g2, gs

    zero = jnp.zeros((C, TAPS), f32)
    g1, g2, gs = lax.fori_loop(0, BZ, weights, (zero, zero, jnp.zeros((C, X), f32)))
    grad_ref[...] = jnp.zeros_like(grad_ref)
    for i, g in enumerate((g1, g2)):
        for k in range(3):
            grad_ref[i, C * k : C * k + C] = g[:, X * k : X * k + X]
        grad_ref[i, 48:, :48] = g[:8, 3 * X :]
        grad_ref[i, 48:, 64:112] = g[8:, 3 * X :]
    grad_ref[0, 48:49, 48:64] = jnp.sum(jnp.transpose(gs), axis=0, keepdims=True)


def finish(a_ref, b_ref, first_ref, second_ref, speed_ref):
    a, b = a_ref[...], b_ref[...]
    total = jnp.sum(a * a) + jnp.sum(b * b)
    count = 54.0 * C * C + C
    factor = 1.0 / jnp.maximum(jnp.sqrt(jnp.full((1, 1), total)) / jnp.sqrt(f32(count)), 1.0)
    a, b = a * factor, b * factor
    for out, g in ((first_ref, a), (second_ref, b)):
        for t in range(27):
            row, lane = C * (t // 8), C * (t % 8)
            if t < 24:
                out[t] = g[row : row + C, lane : lane + C]
            else:
                out[t, :8] = g[48:, lane : lane + C]
                out[t, 8:] = g[48:, 64 + lane : 64 + lane + C]
    speed_ref[...] = a[48:49, 48:64]


def call(kernel, outs, scratch=(), flops=0):
    smem = pl.BlockSpec(memory_space=pltpu.SMEM)
    vmem = pl.BlockSpec(memory_space=pltpu.VMEM)

    def run(at, *args):
        args = ((at,) if at is not None else ()) + args
        specs = [smem if (i == 0 and at is not None) else vmem for i in range(len(args))]
        many = isinstance(outs, (list, tuple))
        size = sum(a.size * a.dtype.itemsize for a in args)
        return pl.pallas_call(
            kernel,
            out_shape=outs,
            in_specs=specs,
            out_specs=[vmem] * len(outs) if many else vmem,
            scratch_shapes=list(scratch),
            cost_estimate=pl.CostEstimate(flops=flops, bytes_accessed=size, transcendentals=0),
            compiler_params=pltpu.CompilerParams(vmem_limit_bytes=16 * 1024 * 1024),
        )(*args)

    return run


def shape(dims, dtype=bf16):
    return jax.ShapeDtypeStruct(dims, dtype)


def even(value, axis):
    n = lax.axis_size(axis)
    return lax.ppermute(value, axis, [(i, i ^ 1) for i in range(n)])


def odd(value, axis):
    n = lax.axis_size(axis)
    pairs = [(i, i + 1) for i in range(1, n - 1, 2)]
    return lax.ppermute(value, axis, pairs + [(j, i) for i, j in pairs])


def groups(n, unit):
    size = max(1, min(4, n // unit))
    firsts = [i for i in range(n) if (i // unit) % size == 0]
    return [[i + unit * k for k in range(size)] for i in firsts]


def total_of(grad, iz):
    core = iz % 2
    keep = lax.dynamic_index_in_dim(grad, core, 0, keepdims=False)
    give = lax.dynamic_index_in_dim(grad, 1 - core, 0, keepdims=False)
    part = keep + even(give, "gz")
    for axis, unit in (("gy", 1), ("gy", 4), ("gz", 8), ("gz", 2)):
        sets = groups(lax.axis_size(axis), unit)
        if len(sets[0]) > 1:
            copies = jnp.broadcast_to(part[None], (len(sets[0]),) + part.shape)
            part = jnp.sum(lax.all_to_all(copies, axis, 0, 0, axis_index_groups=sets), axis=0)
    other = even(part, "gz")
    return jnp.where(core == 0, part, other), jnp.where(core == 0, other, part)


def on_device(features, labels, sign_map, conv_first, conv_second, speed_weight):
    nz, ny = BZ * lax.axis_size("gz"), BY * lax.axis_size("gy")
    iz, iy = lax.axis_index("gz"), lax.axis_index("gy")
    pz, py = iz % 2, iy % 2
    at = jnp.stack([iz, iy, pz, py]).astype(jnp.int32)
    taps = [w.transpose(2, 3, 4, 0, 1).reshape(27, C, C) for w in (conv_first, conv_second)]
    w1, w2, w1b, w2b, sw, target = call(
        build, [shape((2 * C, 36 * C))] * 4 + [shape((C, X), f32), shape((BZ, BY, X), f32)]
    )(None, *taps, speed_weight.reshape(1, C), labels)

    ft, me, mo = call(prepare, [shape((BZ, BY, C, X)), shape((9, C, X)), shape((9, C, X))])(
        at, features, sign_map
    )
    ro = odd(mo, "gy")
    re = even(me, "gy")
    fy, sy, ma, mb = call(
        extend,
        [shape((BZ, 12, C, X)), shape((BZ, 16, X), f32), shape((27, C, X)), shape((27, C, X))],
    )(at, ft, sign_map, re, ro)
    rb = odd(mb, "gz")
    ra = even(ma, "gz")

    fx, hx, slope1, slope2, top, fe, fo, own, g0 = call(
        lambda *refs: forward(nz, ny, *refs),
        [
            shape((6, 10, 3, C, X)),
            shape((6, 10, 3, C, X)),
            shape((6, 10, C, X), f32),
            shape((BZ, BY, C, X), f32),
            shape((BZ, BY, C, X), f32),
            shape((28, 8, X), SENT),
            shape((28, 8, X), SENT),
            shape((3, BZ, BY, X), f32),
            shape((8, 16, X), f32),
        ],
        [pltpu.VMEM((10, 16, X), f32), pltpu.VMEM((8, 12, 3, C, X), bf16)],
    )(at, fy, sy, ra, rb, target, w1, w2, sw)

    go = odd(fo, "gy")
    ge = even(fe, "gy")
    fa = call(widen, shape((36, 8, X), SENT))(at, fe, ge, go)
    ha = even(fa, "gz")
    ms, fs, s2y = call(
        spread, [shape((48, 8, X), SENT), shape((48, 8, X), SENT), shape((BZ, 12, C, X))]
    )(at, slope2, ge, go)
    fb = call(relay, shape((63, 8, X), SENT))(at, fa, ha)
    hb = odd(fb, "gz")
    hs = odd(fs, "gz")
    hm = even(ms, "gz")
    hc = even(hb, "gz")

    plane = (24, 24, X)
    dpre = call(
        lambda *refs: march(nz, ny, *refs),
        shape((8, 16, X), f32),
        [
            pltpu.VMEM(plane, f32),
            pltpu.VMEM(plane, f32),
            pltpu.VMEM((3,) + plane, f32),
            pltpu.VMEM((3,) + plane, f32),
            pltpu.VMEM((3,) + plane, f32),
            pltpu.VMEM((3,) + plane, f32),
            pltpu.VMEM((3,) + plane, f32),
            pltpu.VMEM((3,) + plane, f32),
            pltpu.VMEM(plane, f32),
            pltpu.VMEM((2,) + plane, f32),
        ],
    )(at, own, fa, ha, hb, hc, g0)

    d_features, grad = call(
        backward,
        [shape((C, BZ, BY, X)), shape((2, 56, X), f32)],
        [pltpu.VMEM((8, 12, 3, C, X), bf16), pltpu.VMEM((6, 10, 3, C, X), bf16)],
    )(at, dpre, slope2, s2y, hm, hs, sw, hx, fx, slope1, top, w1b, w2b)

    a, b = total_of(grad, iz)
    tap_major = shape((27, C, C), f32)
    first, second, speed = call(finish, [tap_major, tap_major, shape((1, C), f32)])(None, a, b)
    first, second = (
        g.reshape(3, 3, 3, C, C).transpose(3, 4, 0, 1, 2) for g in (first, second)
    )
    return d_features, first, second, speed.reshape(C)


def solution(mesh):
    in_specs = (P(None, "gz", "gy", None), P("gz", "gy", None), P("gz", "gy", None), P(), P(), P())
    out_specs = (P(None, "gz", "gy", None), P(), P(), P())

    return jax.shard_map(
        on_device, mesh=mesh, in_specs=in_specs, out_specs=out_specs, check_vma=False
    )
```

```python
import jax
import jax.numpy as jnp
from jax import lax
from jax.experimental import pallas as pl
from jax.experimental.pallas import tpu as pltpu
from jax.sharding import PartitionSpec as P


C = 16
BZ = 4
BY = 8
X = 128
TAPS = 27 * C
A = 0.25
FLOOR = 0.1
SENT = jnp.bfloat16
f32 = jnp.float32
bf16 = jnp.bfloat16


def sides(v):
    axis = v.ndim - 1
    lane = lax.broadcasted_iota(jnp.int32, v.shape, axis)
    low = jnp.where(lane == 0, 0.0, pltpu.roll(v, 1, axis))
    up = jnp.where(lane == X - 1, 0.0, pltpu.roll(v, X - 1, axis))
    return low, up


def put_taps(ref, index, v):
    low, up = sides(v)
    ref[index, :, 0] = low.astype(bf16)
    ref[index, :, 1] = v.astype(bf16)
    ref[index, :, 2] = up.astype(bf16)


def two_rows(weight, taps_ref, z, y):
    patch = taps_ref[pl.ds(z, 3), y : y + 4].reshape(4 * 9 * C, X)
    out = jnp.dot(weight, patch, preferred_element_type=f32)
    return out[:C], out[C:]


def inside(start, shape, limit):
    row = start + lax.broadcasted_iota(jnp.int32, shape, 0)
    return (row >= 0) & (row < limit)


def build(c1_ref, c2_ref, sp_ref, lab_ref, w1_ref, w2_ref, w1b_ref, w2b_ref, sw_ref, labf_ref):
    sw_ref[...] = jnp.transpose(jnp.broadcast_to(sp_ref[...], (X, C)))
    labf_ref[...] = lab_ref[...].astype(f32)
    zero = jnp.zeros((C, C), f32)
    for src, fwd, adj in ((c1_ref, w1_ref, w1b_ref), (c2_ref, w2_ref, w2b_ref)):
        for j in range(2):
            one, two = [], []
            for a in range(3):
                for b in range(4):
                    for c in range(3):
                        tap = (a * 3 + b - j) * 3 + c
                        ok = 0 <= b - j < 3
                        one.append(src[tap].astype(f32) if ok else zero)
                        two.append(src[26 - tap].astype(f32).T if ok else zero)
            fwd[C * j : C * j + C] = jnp.concatenate(one, axis=1).astype(bf16)
            adj[C * j : C * j + C] = jnp.concatenate(two, axis=1).astype(bf16)


def prepare(at, f_ref, s_ref, ft_ref, me_ref, mo_ref):
    py = at[3]
    row = lax.broadcasted_iota(jnp.int32, (BY, X), 0)
    for z in range(BZ):
        ft_ref[z] = jnp.transpose(f_ref[:, z].astype(f32), (1, 0, 2)).astype(bf16)
    for ref, start, high in ((me_ref, 6 - 6 * py, py == 0), (mo_ref, 6 * py, py == 1)):
        for z in range(BZ):
            ref[2 * z : 2 * z + 2] = ft_ref[z, pl.ds(start, 2)]
        parts = []
        for z in range(BZ):
            own = s_ref[z].astype(f32)
            parts.append(jnp.where(high, pltpu.roll(own, 4, 0), own))
        halves = [jnp.where(row < 4, parts[i], pltpu.roll(parts[i + 1], 4, 0)) for i in (0, 2)]
        ref[2 * BZ] = jnp.concatenate(halves, axis=0).astype(bf16)


def extend(at, ft_ref, s_ref, re_ref, ro_ref, fy_ref, sy_ref, ma_ref, mb_ref):
    pz, py = at[2], at[3]
    row = lax.broadcasted_iota(jnp.int32, (BY, X), 0)
    te = re_ref[2 * BZ].astype(f32)
    to = ro_ref[2 * BZ].astype(f32)
    before = jnp.where(py == 0, to, te)
    after = jnp.where(py == 0, te, to)
    for z in range(BZ):
        fy_ref[z, 2 : 2 + BY] = ft_ref[z]
        fy_ref[z, pl.ds(10 - 10 * py, 2)] = re_ref[2 * z : 2 * z + 2]
        fy_ref[z, pl.ds(10 * py, 2)] = ro_ref[2 * z : 2 * z + 2]
        half, low = (z // 2) * 8, (z % 2) * 4
        own = pltpu.roll(s_ref[z].astype(f32), 4, 0)
        b = before[half : half + 8]
        a = after[half : half + 8]
        b = pltpu.roll(b, 4, 0) if low else b
        a = a if low else pltpu.roll(a, 4, 0)
        sy_ref[z] = jnp.concatenate([jnp.where(row < 4, b, own), jnp.where(row < 4, own, a)], axis=0)
    for ref, start, sign in ((ma_ref, 2 - 2 * pz, 1 - pz), (mb_ref, 2 * pz, pz)):
        for k in range(2):
            ref[12 * k : 12 * k + 12] = fy_ref[start + k]
        for k in range(3):
            ref[24 + k] = sy_ref[sign + k].astype(bf16)


def forward(nz, ny, at, fy_ref, sy_ref, ma_ref, mb_ref, lab_ref, w1_ref, w2_ref, sw_ref,
            fc_ref, hx_ref, slope1_ref, slope2_ref, top_ref, me_ref, mo_ref, own_ref, g0_ref, p_ref, fx_ref):
    iz, iy, pz, py = at[0], at[1], at[2], at[3]
    for k in range(BZ):
        put_taps(fx_ref, 2 + k, fy_ref[k].astype(f32))
    for k in range(2):
        put_taps(fx_ref, 6 - 6 * pz + k, ma_ref[12 * k : 12 * k + 12].astype(f32))
        put_taps(fx_ref, 6 * pz + k, mb_ref[12 * k : 12 * k + 12].astype(f32))
    fc_ref[...] = fx_ref[1:7, 1:11]
    w1 = w1_ref[...]
    w2 = w2_ref[...]

    def first(z, carry):
        zg = iz * BZ - 1 + z
        zin = (zg >= 0) & (zg < nz)
        for y in range(0, BY + 2, 2):
            acts = two_rows(w1, fx_ref, z, y)
            hid = []
            for j, act in enumerate(acts):
                yg = iy * BY - 1 + y + j
                keep = jnp.where(zin & (yg >= 0) & (yg < ny), 1.0, 0.0)
                sig = jax.nn.sigmoid(act)
                slope1_ref[z, y + j] = sig * (1.0 + act * (1.0 - sig)) * keep
                hid.append((act * sig * keep)[None])
            hid = jnp.concatenate(hid, axis=0)
            low, up = sides(hid)
            hx_ref[z, y : y + 2, 0] = low.astype(bf16)
            hx_ref[z, y : y + 2, 1] = hid.astype(bf16)
            hx_ref[z, y : y + 2, 2] = up.astype(bf16)
        return carry

    lax.fori_loop(0, BZ + 2, first, 0, unroll=3)
    sw = sw_ref[...]

    def second(z, carry):
        rows = []
        for y in range(0, BY, 2):
            for j, act in enumerate(two_rows(w2, hx_ref, z, y)):
                sig = jax.nn.sigmoid(act)
                top = act * sig
                top_ref[z, y + j] = top
                slope2_ref[z, y + j] = sig * (1.0 + act * (1.0 - sig))
                rows.append(jnp.sum(top * sw, axis=0, keepdims=True))
        own_ref[0, z] = jnp.tanh(jnp.concatenate(rows, axis=0))
        return carry

    lax.fori_loop(0, BZ, second, 0, unroll=4)

    for k in range(BZ):
        p_ref[3 + k] = sy_ref[k]
    for k in range(3):
        p_ref[7 - 7 * pz + k] = ma_ref[24 + k].astype(f32)
        p_ref[7 * pz + k] = mb_ref[24 + k].astype(f32)
    rows_in = inside(iy * BY - 4, (16, X), ny)
    for k in range(10):
        zg = iz * BZ - 3 + k
        p_ref[k] = jnp.where(rows_in & (zg >= 0) & (zg < nz), 2.0 * p_ref[k] - 1.0, 0.0)
    for k in range(8):
        centre, uz, lz = p_ref[k + 1], p_ref[k + 2], p_ref[k]
        ly, uy = pltpu.roll(centre, 1, 0), pltpu.roll(centre, 15, 0)
        lx, ux = sides(centre)
        dz, dy, dx = (uz - lz) * 0.5, (uy - ly) * 0.5, (ux - lx) * 0.5
        g = jnp.sqrt(dz * dz + dy * dy + dx * dx + FLOOR)
        g0_ref[k] = g
        if 2 <= k < 6:
            lap = uz + lz + uy + ly + ux + lx - 6.0 * centre
            base = pltpu.roll(centre + (A * 0.5) * lap, 12, 0)[:8]
            own_ref[1, k - 2] = base + A * own_ref[0, k - 2] * pltpu.roll(g, 12, 0)[:8]
    for z in range(BZ):
        own_ref[2, z] = lab_ref[z]
    for ref, start in ((me_ref, 6 - 6 * py), (mo_ref, 6 * py)):
        ref[:12] = own_ref[...].reshape(12, BY, X).astype(SENT)
        for z in range(BZ):
            ref[12 + 4 * z : 16 + 4 * z] = slope2_ref[z, pl.ds(start, 2)].reshape(4, 8, X).astype(SENT)


def widen(at, me_ref, re_ref, ro_ref, ma_ref):
    py = at[3]
    ma_ref[12:24] = me_ref[:12]
    ma_ref[pl.ds(24 - 24 * py, 12)] = re_ref[:12]
    ma_ref[pl.ds(24 * py, 12)] = ro_ref[:12]


def spread(at, slope2_ref, re_ref, ro_ref, ma_ref, mb_ref, s2y_ref):
    pz, py = at[2], at[3]
    for z in range(BZ):
        s2y_ref[z, 2 : 2 + BY] = slope2_ref[z].astype(bf16)
        for ref, start in ((re_ref, 10 - 10 * py), (ro_ref, 10 * py)):
            rows = ref[12 + 4 * z : 16 + 4 * z].astype(f32).reshape(2, C, X)
            s2y_ref[z, pl.ds(start, 2)] = rows.astype(bf16)
    for k in range(2):
        for ref, start in ((ma_ref, 2 - 2 * pz), (mb_ref, 2 * pz)):
            rows = s2y_ref[start + k].astype(f32).reshape(24, 8, X)
            ref[24 * k : 24 + 24 * k] = rows.astype(SENT)


def relay(at, ma_ref, ra_ref, mb_ref):
    pz = at[2]
    mb_ref[:36] = ma_ref[:36]
    for i in range(3):
        mb_ref[36 + 9 * i : 44 + 9 * i] = ra_ref[12 * i : 12 * i + 8]
        mb_ref[44 + 9 * i] = ra_ref[12 * i + 8 + 3 * pz]


def march(nz, ny, at, own_ref, ye_ref, mate_ref, far_ref, far2_ref, g0_ref, dpre_ref,
          sp, lab, ph, w_s, dz_s, dy_s, dx_s, ag_s, ds, dd):
    iz, iy, pz = at[0], at[1], at[2]
    base = 4 * pz

    def place(start, block):
        for k in range(BZ):
            for ref, f in ((sp, 0), (ph, 1), (lab, 2)):
                plane = jnp.concatenate([block(i, f, k).astype(f32) for i in range(3)], axis=0)
                if f == 1:
                    ph[0, start + k] = plane
                else:
                    ref[start + k] = plane

    def piece(ref, first):
        return lambda i, f, k: ref[first + 12 * i + 4 * f + k]

    def mine(i, f, k):
        return own_ref[f, k] if i == 1 else ye_ref[12 * i + 4 * f + k]

    place(8 + 4 * pz, mine)
    place(12 - 4 * pz, piece(mate_ref, 0))
    place(16 * pz + 4 - 4 * pz, piece(far_ref, 0))
    place(16 - 16 * pz + 4 * pz, piece(far2_ref, 0))

    def beyond(i, f, k):
        return far_ref[44 + 9 * i if f == 2 else 36 + 9 * i + 4 * f + k]

    place(16 * pz + 4 * pz, beyond)

    dd[0, 0] = jnp.zeros((24, X), f32)
    rows_in = inside(iy * BY - 8, (24, X), ny)
    first_plane = (iz - pz) * BZ - 8

    def within(z):
        zg = first_plane + z
        return rows_in & (zg >= 0) & (zg < nz)

    for t in (1, 2, 3):

        def step(i, carry, t=t):
            z = base + i
            centre, uz, lz = ph[t - 1, z], ph[t - 1, z + 1], ph[t - 1, z - 1]
            ly, uy = pltpu.roll(centre, 1, 0), pltpu.roll(centre, 23, 0)
            lx, ux = sides(centre)
            dz, dy, dx = (uz - lz) * 0.5, (uy - ly) * 0.5, (ux - lx) * 0.5
            square = dz * dz + dy * dy + dx * dx + FLOOR
            root = lax.rsqrt(square)
            lap = uz + lz + uy + ly + ux + lx - 6.0 * centre
            speed = sp[z]
            ag = A * square * root
            new = jnp.where(within(z), centre + speed * ag + (A * 0.5) * lap, 0.0)
            w_s[t - 1, z] = (A * 0.5) * speed * root
            dz_s[t - 1, z] = dz
            dy_s[t - 1, z] = dy
            dx_s[t - 1, z] = dx
            ag_s[t - 1, z] = ag
            if t < 3:
                ph[t, z] = new
            else:
                dd[0, z] = jnp.where(within(z), jax.nn.sigmoid(new) - lab[z], 0.0)
            return carry

        lax.fori_loop(t, 20 - t, step, 0, unroll=2)

    for n, t in enumerate((3, 2, 1)):
        src, dst = n % 2, (n + 1) % 2

        def back(i, carry, t=t, n=n, src=src, dst=dst):
            l1, a1, a2 = carry
            z = base + i
            d = dd[src, z]
            add = ag_s[t - 1, z] * d
            ds[z] = add if n == 0 else ds[z] + add
            w = w_s[t - 1, z] * d
            e = (A * 0.5) * d
            qz, qy, qx = w * dz_s[t - 1, z], w * dy_s[t - 1, z], w * dx_s[t - 1, z]
            local = (1.0 - 3.0 * A) * d
            local = local + pltpu.roll(e + qy, 1, 0) + pltpu.roll(e - qy, 23, 0)
            local = local + sides(e + qx)[0] + sides(e - qx)[1]
            dd[dst, z - 1] = jnp.where(within(z - 1), l1 + a2 + (e - qz), 0.0)
            return local, e + qz, a1

        zero = dd[0, 0]
        lax.fori_loop(3 + n, 17 - n, back, (zero, zero, zero), unroll=2)

    for k in range(8):
        z = base + 6 + k
        speed = sp[z]
        left = 1.0 - speed * speed
        one = pltpu.roll(ds[z] * left, 20, 0)[:16]
        two = pltpu.roll(dd[1, z] * left, 20, 0)[:16]
        dpre_ref[k] = one + A * two * g0_ref[k]


def backward(at, dpre_ref, slope2_ref, s2y_ref, ra_ref, rb_ref, sw_ref, hx_ref, fx_ref, slope1_ref,
             top_ref, w1_ref, w2_ref, df_ref, grad_ref, dx_ref, ex_ref):
    pz = at[2]
    sw = sw_ref[...]

    def second(z, slope):
        for y in range(BY + 4):
            d = dpre_ref[z, 2 + y : 3 + y, :]
            value = (sw * d * slope(y))[None]
            low, up = sides(value)
            dx_ref[z, y : y + 1, 0] = low.astype(bf16)
            dx_ref[z, y : y + 1, 1] = value.astype(bf16)
            dx_ref[z, y : y + 1, 2] = up.astype(bf16)

    for k in range(BZ):
        def own(y, k=k):
            if 2 <= y < 2 + BY:
                return slope2_ref[k, y - 2]
            return s2y_ref[k, y].astype(f32)

        second(2 + k, own)
    for k in range(2):
        for ref, first, z in ((ra_ref, 0, 6 - 6 * pz), (rb_ref, 0, 6 * pz)):
            def far(y, ref=ref, first=first + 24 * k):
                return ref[first + 2 * y : first + 2 * y + 2].astype(f32).reshape(C, X)

            second(z + k, far)

    w2 = w2_ref[...]
    w1 = w1_ref[...]

    def hidden(z, carry):
        for y in range(0, BY + 2, 2):
            both = two_rows(w2, dx_ref, z, y)
            d = jnp.concatenate([(v * slope1_ref[z, y + j])[None] for j, v in enumerate(both)], axis=0)
            low, up = sides(d)
            ex_ref[z, y : y + 2, 0] = low.astype(bf16)
            ex_ref[z, y : y + 2, 1] = d.astype(bf16)
            ex_ref[z, y : y + 2, 2] = up.astype(bf16)
        return carry

    lax.fori_loop(0, BZ + 2, hidden, 0, unroll=3)

    def features(z, carry):
        rows = []
        for y in range(0, BY, 2):
            a, b = two_rows(w1, ex_ref, z, y)
            rows += [a[None], b[None]]
        plane = jnp.concatenate(rows, axis=0)
        df_ref[:, z] = jnp.transpose(plane, (1, 0, 2)).astype(bf16)
        return carry

    lax.fori_loop(0, BZ, features, 0, unroll=4)

    nt = (((1,), (1,)), ((), ()))

    def weights(z, carry):
        g1, g2, gs = carry
        d2 = jnp.concatenate([dx_ref[z + 2, y + 2, 1] for y in range(BY)], axis=1)
        d1 = jnp.concatenate([ex_ref[z + 1, y + 1, 1] for y in range(BY)], axis=1)
        p2 = [hx_ref[pl.ds(z, 3), y : y + 3].reshape(TAPS, X) for y in range(BY)]
        p1 = [fx_ref[pl.ds(z, 3), y : y + 3].reshape(TAPS, X) for y in range(BY)]
        g2 = g2 + lax.dot_general(d2, jnp.concatenate(p2, axis=1), nt, preferred_element_type=f32)
        g1 = g1 + lax.dot_general(d1, jnp.concatenate(p1, axis=1), nt, preferred_element_type=f32)
        for y in range(BY):
            gs = gs + dpre_ref[z + 2, 4 + y : 5 + y, :] * top_ref[z, y]
        return g1, g2, gs

    zero = jnp.zeros((C, TAPS), f32)
    g1, g2, gs = lax.fori_loop(0, BZ, weights, (zero, zero, jnp.zeros((C, X), f32)), unroll=2)
    grad_ref[...] = jnp.zeros_like(grad_ref)
    for i, g in enumerate((g1, g2)):
        for k in range(3):
            grad_ref[i, C * k : C * k + C] = g[:, X * k : X * k + X]
        grad_ref[i, 48:, :48] = g[:8, 3 * X :]
        grad_ref[i, 48:, 64:112] = g[8:, 3 * X :]
    grad_ref[0, 48:49, 48:64] = jnp.sum(jnp.transpose(gs), axis=0, keepdims=True)


def finish(a_ref, b_ref, first_ref, second_ref, speed_ref):
    a, b = a_ref[...], b_ref[...]
    total = jnp.sum(a * a) + jnp.sum(b * b)
    count = 54.0 * C * C + C
    factor = 1.0 / jnp.maximum(jnp.sqrt(jnp.full((1, 1), total)) / jnp.sqrt(f32(count)), 1.0)
    a, b = a * factor, b * factor
    for out, g in ((first_ref, a), (second_ref, b)):
        for t in range(27):
            row, lane = C * (t // 8), C * (t % 8)
            if t < 24:
                out[t] = g[row : row + C, lane : lane + C]
            else:
                out[t, :8] = g[48:, lane : lane + C]
                out[t, 8:] = g[48:, 64 + lane : 64 + lane + C]
    speed_ref[...] = a[48:49, 48:64]


def call(kernel, outs, scratch=(), flops=0):
    smem = pl.BlockSpec(memory_space=pltpu.SMEM)
    vmem = pl.BlockSpec(memory_space=pltpu.VMEM)

    def run(at, *args):
        args = ((at,) if at is not None else ()) + args
        specs = [smem if (i == 0 and at is not None) else vmem for i in range(len(args))]
        many = isinstance(outs, (list, tuple))
        size = sum(a.size * a.dtype.itemsize for a in args)
        return pl.pallas_call(
            kernel,
            out_shape=outs,
            in_specs=specs,
            out_specs=[vmem] * len(outs) if many else vmem,
            scratch_shapes=list(scratch),
            cost_estimate=pl.CostEstimate(flops=flops, bytes_accessed=size, transcendentals=0),
            compiler_params=pltpu.CompilerParams(vmem_limit_bytes=16 * 1024 * 1024),
        )(*args)

    return run


def shape(dims, dtype=bf16):
    return jax.ShapeDtypeStruct(dims, dtype)


def even(value, axis):
    n = lax.axis_size(axis)
    return lax.ppermute(value, axis, [(i, i ^ 1) for i in range(n)])


def odd(value, axis):
    n = lax.axis_size(axis)
    pairs = [(i, i + 1) for i in range(1, n - 1, 2)]
    return lax.ppermute(value, axis, pairs + [(j, i) for i, j in pairs])


def groups(n, unit):
    size = max(1, min(4, n // unit))
    firsts = [i for i in range(n) if (i // unit) % size == 0]
    return [[i + unit * k for k in range(size)] for i in firsts]


def total_of(grad, iz):
    core = iz % 2
    keep = lax.dynamic_index_in_dim(grad, core, 0, keepdims=False)
    give = lax.dynamic_index_in_dim(grad, 1 - core, 0, keepdims=False)
    part = keep + even(give, "gz")
    for axis, unit in (("gy", 1), ("gy", 4), ("gz", 8), ("gz", 2)):
        sets = groups(lax.axis_size(axis), unit)
        if len(sets[0]) > 1:
            copies = jnp.broadcast_to(part[None], (len(sets[0]),) + part.shape)
            part = jnp.sum(lax.all_to_all(copies, axis, 0, 0, axis_index_groups=sets), axis=0)
    other = even(part, "gz")
    return jnp.where(core == 0, part, other), jnp.where(core == 0, other, part)


def on_device(features, labels, sign_map, conv_first, conv_second, speed_weight):
    nz, ny = BZ * lax.axis_size("gz"), BY * lax.axis_size("gy")
    iz, iy = lax.axis_index("gz"), lax.axis_index("gy")
    pz, py = iz % 2, iy % 2
    at = jnp.stack([iz, iy, pz, py]).astype(jnp.int32)
    taps = [w.transpose(2, 3, 4, 0, 1).reshape(27, C, C) for w in (conv_first, conv_second)]
    w1, w2, w1b, w2b, sw, target = call(
        build, [shape((2 * C, 36 * C))] * 4 + [shape((C, X), f32), shape((BZ, BY, X), f32)]
    )(None, *taps, speed_weight.reshape(1, C), labels)

    ft, me, mo = call(prepare, [shape((BZ, BY, C, X)), shape((9, C, X)), shape((9, C, X))])(
        at, features, sign_map
    )
    ro = odd(mo, "gy")
    re = even(me, "gy")
    fy, sy, ma, mb = call(
        extend,
        [shape((BZ, 12, C, X)), shape((BZ, 16, X), f32), shape((27, C, X)), shape((27, C, X))],
    )(at, ft, sign_map, re, ro)
    rb = odd(mb, "gz")
    ra = even(ma, "gz")

    fx, hx, slope1, slope2, top, fe, fo, own, g0 = call(
        lambda *refs: forward(nz, ny, *refs),
        [
            shape((6, 10, 3, C, X)),
            shape((6, 10, 3, C, X)),
            shape((6, 10, C, X), f32),
            shape((BZ, BY, C, X), f32),
            shape((BZ, BY, C, X), f32),
            shape((28, 8, X), SENT),
            shape((28, 8, X), SENT),
            shape((3, BZ, BY, X), f32),
            shape((8, 16, X), f32),
        ],
        [pltpu.VMEM((10, 16, X), f32), pltpu.VMEM((8, 12, 3, C, X), bf16)],
    )(at, fy, sy, ra, rb, target, w1, w2, sw)

    go = odd(fo, "gy")
    ge = even(fe, "gy")
    fa = call(widen, shape((36, 8, X), SENT))(at, fe, ge, go)
    ha = even(fa, "gz")
    ms, fs, s2y = call(
        spread, [shape((48, 8, X), SENT), shape((48, 8, X), SENT), shape((BZ, 12, C, X))]
    )(at, slope2, ge, go)
    fb = call(relay, shape((63, 8, X), SENT))(at, fa, ha)
    hb = odd(fb, "gz")
    hs = odd(fs, "gz")
    hm = even(ms, "gz")
    hc = even(hb, "gz")

    plane = (24, 24, X)
    dpre = call(
        lambda *refs: march(nz, ny, *refs),
        shape((8, 16, X), f32),
        [
            pltpu.VMEM(plane, f32),
            pltpu.VMEM(plane, f32),
            pltpu.VMEM((3,) + plane, f32),
            pltpu.VMEM((3,) + plane, f32),
            pltpu.VMEM((3,) + plane, f32),
            pltpu.VMEM((3,) + plane, f32),
            pltpu.VMEM((3,) + plane, f32),
            pltpu.VMEM((3,) + plane, f32),
            pltpu.VMEM(plane, f32),
            pltpu.VMEM((2,) + plane, f32),
        ],
    )(at, own, fa, ha, hb, hc, g0)

    d_features, grad = call(
        backward,
        [shape((C, BZ, BY, X)), shape((2, 56, X), f32)],
        [pltpu.VMEM((8, 12, 3, C, X), bf16), pltpu.VMEM((6, 10, 3, C, X), bf16)],
    )(at, dpre, slope2, s2y, hm, hs, sw, hx, fx, slope1, top, w1b, w2b)

    a, b = total_of(grad, iz)
    tap_major = shape((27, C, C), f32)
    first, second, speed = call(finish, [tap_major, tap_major, shape((1, C), f32)])(None, a, b)
    first, second = (
        g.reshape(3, 3, 3, C, C).transpose(3, 4, 0, 1, 2) for g in (first, second)
    )
    return d_features, first, second, speed.reshape(C)


def solution(mesh):
    in_specs = (P(None, "gz", "gy", None), P("gz", "gy", None), P("gz", "gy", None), P(), P(), P())
    out_specs = (P(None, "gz", "gy", None), P(), P(), P())

    return jax.shard_map(
        on_device, mesh=mesh, in_specs=in_specs, out_specs=out_specs, check_vma=False
    )
```
